128 devices in a mesh: slab: 32 (over x, z, core), leaf: 4 (over y).
Axes of the slice: x: 4, y: 4, z: 4, core: 2. Of those that a mesh axis runs over, the one named last changes fastest.
Arguments:
- particles: float32 [3, 128, 16, 256], P(None, 'slab', 'leaf'), may hold values from -1.05 to 1.05, as said below
- near_mask: int32 [16, 128, 16], P(None, 'slab', 'leaf'), may hold values from 0 to 1, as said below
Outputs:
- velocity: float32 [2, 128, 16, 256], P(None, 'slab', 'leaf')
The draws below stay inside these ranges and needn't reach their ends.
Inputs may be any that keep to these rules, and one draw needn't show every extreme that they name: `particles`: entries 0 and 1 of the first dimension are offsets; entry 2 is the circulation. near_mask[o, i, j] = near_mask[15 - o, i + dx, j + dy], where (dx, dy) is step o of the 16 steps with max(|dx|, |dy|) = 2 in row-major order over dx, then dy; it is 0 where leaf (i + dx, j + dy) lies outside the grid.
All inputs are finite; a program needn't handle non-finite values.
Results may differ from the reference program's by a relative error of at most 0.0003.
Values sent between devices are 32-bit elements; how exact they have to be, the bound alone decides.
No kernel may reach another device: no remote copies, remote signals or barrier semaphores. Data moves between devices by JAX's collectives and lax.ppermute only.
A program may use at most 64 MiB of HBM per device.

```python
import math
from functools import partial
import jax
import jax.numpy as jnp
import numpy as np
from jax import lax

C = 4
P_SIZE = 256
ORDER = 10
GX = 128
GY = 16
N_SLAB = 32
N_LEAF = 4


cycle_steps = [(a, b) for a in range(-2, 3) for b in range(-2, 3) if max(abs(a), abs(b)) == 2]


def leaf_classes(key):
    base_key = jax.random.fold_in(key, 7)
    first_key, second_key = jax.random.split(base_key)
    own_class = jax.random.randint(first_key, (GX, GY), 0, 2)
    region = jax.random.randint(second_key, (GX // 4, GY // 4), 0, 3)
    spread = jnp.repeat(jnp.repeat(region, 4, axis=0), 4, axis=1)
    return (own_class + spread).astype(jnp.int32)


def draw_particles(key, part):
    classes = leaf_classes(key)
    half_width = 0.3 + 0.25 * classes.astype(jnp.float32)
    draw_key = jax.random.fold_in(key, 11)
    key_x, key_y, key_strength = jax.random.split(draw_key, 3)
    offset_x = jax.random.uniform(key_x, (GX, GY, P_SIZE), jnp.float32, -1.0, 1.0) * half_width[:, :, None]
    offset_y = jax.random.uniform(key_y, (GX, GY, P_SIZE), jnp.float32, -1.0, 1.0) * half_width[:, :, None]
    strength = jax.random.normal(key_strength, (GX, GY, P_SIZE), jnp.float32) / 16.0
    return jnp.stack([offset_x, offset_y, strength])


def draw_near_mask(key, part):
    classes = leaf_classes(key)
    padded = jnp.pad(classes, 2, constant_values=-10)
    layers = []
    for step_x, step_y in cycle_steps:
        beside = padded[2 + step_x:2 + step_x + GX, 2 + step_y:2 + step_y + GY]
        layers.append((classes + beside >= 3).astype(jnp.int32))
    return jnp.stack(layers)


def setup_inputs(seed: int = 0) -> dict:
    keys = jax.random.split(jax.random.key(seed), 3)
    return {
        "particles": draw_particles(jax.random.fold_in(keys[2], 71), 0),
        "near_mask": draw_near_mask(jax.random.fold_in(keys[2], 71), 0),
    }


DELTA_SQUARED = 0.0025
TWO_PI = 2.0 * math.pi
inner_steps = [(a, b) for a in range(-1, 2) for b in range(-1, 2)]
cycle_steps = [(a, b) for a in range(-2, 3) for b in range(-2, 3) if max(abs(a), abs(b)) == 2]


def complex_powers(base_real, base_imaginary, count):
    power_real = [jnp.ones_like(base_real)]
    power_imaginary = [jnp.zeros_like(base_imaginary)]
    for repeat in range(1, count):
        last_real = power_real[-1]
        last_imaginary = power_imaginary[-1]
        power_real.append(last_real * base_real - last_imaginary * base_imaginary)
        power_imaginary.append(last_real * base_imaginary + last_imaginary * base_real)
    return jnp.stack(power_real, -1), jnp.stack(power_imaginary, -1)


def translation(shift_real, shift_imaginary):
    hankel = np.arange(ORDER)[:, None] + np.arange(ORDER)[None, :] + 1
    weights = np.array([[math.comb(i + k, k) * (-1.0) ** (k + 1) for k in range(ORDER)] for i in range(ORDER)], dtype=np.float32)
    denominator = shift_real * shift_real + shift_imaginary * shift_imaginary
    inverse_real = shift_real / denominator
    inverse_imaginary = -shift_imaginary / denominator
    power_real, power_imaginary = complex_powers(inverse_real, inverse_imaginary, 2 * ORDER)
    return power_real[..., hankel] * weights, power_imaginary[..., hankel] * weights


def apply_translation(matrix_real, matrix_imaginary, source_real, source_imaginary):
    source_real = source_real[..., None, :]
    source_imaginary = source_imaginary[..., None, :]
    out_real = jnp.sum(matrix_real * source_real - matrix_imaginary * source_imaginary, -1)
    out_imaginary = jnp.sum(matrix_real * source_imaginary + matrix_imaginary * source_real, -1)
    return out_real, out_imaginary


def pair_row(step_x, step_y, pieces):
    target_x, target_y, source_x, source_y, circulation = pieces
    delta_x = target_x[:, :, None] - (step_x + source_x[:, None, :])
    delta_y = target_y[:, :, None] - (step_y + source_y[:, None, :])
    factor = circulation[:, None, :] / (delta_x * delta_x + delta_y * delta_y + DELTA_SQUARED)
    return jnp.sum(factor * delta_x, -1), -jnp.sum(factor * delta_y, -1)


def reference(particles, near_mask):
    float_type = particles.dtype
    offset_x, offset_y, strength = particles[0], particles[1], particles[2]
    power_real, power_imaginary = complex_powers(offset_x, offset_y, ORDER)
    leaf_real = jnp.sum(strength[..., None] * power_real, axis=2)
    leaf_imaginary = jnp.sum(strength[..., None] * power_imaginary, axis=2)
    row_index = jnp.arange(GX, dtype=jnp.int32)
    column_index = jnp.arange(GY, dtype=jnp.int32)
    row_block = row_index // C
    column_block = column_index // C
    centred_x = (row_index % C).astype(float_type) - (C - 1) / 2.0
    centred_y = (column_index % C).astype(float_type) - (C - 1) / 2.0
    block_power_real, block_power_imaginary = complex_powers(centred_x[:, None, None] + offset_x, centred_y[None, :, None] + offset_y, ORDER)

    def block_sum(values):
        summed = jnp.sum((strength[..., None] * values).reshape(N_SLAB, C, N_LEAF, C, P_SIZE, ORDER), axis=(1, 3, 4))
        return summed.reshape(N_SLAB * N_LEAF, ORDER)

    block_real = block_sum(block_power_real)
    block_imaginary = block_sum(block_power_imaginary)

    mask_float = near_mask.astype(float_type)
    padded = jnp.pad(particles, ((0, 0), (2, 2), (2, 2), (0, 0)))
    sum_real = jnp.zeros((GX, GY, P_SIZE), float_type)
    sum_imaginary = jnp.zeros((GX, GY, P_SIZE), float_type)
    for number, (step_x, step_y) in enumerate(inner_steps + cycle_steps):
        source = padded[:, 2 + step_x:2 + step_x + GX, 2 + step_y:2 + step_y + GY, :]
        if number < 9:
            circulation = source[2]
        else:
            circulation = source[2] * mask_float[number - 9][..., None]
        near_real, near_imaginary = lax.map(partial(pair_row, step_x, step_y), (offset_x, offset_y, source[0], source[1], circulation))
        sum_real = sum_real + near_real
        sum_imaginary = sum_imaginary + near_imaginary

    margin = 2 * C - 1
    padded_real = jnp.pad(leaf_real, ((margin, margin), (margin, margin), (0, 0)))
    padded_imaginary = jnp.pad(leaf_imaginary, ((margin, margin), (margin, margin), (0, 0)))
    local_real = jnp.zeros((GX, GY, ORDER), float_type)
    local_imaginary = jnp.zeros((GX, GY, ORDER), float_type)
    for number, (step_x, step_y) in enumerate(cycle_steps):
        source_real = padded_real[margin + step_x:margin + step_x + GX, margin + step_y:margin + step_y + GY, :]
        source_imaginary = padded_imaginary[margin + step_x:margin + step_x + GX, margin + step_y:margin + step_y + GY, :]
        matrix_real, matrix_imaginary = translation(jnp.asarray(float(step_x), float_type), jnp.asarray(float(step_y), float_type))
        part_real, part_imaginary = apply_translation(matrix_real, matrix_imaginary, source_real, source_imaginary)
        weight = (1.0 - mask_float[number])[..., None]
        local_real = local_real + weight * part_real
        local_imaginary = local_imaginary + weight * part_imaginary

    far_table = np.array([(a, b) for a in range(-margin, margin + 1) for b in range(-margin, margin + 1) if max(abs(a), abs(b)) >= 3], dtype=np.int32)

    def far_step(totals, offset):
        source_real = lax.dynamic_slice(padded_real, (margin + offset[0], margin + offset[1], jnp.int32(0)), (GX, GY, ORDER))
        source_imaginary = lax.dynamic_slice(padded_imaginary, (margin + offset[0], margin + offset[1], jnp.int32(0)), (GX, GY, ORDER))
        near_rows = jnp.abs((row_index + offset[0]) // C - row_block) <= 1
        near_columns = jnp.abs((column_index + offset[1]) // C - column_block) <= 1
        adjacent = (near_rows[:, None] & near_columns[None, :]).astype(float_type)[..., None]
        matrix_real, matrix_imaginary = translation(offset[0].astype(float_type), offset[1].astype(float_type))
        part_real, part_imaginary = apply_translation(matrix_real, matrix_imaginary, source_real, source_imaginary)
        return (totals[0] + adjacent * part_real, totals[1] + adjacent * part_imaginary), None

    (local_real, local_imaginary), unused = lax.scan(far_step, (local_real, local_imaginary), jnp.asarray(far_table))

    def block_step(totals, pieces):
        index, multipole_real, multipole_imaginary = pieces
        block_x = index // N_LEAF
        block_y = index % N_LEAF
        shift_real = (block_x * C).astype(float_type) + (C - 1) / 2.0 - row_index.astype(float_type)
        shift_imaginary = (block_y * C).astype(float_type) + (C - 1) / 2.0 - column_index.astype(float_type)
        remote = jnp.maximum(jnp.abs(block_x - row_block)[:, None], jnp.abs(block_y - column_block)[None, :]) >= 2
        shift_real = jnp.where(remote, shift_real[:, None], 1.0)
        shift_imaginary = jnp.where(remote, shift_imaginary[None, :], 1.0)
        matrix_real, matrix_imaginary = translation(shift_real, shift_imaginary)
        part_real, part_imaginary = apply_translation(matrix_real, matrix_imaginary, multipole_real, multipole_imaginary)
        weight = remote.astype(float_type)[..., None]
        return (totals[0] + weight * part_real, totals[1] + weight * part_imaginary), None

    (local_real, local_imaginary), unused = lax.scan(block_step, (local_real, local_imaginary), (jnp.arange(N_SLAB * N_LEAF, dtype=jnp.int32), block_real, block_imaginary))

    sum_real = sum_real + jnp.sum(local_real[:, :, None, :] * power_real - local_imaginary[:, :, None, :] * power_imaginary, -1)
    sum_imaginary = sum_imaginary + jnp.sum(local_real[:, :, None, :] * power_imaginary + local_imaginary[:, :, None, :] * power_real, -1)
    return jnp.stack([sum_imaginary, sum_real]) / TWO_PI
```

```python
import functools
import math

import jax
import jax.numpy as jnp
import numpy as np
from jax import lax
from jax.experimental import pallas as pl
from jax.experimental.pallas import tpu as pltpu
from jax.sharding import Mesh
from jax.sharding import PartitionSpec as P

ORDER = 10
SIDE = 4
LEAVES = 16
SIZE = 256
FEATURES = 32
DELTA_SQUARED = 0.0025
TWO_PI = 2.0 * math.pi
SLAB = ("slab_0", "slab_1", "slab_2")
ALL = ("slab_0", "slab_1", "slab_2", "leaf")
F32 = jnp.float32
BF16 = jnp.bfloat16
VMEM_LIMIT = 56 << 20
cycle_steps = [(a, b) for a in range(-2, 3) for b in range(-2, 3) if max(abs(a), abs(b)) == 2]
near_steps = [(a, b) for a in range(-2, 3) for b in range(-2, 3)]


def exchange_pairs(partner):
    pairs = []
    for x in range(4):
        for z in range(4):
            for c in range(2):
                for y in range(4):
                    other = partner(x, z, c, y)
                    if other is not None:
                        a, b, d, e = other
                        pairs.append((((x * 4 + z) * 2 + c) * 4 + y, ((a * 4 + b) * 2 + d) * 4 + e))
    return pairs


def slab_between_chips(x, z, c, y):
    slab = (x * 4 + z) * 2 + c
    other = slab + 1 if c == 1 else slab - 1
    if not 0 <= other < 32:
        return None
    return (other // 8, (other // 2) % 4, other % 2, y)


def near_side(k):
    return k ^ 1


def far_side(k):
    return 3 - k


SWAPS = {
    "core": exchange_pairs(lambda x, z, c, y: (x, z, 1 - c, y)),
    "slab": exchange_pairs(slab_between_chips),
    "leaf_near": exchange_pairs(lambda x, z, c, y: (x, z, c, near_side(y))),
    "leaf_far": exchange_pairs(lambda x, z, c, y: (x, z, c, far_side(y))),
    "z_near": exchange_pairs(lambda x, z, c, y: (x, near_side(z), c, y)),
    "z_far": exchange_pairs(lambda x, z, c, y: (x, far_side(z), c, y)),
    "x_near": exchange_pairs(lambda x, z, c, y: (near_side(x), z, c, y)),
    "x_far": exchange_pairs(lambda x, z, c, y: (far_side(x), z, c, y)),
}


def swap(value, name):
    return lax.ppermute(value, ALL, SWAPS[name])


def pieces(value, count):
    parts = []
    for unused in range(count):
        part = value.astype(BF16).astype(F32)
        parts.append(part)
        value = value - part
    return parts


def build_features(wx, wy, g, ox, oy, stage_t, stage_s, stage_w, t_ref, s_ref, w_ref, first, with_target):
    count = wx.shape[0]
    one = jnp.ones_like(wx)
    zero = jnp.zeros_like(wx)
    coarse_x = jnp.round(wx * 32.0) * (1.0 / 32.0)
    coarse_y = jnp.round(wy * 32.0) * (1.0 / 32.0)
    fine_x = wx - coarse_x
    fine_y = wy - coarse_y
    big_x = coarse_x + ox
    big_y = coarse_y + oy
    big = pieces(big_x * big_x + big_y * big_y, 2)
    rest = 2.0 * (big_x * fine_x + big_y * fine_y) + fine_x * fine_x + fine_y * fine_y
    px = pieces(fine_x, 2)
    py = pieces(fine_y, 2)
    if with_target:
        rows = [big_x, big_y, big[0], big[1], one, one, zero, zero]
        rows += [big_x, big_x, big_y, big_y, px[0], px[1], py[0], py[1]]
        rows += [px[0], px[0], px[1], py[0], py[0], py[1]]
        rows += pieces(rest + DELTA_SQUARED, 3) + [one, one, one]
        rows += [zero] * (FEATURES - len(rows))
        for f, row in enumerate(rows):
            stage_t[:count, f, :] = row
    twice = lambda v: -2.0 * v
    rows = [twice(big_x), twice(big_y), one, one, big[0], big[1], zero, zero]
    rows += [twice(px[0]), twice(px[1]), twice(py[0]), twice(py[1])]
    rows += [twice(big_x), twice(big_x), twice(big_y), twice(big_y)]
    rows += [twice(px[0]), twice(px[1]), twice(px[0]), twice(py[0]), twice(py[1]), twice(py[0])]
    rows += [one, one, one] + pieces(rest, 3)
    rows += [zero] * (FEATURES - len(rows))
    for f, row in enumerate(rows):
        stage_s[:count, f, :] = row
    rows = pieces(g, 3) + pieces(g * (wx + ox), 3) + pieces(g * (wy + oy), 3)
    rows += [zero] * (16 - len(rows))
    for f, row in enumerate(rows):
        stage_w[:count, f, :] = row
    for n in range(count):
        if with_target:
            t_ref[first + n] = stage_t[n].astype(BF16)
        s_ref[first + n] = jnp.transpose(stage_s[n]).astype(BF16)
        w_ref[first + n] = stage_w[n].astype(BF16)


def power_list(base_re, base_im, count):
    re = [jnp.ones_like(base_re)]
    im = [jnp.zeros_like(base_im)]
    for unused in range(1, count):
        a, b = re[-1], im[-1]
        re.append(a * base_re - b * base_im)
        im.append(a * base_im + b * base_re)
    return re, im


def row_of(n):
    return lax.broadcasted_iota(jnp.int32, (n, 1), 0)


def leaf_offsets():
    n = row_of(LEAVES)
    ox = (n >> 2).astype(F32) - 1.5
    oy = (n & 3).astype(F32) - 1.5
    return ox, oy


def own_rows(ref, part):
    return jnp.concatenate([ref[part, i] for i in range(SIDE)], axis=0)


SLAB_ROWS = 72
LEAF_ROWS = 96


def prepare_own(info, part_ref, t_ref, s_ref, w_ref, m_ref, f_ref, a_ref, b_ref, stage_t, stage_s, stage_w):
    wx = own_rows(part_ref, 0)
    wy = own_rows(part_ref, 1)
    g = own_rows(part_ref, 2)
    ox, oy = leaf_offsets()
    lane = lax.broadcasted_iota(jnp.int32, (LEAVES, 128), 1)
    table = jnp.zeros((LEAVES, 128), F32)
    for start, base_re, base_im in ((0, wx, wy), (32, wx + ox, wy + oy)):
        re, im = power_list(base_re, base_im, ORDER)
        for k in range(ORDER):
            table = jnp.where(lane == start + k, jnp.sum(g * re[k], 1, keepdims=True), table)
            if k:
                table = jnp.where(lane == start + ORDER + k, jnp.sum(g * im[k], 1, keepdims=True), table)
    turned = jnp.transpose(table)
    leaf_part = jnp.concatenate([turned[0:24], jnp.zeros((24, 112), F32)], axis=1)
    block_part = jnp.sum(turned[32:56], axis=1, keepdims=True)
    me = info[0] * 4 + info[1]
    wide = lax.broadcasted_iota(jnp.int32, (24, 128), 1)
    block_row = jnp.where(wide == me, block_part, 0.0)
    m_ref[...] = leaf_part
    f_ref[...] = block_row
    even = info[2] == 0
    for c in range(3):
        first = jnp.concatenate([part_ref[c, 0], part_ref[c, 1]], axis=0)
        last = jnp.concatenate([part_ref[c, 2], part_ref[c, 3]], axis=0)
        a_ref[8 * c : 8 * c + 8] = jnp.where(even, last, first)
        b_ref[8 * c : 8 * c + 8] = jnp.where(even, first, last)
    none = jnp.zeros((24, 128), F32)
    for ref in (a_ref, b_ref):
        ref[24:48, 0:128] = leaf_part
        ref[24:48, 128:256] = none
        ref[48:72, 0:128] = block_row
        ref[48:72, 128:256] = none
    build_features(wx, wy, g, ox, oy, stage_t, stage_s, stage_w, t_ref, s_ref, w_ref, 0, True)


def prepare_slab(
    info, part_ref, ra_ref, rb_ref, m_ref, f_ref, after_ref, s_ref, w_ref, m_out, f_out, near_ref, far_ref, stage_s, stage_w
):
    even = info[2] == 0
    leaf_even = info[3] == 0
    halo = []
    for c in range(3):
        ra = ra_ref[8 * c : 8 * c + 8]
        rb = rb_ref[8 * c : 8 * c + 8]
        before = jnp.where(even, rb, ra)
        after = jnp.where(even, ra, rb)
        halo.append(jnp.concatenate([before, after], axis=0))
        rows = [before[0:4], before[4:8]] + [part_ref[c, i] for i in range(SIDE)] + [after[0:4], after[4:8]]
        left = jnp.concatenate([r[0:2] for r in rows], axis=0)
        right = jnp.concatenate([r[2:4] for r in rows], axis=0)
        near_ref[16 * c : 16 * c + 16] = jnp.where(leaf_even, right, left)
        far_ref[16 * c : 16 * c + 16] = jnp.where(leaf_even, left, right)
    ma = ra_ref[24:48, 0:16]
    mb = rb_ref[24:48, 0:16]
    window = jnp.concatenate(
        [m_ref[:, 0:16], jnp.where(even, mb, ma), jnp.where(even, ma, mb), jnp.zeros((24, 80), F32)], axis=1
    )
    blocks = f_ref[...] + ra_ref[48:72, 0:128]
    m_out[...] = window
    f_out[...] = blocks
    none = jnp.zeros((24, 128), F32)
    for ref in (near_ref, far_ref):
        ref[48:72, 0:128] = window
        ref[48:72, 128:256] = none
    near_ref[72:96, 0:128] = blocks
    near_ref[72:96, 128:256] = none
    n = row_of(LEAVES)
    i = (n >> 2) - 2
    ox = jnp.where(i >= 0, i + 4, i).astype(F32) - 1.5
    oy = (n & 3).astype(F32) - 1.5
    build_features(halo[0], halo[1], halo[2], ox, oy, None, stage_s, stage_w, None, s_ref, w_ref, 0, False)


def leaf_halo(which, info, r_ref, s_ref, w_ref, stage_s, stage_w):
    leaf_even = info[3] == 0
    to_right = leaf_even if which == 0 else jnp.logical_not(leaf_even)
    valid = jnp.float32(1.0) if which == 0 else info[4].astype(F32)
    n = row_of(LEAVES)
    ox = (n >> 1).astype(F32) - 3.5
    side = (n & 1).astype(F32)
    oy = jnp.where(to_right, side + 4.0, side - 2.0) - 1.5
    build_features(
        r_ref[0:16], r_ref[16:32], r_ref[32:48] * valid, ox, oy, None, stage_s, stage_w, None, s_ref, w_ref, 0, False
    )


def prepare_leaf_near(info, r_ref, f_ref, send_ref, after_ref, s_ref, w_ref, f_out, send_out, stage_s, stage_w):
    blocks = f_ref[...] + r_ref[72:96, 0:128]
    f_out[...] = blocks
    send_out[0:72] = send_ref[...]
    send_out[72:96, 0:128] = blocks
    send_out[72:96, 128:256] = jnp.zeros((24, 128), F32)
    leaf_halo(0, info, r_ref, s_ref, w_ref, stage_s, stage_w)


def prepare_leaf_far(info, r_ref, f_ref, after_ref, s_ref, w_ref, f_out, stage_s, stage_w):
    f_out[...] = f_ref[...] + r_ref[72:96, 0:128]
    leaf_halo(1, info, r_ref, s_ref, w_ref, stage_s, stage_w)


def direct(bodies, unroll, zero, info, table, mask, t_ref, s_ref, w_ref, *refs):
    acc_ref = refs[-1]
    if zero:
        acc_ref[...] = jnp.zeros_like(acc_ref)
    else:
        acc_ref[...] = refs[0][...]
    shift = info[5]

    def step(b, unused):
        for n in range(unroll):
            at = (b * unroll + n) * 3 + shift
            t = table[at]
            s = table[at + 1]
            weight = mask[table[at + 2] * LEAVES + t]
            distance = jnp.dot(s_ref[s], t_ref[t], preferred_element_type=F32)
            kernel = 1.0 / distance
            high = kernel.astype(BF16)
            low = (kernel - high.astype(F32)).astype(BF16)
            w = w_ref[s]
            total = jnp.dot(w, high, preferred_element_type=F32) + jnp.dot(w, low, preferred_element_type=F32)
            acc_ref[t] = acc_ref[t] + weight * total
        return 0

    lax.fori_loop(0, bodies, step, 0)


def pair_table(kind, to_right=False):
    out = []
    for t in range(LEAVES):
        i, j = divmod(t, SIDE)
        for a, b in near_steps:
            o = cycle_steps.index((a, b)) if max(abs(a), abs(b)) == 2 else 16
            si, sj = i + a, j + b
            in_row, in_column = 0 <= si < SIDE, 0 <= sj < SIDE
            if kind == "own" and in_row and in_column:
                out.append((t, si * SIDE + sj, o))
            if kind == "slab" and not in_row and in_column:
                out.append((t, ((si + 2) if si < 0 else (si - 2)) * SIDE + sj, o))
            if kind == "leaf" and not in_column and (sj >= SIDE) == to_right:
                out.append((t, (si + 2) * 2 + (sj - SIDE if to_right else sj + 2), o))
    return np.array(out, np.int32)


def finish(info, part_ref, nm_ref, acc_ref, m_ref, r1_ref, r2_ref, f_ref, out_ref):
    leaf_even = info[3] == 0
    valid = info[4].astype(F32)
    wx = own_rows(part_ref, 0)
    wy = own_rows(part_ref, 1)
    ox, oy = leaf_offsets()
    n = row_of(LEAVES)
    ti = n >> 2
    tj = n & 3
    lane = lax.broadcasted_iota(jnp.int32, (LEAVES, 128), 1)
    k = lane >> 4
    r = lane & 15
    si = jnp.where(k == 0, r >> 2, jnp.where(k == 1, (r >> 2) - 4, (r >> 2) + 4))
    near_shift = jnp.where(leaf_even, 4, -4)
    xs = []
    ys = []
    weights = []
    for column in (0, near_shift, -near_shift):
        sj = (r & 3) + column
        dx = si - ti
        dy = sj - tj
        reach = jnp.maximum(jnp.abs(dx), jnp.abs(dy))
        weight = jnp.where(reach >= 3, 1.0, 0.0).astype(F32)
        for o, (a, b) in enumerate(cycle_steps):
            hit = jnp.logical_and(dx == a, dy == b)
            weight = jnp.where(hit, 1.0 - nm_ref[:, o : o + 1], weight)
        weight = jnp.where(k < 3, weight, 0.0)
        used = jnp.logical_and(reach >= 2, k < 3)
        xs.append(jnp.where(used, dx.astype(F32), 1.0))
        ys.append(jnp.where(used, dy.astype(F32), 1.0))
        weights.append(weight)
    bx = (lane >> 2) - info[0]
    by = (lane & 3) - info[1]
    remote = jnp.maximum(jnp.abs(bx), jnp.abs(by)) >= 2
    xs.append(jnp.where(remote, (bx * SIDE - ti).astype(F32) + 1.5, 1.0))
    ys.append(jnp.where(remote, (by * SIDE - tj).astype(F32) + 1.5, 1.0))
    weights.append(jnp.where(remote, 1.0, 0.0).astype(F32))
    tx = jnp.concatenate(xs, axis=1)
    ty = jnp.concatenate(ys, axis=1)
    weight = jnp.concatenate(weights, axis=1)
    square = tx * tx + ty * ty
    inv_x = tx / square
    inv_y = -ty / square
    h_re = [weight * inv_x]
    h_im = [weight * inv_y]
    for order in range(1, 2 * ORDER - 1):
        a, b = h_re[-1], h_im[-1]
        h_re.append((a * inv_x - b * inv_y) * float(order))
        h_im.append((a * inv_y + b * inv_x) * float(order))

    def source(row):
        return jnp.concatenate(
            [
                m_ref[row : row + 1, :],
                r1_ref[48 + row : 49 + row, 0:128],
                r2_ref[48 + row : 49 + row, 0:128] * valid,
                f_ref[row : row + 1, :],
            ],
            axis=1,
        )

    a_re = []
    a_im = []
    for k_ in range(ORDER):
        scale = (-1.0) ** (k_ + 1) / math.factorial(k_)
        a_re.append(jnp.broadcast_to(source(k_) * scale, (LEAVES, 512)))
        a_im.append(jnp.broadcast_to(source(ORDER + k_) * scale, (LEAVES, 512)))
    p_re, p_im = power_list(wx, wy, ORDER)
    x = wx + ox
    y = wy + oy
    rows = lambda at: acc_ref[:, at, :] + acc_ref[:, at + 1, :] + acc_ref[:, at + 2, :]
    total = rows(0)
    sum_re = x * total - rows(3)
    sum_im = rows(6) - y * total
    for m in range(ORDER):
        part_re = jnp.zeros((LEAVES, 512), F32)
        part_im = jnp.zeros((LEAVES, 512), F32)
        for k_ in range(ORDER):
            part_re = part_re + (h_re[m + k_] * a_re[k_] - h_im[m + k_] * a_im[k_])
            part_im = part_im + (h_re[m + k_] * a_im[k_] + h_im[m + k_] * a_re[k_])
        scale = 1.0 / math.factorial(m)
        l_re = jnp.sum(part_re, 1, keepdims=True) * scale
        l_im = jnp.sum(part_im, 1, keepdims=True) * scale
        sum_re = sum_re + (l_re * p_re[m] - l_im * p_im[m])
        sum_im = sum_im + (l_re * p_im[m] + l_im * p_re[m])
    sum_re = sum_re * (1.0 / TWO_PI)
    sum_im = sum_im * (1.0 / TWO_PI)
    for i in range(SIDE):
        out_ref[0, i] = sum_im[4 * i : 4 * i + 4]
        out_ref[1, i] = sum_re[4 * i : 4 * i + 4]


V = pl.BlockSpec(memory_space=pltpu.VMEM)
S = pl.BlockSpec(memory_space=pltpu.SMEM)
A = pl.BlockSpec(memory_space=pl.ANY)


def shaped(*shape, dtype=F32):
    return jax.ShapeDtypeStruct(shape, dtype)


def call(kernel, name, in_specs, outs, scratch, cost, aliases=None):
    return pl.pallas_call(
        kernel,
        out_shape=outs,
        in_specs=in_specs,
        out_specs=jax.tree.map(lambda unused: V, outs),
        scratch_shapes=scratch,
        name=name,
        input_output_aliases=aliases or {},
        cost_estimate=pl.CostEstimate(flops=cost, bytes_accessed=1 << 20, transcendentals=0),
        compiler_params=pltpu.CompilerParams(vmem_limit_bytes=VMEM_LIMIT),
    )


def features_out(count):
    return [shaped(count, SIZE, FEATURES, dtype=BF16), shaped(count, 16, SIZE, dtype=BF16)]


def stages(with_target):
    out = [pltpu.VMEM((LEAVES, FEATURES, SIZE), F32), pltpu.VMEM((LEAVES, 16, SIZE), F32)]
    return ([pltpu.VMEM((LEAVES, FEATURES, SIZE), F32)] if with_target else []) + out


SMALL = 4_000_000
PAIR = 400_000_000


def run_direct(name, info, table, mask, feats, acc, bodies, unroll, shift):
    zero = acc is None
    ins = [info.at[5].set(shift) if shift is not None else info, table, mask, *feats]
    if not zero:
        ins.append(acc)
    return call(
        functools.partial(direct, bodies, unroll, zero),
        name,
        [S, S, S, V, V, V] + ([] if zero else [V]),
        shaped(LEAVES, 16, SIZE),
        [],
        PAIR * bodies * unroll,
        {} if zero else {6: 0},
    )(*ins)


def body(particles, near_mask):
    slab = lax.axis_index(SLAB)
    leaf = lax.axis_index("leaf")
    has_far = jnp.logical_and(leaf > 0, leaf < 3).astype(jnp.int32)
    zero = jnp.zeros_like(slab)
    info = jnp.stack([slab, leaf, slab % 2, leaf % 2, has_far, zero, zero, zero]).astype(jnp.int32)
    mask_rows = near_mask.reshape(16, LEAVES).astype(F32)
    mask = jnp.concatenate([mask_rows.reshape(-1), jnp.ones((LEAVES,), F32)])
    mask_turned = mask_rows.T

    t0, s0, w0, m0, f0, send_a, send_b = call(
        prepare_own,
        "prepare_own",
        [S, V],
        [shaped(LEAVES, FEATURES, SIZE, dtype=BF16), *features_out(LEAVES), shaped(24, 128), shaped(24, 128)]
        + [shaped(SLAB_ROWS, SIZE)] * 2,
        stages(True),
        SMALL,
    )(info, particles)
    recv_a = swap(send_a, "core")
    recv_b = swap(send_b, "slab")
    own = jnp.asarray(pair_table("own").reshape(-1))
    feats = (t0, s0, w0)
    acc = run_direct("direct_own_0", info, own, mask, feats, None, 3, 28, None)
    s1, w1, m1, f1, send_near, send_far = call(
        prepare_slab,
        "prepare_slab",
        [S, V, V, V, V, V, A],
        [*features_out(LEAVES), shaped(24, 128), shaped(24, 128), shaped(LEAF_ROWS, SIZE), shaped(72, SIZE)],
        stages(False),
        SMALL,
    )(info, particles, recv_a, recv_b, m0, f0, acc)
    send_near, acc = lax.optimization_barrier((send_near, acc))
    recv_near = swap(send_near, "leaf_near")
    own_1 = jnp.asarray(pair_table("own")[84:140].reshape(-1))
    own_2 = jnp.asarray(pair_table("own")[140:].reshape(-1))
    acc = run_direct("direct_own_1", info, own_1, mask, feats, acc, 2, 28, None)
    s2, w2, f2, send_far = call(
        prepare_leaf_near,
        "prepare_leaf_near",
        [S, V, V, V, A],
        [*features_out(LEAVES), shaped(24, 128), shaped(LEAF_ROWS, SIZE)],
        stages(False),
        SMALL,
    )(info, recv_near, f1, send_far, acc)
    send_far, acc = lax.optimization_barrier((send_far, acc))
    recv_far = swap(send_far, "leaf_far")
    acc = run_direct("direct_own_2", info, own_2, mask, feats, acc, 2, 28, None)
    s3, w3, f3 = call(
        prepare_leaf_far,
        "prepare_leaf_far",
        [S, V, V, A],
        [*features_out(LEAVES), shaped(24, 128)],
        stages(False),
        SMALL,
    )(info, recv_far, f2, acc)
    f3, acc = lax.optimization_barrier((f3, acc))
    got = swap(f3, "z_near")
    slab_pairs = jnp.asarray(pair_table("slab").reshape(-1))
    acc = run_direct("direct_slab", info, slab_pairs, mask, (t0, s1, w1), acc, 3, 28, None)
    got, acc = lax.optimization_barrier((got, acc))
    f4 = f3 + got
    f4, acc = lax.optimization_barrier((f4, acc))
    got = swap(f4, "z_far")
    right = pair_table("leaf", True).reshape(-1)
    left = pair_table("leaf", False).reshape(-1)
    parity = leaf % 2
    near_pairs = jnp.asarray(np.concatenate([right, left]))
    far_pairs = jnp.asarray(np.concatenate([left, right]))
    acc = run_direct("direct_leaf_near", info, near_pairs, mask, (t0, s2, w2), acc, 2, 30, parity * 180)
    got, acc = lax.optimization_barrier((got, acc))
    f5 = f4 + got
    f5, acc = lax.optimization_barrier((f5, acc))
    got = swap(f5, "x_near")
    acc = run_direct("direct_leaf_far_0", info, far_pairs, mask, (t0, s3, w3), acc, 1, 30, parity * 180)
    got, acc = lax.optimization_barrier((got, acc))
    f6 = f5 + got
    f6, acc = lax.optimization_barrier((f6, acc))
    got = swap(f6, "x_far")
    acc = run_direct("direct_leaf_far_1", info, far_pairs, mask, (t0, s3, w3), acc, 1, 30, parity * 180 + 90)
    got, acc = lax.optimization_barrier((got, acc))
    f7 = f6 + got
    return call(
        finish, "finish", [S] + [V] * 7, shaped(2, SIDE, SIDE, SIZE), [], SMALL
    )(info, particles, mask_turned, acc, m1, recv_near, recv_far, f7)


def solution(mesh):
    finer = Mesh(mesh.devices.reshape(4, 4, 2, mesh.shape["leaf"]), ALL)
    in_specs = (P(None, SLAB, "leaf", None), P(None, SLAB, "leaf"))
    out_specs = P(None, SLAB, "leaf", None)
    run = jax.shard_map(body, mesh=finer, in_specs=in_specs, out_specs=out_specs, check_vma=False)

    def whole(particles, near_mask):
        with jax.sharding.use_abstract_mesh(mesh.abstract_mesh):
            return run(particles, near_mask)

    return run
```

```python
import functools
import math

import jax
import jax.numpy as jnp
import numpy as np
from jax import lax
from jax.experimental import pallas as pl
from jax.experimental.pallas import tpu as pltpu
from jax.sharding import Mesh
from jax.sharding import PartitionSpec as P

ORDER = 10
SIDE = 4
LEAVES = 16
SIZE = 256
FEATURES = 32
DELTA_SQUARED = 0.0025
TWO_PI = 2.0 * math.pi
SLAB = ("slab_0", "slab_1", "slab_2")
ALL = ("slab_0", "slab_1", "slab_2", "leaf")
F32 = jnp.float32
BF16 = jnp.bfloat16
VMEM_LIMIT = 6 << 20
cycle_steps = [(a, b) for a in range(-2, 3) for b in range(-2, 3) if max(abs(a), abs(b)) == 2]
near_steps = [(a, b) for a in range(-2, 3) for b in range(-2, 3)]


def exchange_pairs(partner):
    pairs = []
    for x in range(4):
        for z in range(4):
            for c in range(2):
                for y in range(4):
                    other = partner(x, z, c, y)
                    if other is not None:
                        a, b, d, e = other
                        pairs.append((((x * 4 + z) * 2 + c) * 4 + y, ((a * 4 + b) * 2 + d) * 4 + e))
    return pairs


def slab_between_chips(x, z, c, y):
    slab = (x * 4 + z) * 2 + c
    other = slab + 1 if c == 1 else slab - 1
    if not 0 <= other < 32:
        return None
    return (other // 8, (other // 2) % 4, other % 2, y)


def near_side(k):
    return k ^ 1


def far_side(k):
    return 3 - k


SWAPS = {
    "core": exchange_pairs(lambda x, z, c, y: (x, z, 1 - c, y)),
    "slab": exchange_pairs(slab_between_chips),
    "leaf_near": exchange_pairs(lambda x, z, c, y: (x, z, c, near_side(y))),
    "leaf_far": exchange_pairs(lambda x, z, c, y: (x, z, c, far_side(y))),
    "z_near": exchange_pairs(lambda x, z, c, y: (x, near_side(z), c, y)),
    "z_far": exchange_pairs(lambda x, z, c, y: (x, far_side(z), c, y)),
    "x_near": exchange_pairs(lambda x, z, c, y: (near_side(x), z, c, y)),
    "x_far": exchange_pairs(lambda x, z, c, y: (far_side(x), z, c, y)),
}


def swap(value, name):
    return lax.ppermute(value, ALL, SWAPS[name])


def pieces(value, count):
    parts = []
    for unused in range(count):
        part = value.astype(BF16).astype(F32)
        parts.append(part)
        value = value - part
    return parts


def build_features(wx, wy, g, ox, oy, stage_t, stage_s, stage_w, t_ref, s_ref, w_ref, first, with_target):
    count = wx.shape[0]
    one = jnp.ones_like(wx)
    zero = jnp.zeros_like(wx)
    coarse_x = jnp.round(wx * 32.0) * (1.0 / 32.0)
    coarse_y = jnp.round(wy * 32.0) * (1.0 / 32.0)
    fine_x = wx - coarse_x
    fine_y = wy - coarse_y
    big_x = coarse_x + ox
    big_y = coarse_y + oy
    big = pieces(big_x * big_x + big_y * big_y, 2)
    rest = 2.0 * (big_x * fine_x + big_y * fine_y) + fine_x * fine_x + fine_y * fine_y
    px = pieces(fine_x, 2)
    py = pieces(fine_y, 2)
    if with_target:
        rows = [big_x, big_y, big[0], big[1], one, one, zero, zero]
        rows += [big_x, big_x, big_y, big_y, px[0], px[1], py[0], py[1]]
        rows += [px[0], px[0], px[1], py[0], py[0], py[1]]
        rows += pieces(rest + DELTA_SQUARED, 3) + [one, one, one]
        rows += [zero] * (FEATURES - len(rows))
        for f, row in enumerate(rows):
            stage_t[:count, f, :] = row
    twice = lambda v: -2.0 * v
    rows = [twice(big_x), twice(big_y), one, one, big[0], big[1], zero, zero]
    rows += [twice(px[0]), twice(px[1]), twice(py[0]), twice(py[1])]
    rows += [twice(big_x), twice(big_x), twice(big_y), twice(big_y)]
    rows += [twice(px[0]), twice(px[1]), twice(px[0]), twice(py[0]), twice(py[1]), twice(py[0])]
    rows += [one, one, one] + pieces(rest, 3)
    rows += [zero] * (FEATURES - len(rows))
    for f, row in enumerate(rows):
        stage_s[:count, f, :] = row
    rows = pieces(g, 3) + pieces(g * (wx + ox), 3) + pieces(g * (wy + oy), 3)
    rows += [zero] * (16 - len(rows))
    for f, row in enumerate(rows):
        stage_w[:count, f, :] = row
    for n in range(count):
        if with_target:
            t_ref[first + n] = stage_t[n].astype(BF16)
        s_ref[first + n] = jnp.transpose(stage_s[n]).astype(BF16)
        w_ref[first + n] = stage_w[n].astype(BF16)


def power_list(base_re, base_im, count):
    re = [jnp.ones_like(base_re)]
    im = [jnp.zeros_like(base_im)]
    for unused in range(1, count):
        a, b = re[-1], im[-1]
        re.append(a * base_re - b * base_im)
        im.append(a * base_im + b * base_re)
    return re, im


def row_of(n):
    return lax.broadcasted_iota(jnp.int32, (n, 1), 0)


def leaf_offsets():
    n = row_of(LEAVES)
    ox = (n >> 2).astype(F32) - 1.5
    oy = (n & 3).astype(F32) - 1.5
    return ox, oy


def own_rows(ref, part):
    return jnp.concatenate([ref[part, i] for i in range(SIDE)], axis=0)


def position():
    slab = lax.axis_index(SLAB)
    leaf = lax.axis_index("leaf")
    between = jnp.logical_and(leaf > 0, leaf < 3).astype(jnp.int32)
    return slab, leaf, slab & 1, leaf & 1, between


SLAB_ROWS = 72
LEAF_ROWS = 96


def prepare_own(part_ref, t_ref, s_ref, w_ref, m_ref, f_ref, a_ref, b_ref, stage_t, stage_s, stage_w):
    info = position()
    wx = own_rows(part_ref, 0)
    wy = own_rows(part_ref, 1)
    g = own_rows(part_ref, 2)
    ox, oy = leaf_offsets()
    lane = lax.broadcasted_iota(jnp.int32, (LEAVES, 128), 1)
    table = jnp.zeros((LEAVES, 128), F32)
    for start, base_re, base_im in ((0, wx, wy), (32, wx + ox, wy + oy)):
        re, im = power_list(base_re, base_im, ORDER)
        for k in range(ORDER):
            table = jnp.where(lane == start + k, jnp.sum(g * re[k], 1, keepdims=True), table)
            if k:
                table = jnp.where(lane == start + ORDER + k, jnp.sum(g * im[k], 1, keepdims=True), table)
    turned = jnp.transpose(table)
    leaf_part = jnp.concatenate([turned[0:24], jnp.zeros((24, 112), F32)], axis=1)
    block_part = jnp.sum(turned[32:56], axis=1, keepdims=True)
    me = info[0] * 4 + info[1]
    wide = lax.broadcasted_iota(jnp.int32, (24, 128), 1)
    block_row = jnp.where(wide == me, block_part, 0.0)
    m_ref[...] = leaf_part
    f_ref[...] = block_row
    even = info[2] == 0
    for c in range(3):
        first = jnp.concatenate([part_ref[c, 0], part_ref[c, 1]], axis=0)
        last = jnp.concatenate([part_ref[c, 2], part_ref[c, 3]], axis=0)
        a_ref[8 * c : 8 * c + 8] = jnp.where(even, last, first)
        b_ref[8 * c : 8 * c + 8] = jnp.where(even, first, last)
    none = jnp.zeros((24, 128), F32)
    for ref in (a_ref, b_ref):
        ref[24:48, 0:128] = leaf_part
        ref[24:48, 128:256] = none
        ref[48:72, 0:128] = block_row
        ref[48:72, 128:256] = none
    build_features(wx, wy, g, ox, oy, stage_t, stage_s, stage_w, t_ref, s_ref, w_ref, 0, True)


def prepare_slab(
    part_ref, ra_ref, rb_ref, m_ref, f_ref, after_ref, s_ref, w_ref, m_out, f_out, near_ref, far_ref, stage_s, stage_w
):
    info = position()
    even = info[2] == 0
    leaf_even = info[3] == 0
    halo = []
    for c in range(3):
        ra = ra_ref[8 * c : 8 * c + 8]
        rb = rb_ref[8 * c : 8 * c + 8]
        before = jnp.where(even, rb, ra)
        after = jnp.where(even, ra, rb)
        halo.append(jnp.concatenate([before, after], axis=0))
        rows = [before[0:4], before[4:8]] + [part_ref[c, i] for i in range(SIDE)] + [after[0:4], after[4:8]]
        left = jnp.concatenate([r[0:2] for r in rows], axis=0)
        right = jnp.concatenate([r[2:4] for r in rows], axis=0)
        near_ref[16 * c : 16 * c + 16] = jnp.where(leaf_even, right, left)
        far_ref[16 * c : 16 * c + 16] = jnp.where(leaf_even, left, right)
    ma = ra_ref[24:48, 0:16]
    mb = rb_ref[24:48, 0:16]
    window = jnp.concatenate(
        [m_ref[:, 0:16], jnp.where(even, mb, ma), jnp.where(even, ma, mb), jnp.zeros((24, 80), F32)], axis=1
    )
    blocks = f_ref[...] + ra_ref[48:72, 0:128]
    m_out[...] = window
    f_out[...] = blocks
    none = jnp.zeros((24, 128), F32)
    near_ref[48:72, 0:128] = jnp.concatenate([none[:, 0:48], window[:, 0:48], none[:, 0:32]], axis=1)
    near_ref[48:72, 128:256] = none
    far_ref[48:72, 0:128] = window
    far_ref[48:72, 128:256] = none
    near_ref[72:96, 0:128] = blocks
    near_ref[72:96, 128:256] = none
    n = row_of(LEAVES)
    i = (n >> 2) - 2
    ox = jnp.where(i >= 0, i + 4, i).astype(F32) - 1.5
    oy = (n & 3).astype(F32) - 1.5
    build_features(halo[0], halo[1], halo[2], ox, oy, None, stage_s, stage_w, None, s_ref, w_ref, 0, False)


def leaf_halo(which, r_ref, s_ref, w_ref, stage_s, stage_w):
    info = position()
    leaf_even = info[3] == 0
    to_right = leaf_even if which == 0 else jnp.logical_not(leaf_even)
    valid = jnp.float32(1.0) if which == 0 else info[4].astype(F32)
    n = row_of(LEAVES)
    ox = (n >> 1).astype(F32) - 3.5
    side = (n & 1).astype(F32)
    oy = jnp.where(to_right, side + 4.0, side - 2.0) - 1.5
    build_features(
        r_ref[0:16], r_ref[16:32], r_ref[32:48] * valid, ox, oy, None, stage_s, stage_w, None, s_ref, w_ref, 0, False
    )


def prepare_leaf_near(r_ref, f_ref, send_ref, after_ref, s_ref, w_ref, f_out, send_out, stage_s, stage_w):
    blocks = f_ref[...] + r_ref[72:96, 0:128]
    f_out[...] = blocks
    send_out[0:72] = send_ref[...]
    send_out[72:96, 0:128] = blocks
    send_out[72:96, 128:256] = jnp.zeros((24, 128), F32)
    leaf_halo(0, r_ref, s_ref, w_ref, stage_s, stage_w)


def prepare_leaf_far(r_ref, f_ref, after_ref, s_ref, w_ref, f_out, stage_s, stage_w):
    f_out[...] = f_ref[...] + r_ref[72:96, 0:128]
    leaf_halo(1, r_ref, s_ref, w_ref, stage_s, stage_w)


def direct(bodies, unroll, zero, by_side, table, mask, t_ref, s_ref, w_ref, *refs):
    acc_ref = refs[-1]
    if zero:
        acc_ref[...] = jnp.zeros_like(acc_ref)
    else:
        acc_ref[...] = refs[0][...]
    shift = position()[3] * by_side if by_side else 0

    def step(b, unused):
        for n in range(unroll):
            at = (b * unroll + n) * 3 + shift
            t = table[at]
            s = table[at + 1]
            o = table[at + 2]
            weight = jnp.where(o == 16, 1, mask[t >> 2, t & 3, o & 15]).astype(F32)
            distance = jnp.dot(s_ref[s], t_ref[t], preferred_element_type=F32)
            kernel = 1.0 / distance
            high = kernel.astype(BF16)
            low = (kernel - high.astype(F32)).astype(BF16)
            w = w_ref[s]
            total = jnp.dot(w, high, preferred_element_type=F32) + jnp.dot(w, low, preferred_element_type=F32)
            acc_ref[t] = acc_ref[t] + weight * total
        return 0

    lax.fori_loop(0, bodies, step, 0)


def pair_table(kind, to_right=False):
    out = []
    for t in range(LEAVES):
        i, j = divmod(t, SIDE)
        for a, b in near_steps:
            o = cycle_steps.index((a, b)) if max(abs(a), abs(b)) == 2 else 16
            si, sj = i + a, j + b
            in_row, in_column = 0 <= si < SIDE, 0 <= sj < SIDE
            if kind == "own" and in_row and in_column:
                out.append((t, si * SIDE + sj, o))
            if kind == "slab" and not in_row and in_column:
                out.append((t, ((si + 2) if si < 0 else (si - 2)) * SIDE + sj, o))
            if kind == "leaf" and not in_column and (sj >= SIDE) == to_right:
                out.append((t, (si + 2) * 2 + (sj - SIDE if to_right else sj + 2), o))
    return np.array(out, np.int32)


WIDE = 3 * 128


def finish(part_ref, nm_ref, acc_ref, m_ref, r1_ref, r2_ref, f_ref, got_ref, out_ref, h_ref, a_ref):
    info = position()
    leaf_even = info[3] == 0
    valid = info[4].astype(F32)
    n = row_of(LEAVES)
    ti = n >> 2
    tj = n & 3
    lane = lax.broadcasted_iota(jnp.int32, (LEAVES, 128), 1)
    near_mask = jnp.concatenate([nm_ref[i] for i in range(SIDE)], axis=0).astype(F32)
    near_shift = jnp.where(leaf_even, 4, -4)
    second = lane >= 48
    place = jnp.where(second, lane - 48, lane)
    k = place >> 4
    r = place & 15
    si = jnp.where(k == 0, r >> 2, jnp.where(k == 1, (r >> 2) - 4, (r >> 2) + 4))
    xs = []
    ys = []
    weights = []
    for column, lanes in ((jnp.where(second, near_shift, 0), 96), (-near_shift, 48)):
        dx = si - ti
        dy = (r & 3) + column - tj
        reach = jnp.maximum(jnp.abs(dx), jnp.abs(dy))
        weight = jnp.where(reach >= 3, 1.0, 0.0).astype(F32)
        for o, (a, b) in enumerate(cycle_steps):
            hit = jnp.logical_and(dx == a, dy == b)
            weight = jnp.where(hit, 1.0 - near_mask[:, o : o + 1], weight)
        inside = lane < lanes
        used = jnp.logical_and(reach >= 2, inside)
        xs.append(jnp.where(used, dx.astype(F32), 1.0))
        ys.append(jnp.where(used, dy.astype(F32), 1.0))
        weights.append(jnp.where(inside, weight, 0.0))
    bx = (lane >> 2) - info[0]
    by = (lane & 3) - info[1]
    remote = jnp.maximum(jnp.abs(bx), jnp.abs(by)) >= 2
    xs.append(jnp.where(remote, (bx * SIDE - ti).astype(F32) + 1.5, 1.0))
    ys.append(jnp.where(remote, (by * SIDE - tj).astype(F32) + 1.5, 1.0))
    weights.append(jnp.where(remote, 1.0, 0.0).astype(F32))
    for group in range(3):
        span = slice(128 * group, 128 * group + 128)
        tx, ty, weight = xs[group], ys[group], weights[group]
        square = tx * tx + ty * ty
        inv_x = tx / square
        inv_y = -ty / square
        re = weight * inv_x
        im = weight * inv_y
        h_ref[0, :, span] = re
        h_ref[1, :, span] = im
        for order in range(1, 2 * ORDER - 1):
            re, im = (re * inv_x - im * inv_y) * float(order), (re * inv_y + im * inv_x) * float(order)
            h_ref[2 * order, :, span] = re
            h_ref[2 * order + 1, :, span] = im
    row = row_of(24)
    which = jnp.where(row >= ORDER, row - ORDER, row)
    scale = jnp.zeros((24, 1), F32)
    for k_ in range(ORDER):
        scale = jnp.where(which == k_, (-1.0) ** (k_ + 1) / math.factorial(k_), scale)
    a_ref[:, 0:128] = (m_ref[...] + r1_ref[48:72, 0:128]) * scale
    a_ref[:, 128:256] = r2_ref[48:72, 0:128] * (valid * scale)
    a_ref[:, 256:384] = (f_ref[...] + got_ref[...]) * scale
    wx = own_rows(part_ref, 0)
    wy = own_rows(part_ref, 1)
    ox, oy = leaf_offsets()
    x = wx + ox
    y = wy + oy
    rows = lambda at: acc_ref[:, at, :] + acc_ref[:, at + 1, :] + acc_ref[:, at + 2, :]
    total = rows(0)
    sum_re = x * total - rows(3)
    sum_im = rows(6) - y * total
    locals_ = [[None] * ORDER, [None] * ORDER]
    half = ORDER // 2
    for first in (0, half):
        sums_re = [0.0] * half
        sums_im = [0.0] * half
        for group in range(3):
            span = slice(128 * group, 128 * group + 128)
            part_re = [None] * half
            part_im = [None] * half
            for k_ in range(ORDER):
                a_re = a_ref[k_ : k_ + 1, span]
                a_im = a_ref[ORDER + k_ : ORDER + k_ + 1, span]
                for m in range(half):
                    at = first + m + k_
                    h_re = h_ref[2 * at, :, span]
                    h_im = h_ref[2 * at + 1, :, span]
                    term_re = h_re * a_re - h_im * a_im
                    term_im = h_re * a_im + h_im * a_re
                    part_re[m] = term_re if k_ == 0 else part_re[m] + term_re
                    part_im[m] = term_im if k_ == 0 else part_im[m] + term_im
            for m in range(half):
                sums_re[m] = sums_re[m] + part_re[m]
                sums_im[m] = sums_im[m] + part_im[m]
        for m in range(half):
            factor = 1.0 / math.factorial(first + m)
            locals_[0][first + m] = jnp.sum(sums_re[m], 1, keepdims=True) * factor
            locals_[1][first + m] = jnp.sum(sums_im[m], 1, keepdims=True) * factor
    p_re = jnp.ones_like(wx)
    p_im = jnp.zeros_like(wx)
    for m in range(ORDER):
        if m:
            p_re, p_im = p_re * wx - p_im * wy, p_re * wy + p_im * wx
        sum_re = sum_re + (locals_[0][m] * p_re - locals_[1][m] * p_im)
        sum_im = sum_im + (locals_[0][m] * p_im + locals_[1][m] * p_re)
    sum_re = sum_re * (1.0 / TWO_PI)
    sum_im = sum_im * (1.0 / TWO_PI)
    for i in range(SIDE):
        out_ref[0, i] = sum_im[4 * i : 4 * i + 4]
        out_ref[1, i] = sum_re[4 * i : 4 * i + 4]


V = pl.BlockSpec(memory_space=pltpu.VMEM)
S = pl.BlockSpec(memory_space=pltpu.SMEM)
A = pl.BlockSpec(memory_space=pl.ANY)


def shaped(*shape, dtype=F32):
    return jax.ShapeDtypeStruct(shape, dtype)


def call(kernel, name, in_specs, outs, scratch, cost, aliases=None):
    return pl.pallas_call(
        kernel,
        out_shape=outs,
        in_specs=in_specs,
        out_specs=jax.tree.map(lambda unused: V, outs),
        scratch_shapes=scratch,
        name=name,
        input_output_aliases=aliases or {},
        cost_estimate=pl.CostEstimate(flops=cost, bytes_accessed=1 << 20, transcendentals=0),
        compiler_params=pltpu.CompilerParams(vmem_limit_bytes=VMEM_LIMIT),
    )


def features_out(count):
    return [shaped(count, SIZE, FEATURES, dtype=BF16), shaped(count, 16, SIZE, dtype=BF16)]


def stages(with_target):
    out = [pltpu.VMEM((LEAVES, FEATURES, SIZE), F32), pltpu.VMEM((LEAVES, 16, SIZE), F32)]
    return ([pltpu.VMEM((LEAVES, FEATURES, SIZE), F32)] if with_target else []) + out


SMALL = 4_000_000
PAIR = 400_000_000


def run_direct(name, table, mask, feats, acc, bodies, unroll, by_side=0):
    zero = acc is None
    ins = [jnp.asarray(table.reshape(-1)), mask, *feats]
    if not zero:
        ins.append(acc)
    return call(
        functools.partial(direct, bodies, unroll, zero, by_side),
        name,
        [S, S, V, V, V] + ([] if zero else [V]),
        shaped(LEAVES, 16, SIZE),
        [],
        PAIR * bodies * unroll,
        {} if zero else {5: 0},
    )(*ins)


def body(particles, near_mask):
    mask = near_mask.transpose(1, 2, 0)
    t0, s0, w0, m0, f0, send_a, send_b = call(
        prepare_own,
        "prepare_own",
        [V],
        [shaped(LEAVES, FEATURES, SIZE, dtype=BF16), *features_out(LEAVES), shaped(24, 128), shaped(24, 128)]
        + [shaped(SLAB_ROWS, SIZE)] * 2,
        stages(True),
        SMALL,
    )(particles)
    recv_a = swap(send_a, "core")
    recv_b = swap(send_b, "slab")
    own = pair_table("own")
    feats = (t0, s0, w0)
    acc = run_direct("direct_own_0", own, mask, feats, None, 2, 49)
    s1, w1, m1, f1, send_near, send_far = call(
        prepare_slab,
        "prepare_slab",
        [V, V, V, V, V, A],
        [*features_out(LEAVES), shaped(24, 128), shaped(24, 128), shaped(LEAF_ROWS, SIZE), shaped(72, SIZE)],
        stages(False),
        SMALL,
    )(particles, recv_a, recv_b, m0, f0, acc)
    send_near, acc = lax.optimization_barrier((send_near, acc))
    recv_near = swap(send_near, "leaf_near")
    acc = run_direct("direct_own_1", own[98:147], mask, feats, acc, 1, 49)
    s2, w2, f2, send_far = call(
        prepare_leaf_near,
        "prepare_leaf_near",
        [V, V, V, A],
        [*features_out(LEAVES), shaped(24, 128), shaped(LEAF_ROWS, SIZE)],
        stages(False),
        SMALL,
    )(recv_near, f1, send_far, acc)
    send_far, acc = lax.optimization_barrier((send_far, acc))
    recv_far = swap(send_far, "leaf_far")
    acc = run_direct("direct_own_2", own[147:], mask, feats, acc, 1, 49)
    s3, w3, f3 = call(
        prepare_leaf_far,
        "prepare_leaf_far",
        [V, V, A],
        [*features_out(LEAVES), shaped(24, 128)],
        stages(False),
        SMALL,
    )(recv_far, f2, acc)
    f3, acc = lax.optimization_barrier((f3, acc))
    got = swap(f3, "z_near")
    acc = run_direct("direct_slab", pair_table("slab"), mask, (t0, s1, w1), acc, 2, 42)
    got, acc = lax.optimization_barrier((got, acc))
    f4 = f3 + got
    f4, acc = lax.optimization_barrier((f4, acc))
    got = swap(f4, "z_far")
    right = pair_table("leaf", True)
    left = pair_table("leaf", False)
    near_pairs = np.concatenate([right, left])
    far_pairs = np.concatenate([left, right])
    acc = run_direct("direct_leaf_near", near_pairs, mask, (t0, s2, w2), acc, 1, 60, 180)
    got, acc = lax.optimization_barrier((got, acc))
    f5 = f4 + got
    f5, acc = lax.optimization_barrier((f5, acc))
    got = swap(f5, "x_near")
    acc = run_direct("direct_leaf_far_0", far_pairs, mask, (t0, s3, w3), acc, 1, 30, 180)
    got, acc = lax.optimization_barrier((got, acc))
    f6 = f5 + got
    f6, acc = lax.optimization_barrier((f6, acc))
    got = swap(f6, "x_far")
    far_late = np.concatenate([far_pairs[30:], far_pairs[:30]])
    acc = run_direct("direct_leaf_far_1", far_late, mask, (t0, s3, w3), acc, 1, 30, 180)
    got, acc = lax.optimization_barrier((got, acc))
    return call(
        finish,
        "finish",
        [V] * 8,
        shaped(2, SIDE, SIDE, SIZE),
        [pltpu.VMEM((4 * ORDER - 2, LEAVES, WIDE), F32), pltpu.VMEM((24, WIDE), F32)],
        SMALL,
    )(particles, mask, acc, m1, recv_near, recv_far, f6, got)


def solution(mesh):
    finer = Mesh(mesh.devices.reshape(4, 4, 2, mesh.shape["leaf"]), ALL)
    in_specs = (P(None, SLAB, "leaf", None), P(None, SLAB, "leaf"))
    out_specs = P(None, SLAB, "leaf", None)
    run = jax.shard_map(body, mesh=finer, in_specs=in_specs, out_specs=out_specs, check_vma=False)

    def whole(particles, near_mask):
        with jax.sharding.use_abstract_mesh(mesh.abstract_mesh):
            return run(particles, near_mask)

    return run
```

```python
import functools
import math

import jax
import jax.numpy as jnp
import numpy as np
from jax import lax
from jax.experimental import pallas as pl
from jax.experimental.pallas import tpu as pltpu
from jax.sharding import Mesh
from jax.sharding import PartitionSpec as P

ORDER = 10
SIDE = 4
LEAVES = 16
SIZE = 256
FEATURES = 32
DELTA_SQUARED = 0.0025
TWO_PI = 2.0 * math.pi
SLAB = ("slab_0", "slab_1", "slab_2")
ALL = ("slab_0", "slab_1", "slab_2", "leaf")
F32 = jnp.float32
BF16 = jnp.bfloat16
VMEM_LIMIT = 6 << 20
cycle_steps = [(a, b) for a in range(-2, 3) for b in range(-2, 3) if max(abs(a), abs(b)) == 2]
near_steps = [(a, b) for a in range(-2, 3) for b in range(-2, 3)]


def exchange_pairs(partner):
    pairs = []
    for x in range(4):
        for z in range(4):
            for c in range(2):
                for y in range(4):
                    other = partner(x, z, c, y)
                    if other is not None:
                        a, b, d, e = other
                        pairs.append((((x * 4 + z) * 2 + c) * 4 + y, ((a * 4 + b) * 2 + d) * 4 + e))
    return pairs


def slab_between_chips(x, z, c, y):
    slab = (x * 4 + z) * 2 + c
    other = slab + 1 if c == 1 else slab - 1
    if not 0 <= other < 32:
        return None
    return (other // 8, (other // 2) % 4, other % 2, y)


def near_side(k):
    return k ^ 1


def far_side(k):
    return 3 - k


SWAPS = {
    "core": exchange_pairs(lambda x, z, c, y: (x, z, 1 - c, y)),
    "slab": exchange_pairs(slab_between_chips),
    "leaf_near": exchange_pairs(lambda x, z, c, y: (x, z, c, near_side(y))),
    "leaf_far": exchange_pairs(lambda x, z, c, y: (x, z, c, far_side(y))),
    "z_near": exchange_pairs(lambda x, z, c, y: (x, near_side(z), c, y)),
    "z_far": exchange_pairs(lambda x, z, c, y: (x, far_side(z), c, y)),
    "x_near": exchange_pairs(lambda x, z, c, y: (near_side(x), z, c, y)),
    "x_far": exchange_pairs(lambda x, z, c, y: (far_side(x), z, c, y)),
}


def swap(value, name):
    return lax.ppermute(value, ALL, SWAPS[name])


def pieces(value, count):
    parts = []
    for unused in range(count):
        part = value.astype(BF16).astype(F32)
        parts.append(part)
        value = value - part
    return parts


def build_features(wx, wy, g, ox, oy, stage_t, stage_s, stage_w, t_ref, s_ref, w_ref, first, with_target):
    count = wx.shape[0]
    one = jnp.ones_like(wx)
    zero = jnp.zeros_like(wx)
    coarse_x = jnp.round(wx * 32.0) * (1.0 / 32.0)
    coarse_y = jnp.round(wy * 32.0) * (1.0 / 32.0)
    fine_x = wx - coarse_x
    fine_y = wy - coarse_y
    big_x = coarse_x + ox
    big_y = coarse_y + oy
    big = pieces(big_x * big_x + big_y * big_y, 2)
    rest = 2.0 * (big_x * fine_x + big_y * fine_y) + fine_x * fine_x + fine_y * fine_y
    px = pieces(fine_x, 2)
    py = pieces(fine_y, 2)
    if with_target:
        rows = [big_x, big_y, big[0], big[1], one, one, zero, zero]
        rows += [big_x, big_x, big_y, big_y, px[0], px[1], py[0], py[1]]
        rows += [px[0], px[0], px[1], py[0], py[0], py[1]]
        rows += pieces(rest + DELTA_SQUARED, 3) + [one, one, one]
        rows += [zero] * (FEATURES - len(rows))
        for f, row in enumerate(rows):
            stage_t[:count, f, :] = row
    twice = lambda v: -2.0 * v
    rows = [twice(big_x), twice(big_y), one, one, big[0], big[1], zero, zero]
    rows += [twice(px[0]), twice(px[1]), twice(py[0]), twice(py[1])]
    rows += [twice(big_x), twice(big_x), twice(big_y), twice(big_y)]
    rows += [twice(px[0]), twice(px[1]), twice(px[0]), twice(py[0]), twice(py[1]), twice(py[0])]
    rows += [one, one, one] + pieces(rest, 3)
    rows += [zero] * (FEATURES - len(rows))
    for f, row in enumerate(rows):
        stage_s[:count, f, :] = row
    rows = pieces(g, 3) + pieces(g * (wx + ox), 3) + pieces(g * (wy + oy), 3)
    rows += [zero] * (16 - len(rows))
    for f, row in enumerate(rows):
        stage_w[:count, f, :] = row
    for n in range(count):
        if with_target:
            t_ref[first + n] = stage_t[n].astype(BF16)
        s_ref[first + n] = jnp.transpose(stage_s[n]).astype(BF16)
        w_ref[first + n] = stage_w[n].astype(BF16)


def power_list(base_re, base_im, count):
    re = [jnp.ones_like(base_re)]
    im = [jnp.zeros_like(base_im)]
    for unused in range(1, count):
        a, b = re[-1], im[-1]
        re.append(a * base_re - b * base_im)
        im.append(a * base_im + b * base_re)
    return re, im


def row_of(n):
    return lax.broadcasted_iota(jnp.int32, (n, 1), 0)


def leaf_offsets():
    n = row_of(LEAVES)
    ox = (n >> 2).astype(F32) - 1.5
    oy = (n & 3).astype(F32) - 1.5
    return ox, oy


def own_rows(ref, part):
    return jnp.concatenate([ref[part, i] for i in range(SIDE)], axis=0)


def position():
    slab = lax.axis_index(SLAB)
    leaf = lax.axis_index("leaf")
    between = jnp.logical_and(leaf > 0, leaf < 3).astype(jnp.int32)
    return slab, leaf, slab & 1, leaf & 1, between


SLAB_ROWS = 72
LEAF_ROWS = 96


def prepare_own(part_ref, t_ref, s_ref, w_ref, m_ref, f_ref, a_ref, b_ref, stage_t, stage_s, stage_w):
    info = position()
    wx = own_rows(part_ref, 0)
    wy = own_rows(part_ref, 1)
    g = own_rows(part_ref, 2)
    ox, oy = leaf_offsets()
    lane = lax.broadcasted_iota(jnp.int32, (LEAVES, 128), 1)
    table = jnp.zeros((LEAVES, 128), F32)
    for start, base_re, base_im in ((0, wx, wy), (32, wx + ox, wy + oy)):
        re, im = power_list(base_re, base_im, ORDER)
        for k in range(ORDER):
            table = jnp.where(lane == start + k, jnp.sum(g * re[k], 1, keepdims=True), table)
            if k:
                table = jnp.where(lane == start + ORDER + k, jnp.sum(g * im[k], 1, keepdims=True), table)
    turned = jnp.transpose(table)
    leaf_part = jnp.concatenate([turned[0:24], jnp.zeros((24, 112), F32)], axis=1)
    block_part = jnp.sum(turned[32:56], axis=1, keepdims=True)
    me = info[0] * 4 + info[1]
    wide = lax.broadcasted_iota(jnp.int32, (24, 128), 1)
    block_row = jnp.where(wide == me, block_part, 0.0)
    m_ref[...] = leaf_part
    f_ref[...] = block_row
    even = info[2] == 0
    for c in range(3):
        first = jnp.concatenate([part_ref[c, 0], part_ref[c, 1]], axis=0)
        last = jnp.concatenate([part_ref[c, 2], part_ref[c, 3]], axis=0)
        a_ref[8 * c : 8 * c + 8] = jnp.where(even, last, first)
        b_ref[8 * c : 8 * c + 8] = jnp.where(even, first, last)
    none = jnp.zeros((24, 128), F32)
    for ref in (a_ref, b_ref):
        ref[24:48, 0:128] = leaf_part
        ref[24:48, 128:256] = none
        ref[48:72, 0:128] = block_row
        ref[48:72, 128:256] = none
    build_features(wx, wy, g, ox, oy, stage_t, stage_s, stage_w, t_ref, s_ref, w_ref, 0, True)


def pack_slab(part_ref, ra_ref, rb_ref, m_ref, f_ref, after_ref, m_out, f_out, near_ref, far_ref):
    info = position()
    even = info[2] == 0
    leaf_even = info[3] == 0
    for c in range(3):
        ra = ra_ref[8 * c : 8 * c + 8]
        rb = rb_ref[8 * c : 8 * c + 8]
        before = jnp.where(even, rb, ra)
        after = jnp.where(even, ra, rb)
        rows = [before[0:4], before[4:8]] + [part_ref[c, i] for i in range(SIDE)] + [after[0:4], after[4:8]]
        left = jnp.concatenate([r[0:2] for r in rows], axis=0)
        right = jnp.concatenate([r[2:4] for r in rows], axis=0)
        near_ref[16 * c : 16 * c + 16] = jnp.where(leaf_even, right, left)
        far_ref[16 * c : 16 * c + 16] = jnp.where(leaf_even, left, right)
    ma = ra_ref[24:48, 0:16]
    mb = rb_ref[24:48, 0:16]
    window = jnp.concatenate(
        [m_ref[:, 0:16], jnp.where(even, mb, ma), jnp.where(even, ma, mb), jnp.zeros((24, 80), F32)], axis=1
    )
    blocks = f_ref[...] + ra_ref[48:72, 0:128]
    m_out[...] = window
    f_out[...] = blocks
    none = jnp.zeros((24, 128), F32)
    near_ref[48:72, 0:128] = jnp.concatenate([none[:, 0:48], window[:, 0:48], none[:, 0:32]], axis=1)
    near_ref[48:72, 128:256] = none
    far_ref[48:72, 0:128] = window
    far_ref[48:72, 128:256] = none
    near_ref[72:96, 0:128] = blocks
    near_ref[72:96, 128:256] = none


def slab_halo(ra_ref, rb_ref, s_ref, w_ref, stage_s, stage_w):
    even = position()[2] == 0
    halo = []
    for c in range(3):
        ra = ra_ref[8 * c : 8 * c + 8]
        rb = rb_ref[8 * c : 8 * c + 8]
        halo.append(jnp.concatenate([jnp.where(even, rb, ra), jnp.where(even, ra, rb)], axis=0))
    n = row_of(LEAVES)
    i = (n >> 2) - 2
    ox = jnp.where(i >= 0, i + 4, i).astype(F32) - 1.5
    oy = (n & 3).astype(F32) - 1.5
    build_features(halo[0], halo[1], halo[2], ox, oy, None, stage_s, stage_w, None, s_ref, w_ref, 0, False)


def leaf_halo(which, r_ref, s_ref, w_ref, stage_s, stage_w):
    info = position()
    leaf_even = info[3] == 0
    to_right = leaf_even if which == 0 else jnp.logical_not(leaf_even)
    valid = jnp.float32(1.0) if which == 0 else info[4].astype(F32)
    n = row_of(LEAVES)
    ox = (n >> 1).astype(F32) - 3.5
    side = (n & 1).astype(F32)
    oy = jnp.where(to_right, side + 4.0, side - 2.0) - 1.5
    build_features(
        r_ref[0:16], r_ref[16:32], r_ref[32:48] * valid, ox, oy, None, stage_s, stage_w, None, s_ref, w_ref, 0, False
    )


def near_halo(r_ref, s_ref, w_ref, stage_s, stage_w):
    leaf_halo(0, r_ref, s_ref, w_ref, stage_s, stage_w)


def far_halo(r_ref, s_ref, w_ref, stage_s, stage_w):
    leaf_halo(1, r_ref, s_ref, w_ref, stage_s, stage_w)


def pack_near(r_ref, f_ref, send_ref, after_ref, f_out, send_out):
    blocks = f_ref[...] + r_ref[72:96, 0:128]
    f_out[...] = blocks
    send_out[0:72] = send_ref[...]
    send_out[72:96, 0:128] = blocks
    send_out[72:96, 128:256] = jnp.zeros((24, 128), F32)


def chosen(index, values):
    if all(v == values[0] for v in values):
        return values[0]
    out = values[-1]
    for n in range(len(values) - 2, -1, -1):
        out = jnp.where(index == n, values[n], out)
    return out


def direct(tables, by_side, zero, extra, extra_in, mask_ref, t_ref, s_ref, w_ref, *refs):
    if zero:
        acc_ref, rows_ref = refs
        acc_ref[...] = jnp.zeros_like(acc_ref)
        near_mask = jnp.concatenate([mask_ref[i] for i in range(SIDE)], axis=0).astype(F32)
        for o in range(16):
            rows_ref[o, :, 0, :] = jnp.broadcast_to(near_mask[:, o : o + 1], (LEAVES, SIZE))
        rows_ref[16, :, 0, :] = jnp.ones((LEAVES, SIZE), F32)
        mask_ref = rows_ref
    else:
        acc_ref = refs[extra_in + 1]
        acc_ref[...] = refs[0][...]
        others = refs[1 : extra_in + 1] + refs[extra_in + 2 :]
    count = tables.shape[1]

    def step(index, unused):
        for n in range(count):
            t, s, o = (chosen(index, [int(v) for v in tables[:, n, c]]) for c in range(3))
            distance = jnp.dot(s_ref[s], t_ref[t], preferred_element_type=F32)
            kernel = 1.0 / distance
            high = kernel.astype(BF16)
            low = (kernel - high.astype(F32)).astype(BF16)
            w = w_ref[s]
            total = jnp.dot(w, high, preferred_element_type=F32) + jnp.dot(w, low, preferred_element_type=F32)
            if isinstance(o, int) and o == 16:
                acc_ref[t] = acc_ref[t] + total
            else:
                acc_ref[t] = acc_ref[t] + mask_ref[o, t] * total
        return 0

    if by_side:
        step(position()[3], 0)
    elif tables.shape[0] == 1:
        step(0, 0)
    else:
        lax.fori_loop(0, tables.shape[0], step, 0)
    if extra is not None:
        extra(*others)


def pair_table(kind, to_right=False):
    out = []
    for t in range(LEAVES):
        i, j = divmod(t, SIDE)
        for a, b in near_steps:
            o = cycle_steps.index((a, b)) if max(abs(a), abs(b)) == 2 else 16
            si, sj = i + a, j + b
            in_row, in_column = 0 <= si < SIDE, 0 <= sj < SIDE
            if kind == "own" and in_row and in_column:
                out.append((t, si * SIDE + sj, o))
            if kind == "slab" and not in_row and in_column:
                out.append((t, ((si + 2) if si < 0 else (si - 2)) * SIDE + sj, o))
            if kind == "leaf" and not in_column and (sj >= SIDE) == to_right:
                out.append((t, (si + 2) * 2 + (sj - SIDE if to_right else sj + 2), o))
    return np.array(out, np.int32)


def translate(groups, h_ref, a_ref, out_ref):
    for group, (tx, ty, weight) in enumerate(groups):
        span = slice(128 * group, 128 * group + 128)
        square = tx * tx + ty * ty
        inv_x = tx / square
        inv_y = -ty / square
        re = weight * inv_x
        im = weight * inv_y
        h_ref[0, :, span] = re
        h_ref[1, :, span] = im
        for order in range(1, 2 * ORDER - 1):
            re, im = (re * inv_x - im * inv_y) * float(order), (re * inv_y + im * inv_x) * float(order)
            h_ref[2 * order, :, span] = re
            h_ref[2 * order + 1, :, span] = im
    lane = lax.broadcasted_iota(jnp.int32, (LEAVES, 128), 1)
    table = jnp.zeros((LEAVES, 128), F32)
    half = ORDER // 2
    for first in (0, half):
        sums_re = [None] * half
        sums_im = [None] * half
        for group in range(len(groups)):
            span = slice(128 * group, 128 * group + 128)
            for k_ in range(ORDER):
                a_re = a_ref[k_ : k_ + 1, span]
                a_im = a_ref[ORDER + k_ : ORDER + k_ + 1, span]
                for m in range(half):
                    at = first + m + k_
                    h_re = h_ref[2 * at, :, span]
                    h_im = h_ref[2 * at + 1, :, span]
                    term_re = h_re * a_re - h_im * a_im
                    term_im = h_re * a_im + h_im * a_re
                    sums_re[m] = term_re if sums_re[m] is None else sums_re[m] + term_re
                    sums_im[m] = term_im if sums_im[m] is None else sums_im[m] + term_im
        for m in range(half):
            factor = 1.0 / math.factorial(first + m)
            table = jnp.where(lane == first + m, jnp.sum(sums_re[m], 1, keepdims=True) * factor, table)
            table = jnp.where(lane == 64 + first + m, jnp.sum(sums_im[m], 1, keepdims=True) * factor, table)
    out_ref[...] = table


def source_scale():
    row = row_of(24)
    which = jnp.where(row >= ORDER, row - ORDER, row)
    scale = jnp.zeros((24, 1), F32)
    for k_ in range(ORDER):
        scale = jnp.where(which == k_, (-1.0) ** (k_ + 1) / math.factorial(k_), scale)
    return scale


def leaf_field(nm_ref, m_ref, r1_ref, r2_ref, out_ref, h_ref, a_ref):
    info = position()
    leaf_even = info[3] == 0
    valid = info[4].astype(F32)
    n = row_of(LEAVES)
    ti = n >> 2
    tj = n & 3
    lane = lax.broadcasted_iota(jnp.int32, (LEAVES, 128), 1)
    near_mask = jnp.concatenate([nm_ref[i] for i in range(SIDE)], axis=0).astype(F32)
    near_shift = jnp.where(leaf_even, 4, -4)
    second = lane >= 48
    place = jnp.where(second, lane - 48, lane)
    k = place >> 4
    r = place & 15
    si = jnp.where(k == 0, r >> 2, jnp.where(k == 1, (r >> 2) - 4, (r >> 2) + 4))
    groups = []
    for column, lanes in ((jnp.where(second, near_shift, 0), 96), (-near_shift, 48)):
        dx = si - ti
        dy = (r & 3) + column - tj
        reach = jnp.maximum(jnp.abs(dx), jnp.abs(dy))
        weight = jnp.where(reach >= 3, 1.0, 0.0).astype(F32)
        for o, (a, b) in enumerate(cycle_steps):
            hit = jnp.logical_and(dx == a, dy == b)
            weight = jnp.where(hit, 1.0 - near_mask[:, o : o + 1], weight)
        inside = lane < lanes
        used = jnp.logical_and(reach >= 2, inside)
        groups.append(
            (
                jnp.where(used, dx.astype(F32), 1.0),
                jnp.where(used, dy.astype(F32), 1.0),
                jnp.where(inside, weight, 0.0),
            )
        )
    scale = source_scale()
    a_ref[:, 0:128] = (m_ref[...] + r1_ref[48:72, 0:128]) * scale
    a_ref[:, 128:256] = r2_ref[48:72, 0:128] * (valid * scale)
    translate(groups, h_ref, a_ref, out_ref)


def finish(part_ref, acc_ref, near_ref, f_ref, got_ref, out_ref, h_ref, a_ref, l_ref):
    info = position()
    n = row_of(LEAVES)
    ti = n >> 2
    tj = n & 3
    lane = lax.broadcasted_iota(jnp.int32, (LEAVES, 128), 1)
    bx = (lane >> 2) - info[0]
    by = (lane & 3) - info[1]
    remote = jnp.maximum(jnp.abs(bx), jnp.abs(by)) >= 2
    tx = jnp.where(remote, (bx * SIDE - ti).astype(F32) + 1.5, 1.0)
    ty = jnp.where(remote, (by * SIDE - tj).astype(F32) + 1.5, 1.0)
    weight = jnp.where(remote, 1.0, 0.0).astype(F32)
    a_ref[...] = (f_ref[...] + got_ref[...]) * source_scale()
    translate([(tx, ty, weight)], h_ref, a_ref, l_ref)
    local = l_ref[...] + near_ref[...]
    wx = own_rows(part_ref, 0)
    wy = own_rows(part_ref, 1)
    ox, oy = leaf_offsets()
    x = wx + ox
    y = wy + oy
    rows = lambda at: acc_ref[:, at, :] + acc_ref[:, at + 1, :] + acc_ref[:, at + 2, :]
    total = rows(0)
    sum_re = x * total - rows(3)
    sum_im = rows(6) - y * total
    p_re = jnp.ones_like(wx)
    p_im = jnp.zeros_like(wx)
    for m in range(ORDER):
        if m:
            p_re, p_im = p_re * wx - p_im * wy, p_re * wy + p_im * wx
        l_re = local[:, m : m + 1]
        l_im = local[:, 64 + m : 65 + m]
        sum_re = sum_re + (l_re * p_re - l_im * p_im)
        sum_im = sum_im + (l_re * p_im + l_im * p_re)
    sum_re = sum_re * (1.0 / TWO_PI)
    sum_im = sum_im * (1.0 / TWO_PI)
    for i in range(SIDE):
        out_ref[0, i] = sum_im[4 * i : 4 * i + 4]
        out_ref[1, i] = sum_re[4 * i : 4 * i + 4]


V = pl.BlockSpec(memory_space=pltpu.VMEM)
S = pl.BlockSpec(memory_space=pltpu.SMEM)
A = pl.BlockSpec(memory_space=pl.ANY)


def shaped(*shape, dtype=F32):
    return jax.ShapeDtypeStruct(shape, dtype)


def call(kernel, name, in_specs, outs, scratch, cost, aliases=None):
    return pl.pallas_call(
        kernel,
        out_shape=outs,
        in_specs=in_specs,
        out_specs=jax.tree.map(lambda unused: V, outs),
        scratch_shapes=scratch,
        name=name,
        input_output_aliases=aliases or {},
        cost_estimate=pl.CostEstimate(flops=cost, bytes_accessed=1 << 20, transcendentals=0),
        compiler_params=pltpu.CompilerParams(vmem_limit_bytes=VMEM_LIMIT),
    )


def features_out(count):
    return [shaped(count, SIZE, FEATURES, dtype=BF16), shaped(count, 16, SIZE, dtype=BF16)]


def stages(with_target):
    out = [pltpu.VMEM((LEAVES, FEATURES, SIZE), F32), pltpu.VMEM((LEAVES, 16, SIZE), F32)]
    return ([pltpu.VMEM((LEAVES, FEATURES, SIZE), F32)] if with_target else []) + out


SMALL = 4_000_000
PAIR = 400_000_000


def run_direct(name, tables, mask, feats, acc, by_side=False, extra=None, ins=(), outs=(), scratch=()):
    zero = acc is None
    args = [mask, *feats] + ([] if zero else [acc]) + list(ins)
    got = call(
        functools.partial(direct, tables, by_side, zero, extra, len(ins)),
        name,
        [V] * len(args),
        [shaped(LEAVES, 16, SIZE), *outs],
        list(scratch),
        PAIR * (1 if by_side else tables.shape[0]) * tables.shape[1],
        {} if zero else {4: 0},
    )(*args)
    return got if outs else got[0]


def far_scratch(width):
    return [pltpu.VMEM((4 * ORDER - 2, LEAVES, width), F32), pltpu.VMEM((24, width), F32)]


def body(particles, near_mask):
    turned = near_mask.transpose(1, 2, 0)
    t0, s0, w0, m0, f0, send_a, send_b = call(
        prepare_own,
        "prepare_own",
        [V],
        [shaped(LEAVES, FEATURES, SIZE, dtype=BF16), *features_out(LEAVES), shaped(24, 128), shaped(24, 128)]
        + [shaped(SLAB_ROWS, SIZE)] * 2,
        stages(True),
        SMALL,
    )(particles)
    recv_a = swap(send_a, "core")
    recv_b = swap(send_b, "slab")
    own = pair_table("own")
    feats = (t0, s0, w0)
    acc, mask = run_direct(
        "direct_own_0", own[:98].reshape(2, 49, 3), turned, feats, None, outs=[shaped(17, LEAVES, 1, SIZE)]
    )
    m1, f1, send_near, send_far = call(
        pack_slab,
        "pack_slab",
        [V, V, V, V, V, A],
        [shaped(24, 128), shaped(24, 128), shaped(LEAF_ROWS, SIZE), shaped(72, SIZE)],
        [],
        SMALL,
    )(particles, recv_a, recv_b, m0, f0, acc)
    send_near, acc = lax.optimization_barrier((send_near, acc))
    recv_near = swap(send_near, "leaf_near")
    built = dict(outs=features_out(LEAVES), scratch=stages(False))
    acc, s1, w1 = run_direct(
        "direct_own_1", own[None, 98:147], mask, feats, acc, extra=slab_halo, ins=(recv_a, recv_b), **built
    )
    f2, send_far = call(
        pack_near, "pack_near", [V, V, V, A], [shaped(24, 128), shaped(LEAF_ROWS, SIZE)], [], SMALL
    )(recv_near, f1, send_far, acc)
    send_far, acc = lax.optimization_barrier((send_far, acc))
    recv_far = swap(send_far, "leaf_far")
    acc, s2, w2 = run_direct(
        "direct_own_2", own[None, 147:], mask, feats, acc, extra=near_halo, ins=(recv_near,), **built
    )
    recv_far, acc = lax.optimization_barrier((recv_far, acc))
    f3 = f2 + recv_far[72:96, 0:128]
    f3, acc = lax.optimization_barrier((f3, acc))
    got = swap(f3, "z_near")
    acc, s3, w3 = run_direct(
        "direct_slab",
        pair_table("slab").reshape(2, 42, 3),
        mask,
        (t0, s1, w1),
        acc,
        extra=far_halo,
        ins=(recv_far,),
        **built,
    )
    got, acc = lax.optimization_barrier((got, acc))
    f4 = f3 + got
    f4, acc = lax.optimization_barrier((f4, acc))
    got = swap(f4, "z_far")
    right = pair_table("leaf", True)
    left = pair_table("leaf", False)
    near_pairs = np.stack([right, left])
    far_pairs = np.stack([left, right])
    acc, local = run_direct(
        "direct_leaf_near",
        near_pairs,
        mask,
        (t0, s2, w2),
        acc,
        True,
        extra=leaf_field,
        ins=(turned, m1, recv_near, recv_far),
        outs=[shaped(LEAVES, 128)],
        scratch=far_scratch(256),
    )
    got, acc = lax.optimization_barrier((got, acc))
    f5 = f4 + got
    f5, acc = lax.optimization_barrier((f5, acc))
    got = swap(f5, "x_near")
    acc = run_direct("direct_leaf_far_0", far_pairs[:, :30], mask, (t0, s3, w3), acc, True)
    got, acc = lax.optimization_barrier((got, acc))
    f6 = f5 + got
    f6, acc = lax.optimization_barrier((f6, acc))
    got = swap(f6, "x_far")
    acc = run_direct("direct_leaf_far_1", far_pairs[:, 30:], mask, (t0, s3, w3), acc, True)
    got, acc = lax.optimization_barrier((got, acc))
    return call(
        finish,
        "finish",
        [V] * 5,
        shaped(2, SIDE, SIDE, SIZE),
        far_scratch(128) + [pltpu.VMEM((LEAVES, 128), F32)],
        SMALL,
    )(particles, acc, local, f6, got)


def solution(mesh):
    finer = Mesh(mesh.devices.reshape(4, 4, 2, mesh.shape["leaf"]), ALL)
    in_specs = (P(None, SLAB, "leaf", None), P(None, SLAB, "leaf"))
    out_specs = P(None, SLAB, "leaf", None)
    run = jax.shard_map(body, mesh=finer, in_specs=in_specs, out_specs=out_specs, check_vma=False)

    def whole(particles, near_mask):
        with jax.sharding.use_abstract_mesh(mesh.abstract_mesh):
            return run(particles, near_mask)

    return run
```

```python
import functools
import math

import jax
import jax.numpy as jnp
import numpy as np
from jax import lax
from jax.experimental import pallas as pl
from jax.experimental.pallas import tpu as pltpu
from jax.sharding import Mesh
from jax.sharding import PartitionSpec as P

ORDER = 10
SIDE = 4
LEAVES = 16
SIZE = 256
FEATURES = 32
DELTA_SQUARED = 0.0025
TWO_PI = 2.0 * math.pi
SLAB = ("slab_0", "slab_1", "slab_2")
ALL = ("slab_0", "slab_1", "slab_2", "leaf")
F32 = jnp.float32
BF16 = jnp.bfloat16
VMEM_LIMIT = 6 << 20
cycle_steps = [(a, b) for a in range(-2, 3) for b in range(-2, 3) if max(abs(a), abs(b)) == 2]
near_steps = [(a, b) for a in range(-2, 3) for b in range(-2, 3)]


def exchange_pairs(partner):
    pairs = []
    for x in range(4):
        for z in range(4):
            for c in range(2):
                for y in range(4):
                    other = partner(x, z, c, y)
                    if other is not None:
                        a, b, d, e = other
                        pairs.append((((x * 4 + z) * 2 + c) * 4 + y, ((a * 4 + b) * 2 + d) * 4 + e))
    return pairs


def slab_between_chips(x, z, c, y):
    slab = (x * 4 + z) * 2 + c
    other = slab + 1 if c == 1 else slab - 1
    if not 0 <= other < 32:
        return None
    return (other // 8, (other // 2) % 4, other % 2, y)


def near_side(k):
    return k ^ 1


def far_side(k):
    return 3 - k


SWAPS = {
    "core": exchange_pairs(lambda x, z, c, y: (x, z, 1 - c, y)),
    "slab": exchange_pairs(slab_between_chips),
    "leaf_near": exchange_pairs(lambda x, z, c, y: (x, z, c, near_side(y))),
    "leaf_far": exchange_pairs(lambda x, z, c, y: (x, z, c, far_side(y))),
    "z_near": exchange_pairs(lambda x, z, c, y: (x, near_side(z), c, y)),
    "z_far": exchange_pairs(lambda x, z, c, y: (x, far_side(z), c, y)),
    "x_near": exchange_pairs(lambda x, z, c, y: (near_side(x), z, c, y)),
    "x_far": exchange_pairs(lambda x, z, c, y: (far_side(x), z, c, y)),
}


def swap(value, name):
    return lax.ppermute(value, ALL, SWAPS[name])


def pieces(value, count):
    parts = []
    for unused in range(count):
        part = value.astype(BF16).astype(F32)
        parts.append(part)
        value = value - part
    return parts


def build_features(wx, wy, g, ox, oy, stage_t, stage_s, stage_w, t_ref, s_ref, w_ref, first, with_target):
    count = wx.shape[0]
    one = jnp.ones_like(wx)
    zero = jnp.zeros_like(wx)
    coarse_x = jnp.round(wx * 32.0) * (1.0 / 32.0)
    coarse_y = jnp.round(wy * 32.0) * (1.0 / 32.0)
    fine_x = wx - coarse_x
    fine_y = wy - coarse_y
    big_x = coarse_x + ox
    big_y = coarse_y + oy
    big = pieces(big_x * big_x + big_y * big_y, 2)
    rest = 2.0 * (big_x * fine_x + big_y * fine_y) + fine_x * fine_x + fine_y * fine_y
    px = pieces(fine_x, 2)
    py = pieces(fine_y, 2)
    if with_target:
        rows = [big_x, big_y, big[0], big[1], one, one, zero, zero]
        rows += [big_x, big_x, big_y, big_y, px[0], px[1], py[0], py[1]]
        rows += [px[0], px[0], px[1], py[0], py[0], py[1]]
        rows += pieces(rest + DELTA_SQUARED, 3) + [one, one, one]
        rows += [zero] * (FEATURES - len(rows))
        for f, row in enumerate(rows):
            stage_t[:count, f, :] = row
    twice = lambda v: -2.0 * v
    rows = [twice(big_x), twice(big_y), one, one, big[0], big[1], zero, zero]
    rows += [twice(px[0]), twice(px[1]), twice(py[0]), twice(py[1])]
    rows += [twice(big_x), twice(big_x), twice(big_y), twice(big_y)]
    rows += [twice(px[0]), twice(px[1]), twice(px[0]), twice(py[0]), twice(py[1]), twice(py[0])]
    rows += [one, one, one] + pieces(rest, 3)
    rows += [zero] * (FEATURES - len(rows))
    for f, row in enumerate(rows):
        stage_s[:count, f, :] = row
    rows = pieces(g, 3) + pieces(g * (wx + ox), 3) + pieces(g * (wy + oy), 3)
    rows += [zero] * (16 - len(rows))
    for f, row in enumerate(rows):
        stage_w[:count, f, :] = row
    for n in range(count):
        if with_target:
            t_ref[first + n] = stage_t[n].astype(BF16)
        s_ref[first + n] = jnp.transpose(stage_s[n]).astype(BF16)
        w_ref[first + n] = stage_w[n].astype(BF16)


def power_list(base_re, base_im, count):
    re = [jnp.ones_like(base_re)]
    im = [jnp.zeros_like(base_im)]
    for unused in range(1, count):
        a, b = re[-1], im[-1]
        re.append(a * base_re - b * base_im)
        im.append(a * base_im + b * base_re)
    return re, im


def row_of(n):
    return lax.broadcasted_iota(jnp.int32, (n, 1), 0)


def leaf_offsets():
    n = row_of(LEAVES)
    ox = (n >> 2).astype(F32) - 1.5
    oy = (n & 3).astype(F32) - 1.5
    return ox, oy


def own_rows(ref, part):
    return jnp.concatenate([ref[part, i] for i in range(SIDE)], axis=0)


def position():
    slab = lax.axis_index(SLAB)
    leaf = lax.axis_index("leaf")
    between = jnp.logical_and(leaf > 0, leaf < 3).astype(jnp.int32)
    return slab, leaf, slab & 1, leaf & 1, between


SLAB_ROWS = 72
LEAF_ROWS = 96


def prepare_own(part_ref, t_ref, s_ref, w_ref, m_ref, f_ref, a_ref, b_ref, stage_t, stage_s, stage_w):
    info = position()
    wx = own_rows(part_ref, 0)
    wy = own_rows(part_ref, 1)
    g = own_rows(part_ref, 2)
    ox, oy = leaf_offsets()
    lane = lax.broadcasted_iota(jnp.int32, (LEAVES, 128), 1)
    table = jnp.zeros((LEAVES, 128), F32)
    for start, base_re, base_im in ((0, wx, wy), (32, wx + ox, wy + oy)):
        re, im = power_list(base_re, base_im, ORDER)
        for k in range(ORDER):
            table = jnp.where(lane == start + k, jnp.sum(g * re[k], 1, keepdims=True), table)
            if k:
                table = jnp.where(lane == start + ORDER + k, jnp.sum(g * im[k], 1, keepdims=True), table)
    turned = jnp.transpose(table)
    leaf_part = jnp.concatenate([turned[0:24], jnp.zeros((24, 112), F32)], axis=1)
    block_part = jnp.sum(turned[32:56], axis=1, keepdims=True)
    me = info[0] * 4 + info[1]
    wide = lax.broadcasted_iota(jnp.int32, (24, 128), 1)
    block_row = jnp.where(wide == me, block_part, 0.0)
    m_ref[...] = leaf_part
    f_ref[...] = block_row
    even = info[2] == 0
    for c in range(3):
        first = jnp.concatenate([part_ref[c, 0], part_ref[c, 1]], axis=0)
        last = jnp.concatenate([part_ref[c, 2], part_ref[c, 3]], axis=0)
        a_ref[8 * c : 8 * c + 8] = jnp.where(even, last, first)
        b_ref[8 * c : 8 * c + 8] = jnp.where(even, first, last)
    none = jnp.zeros((24, 128), F32)
    for ref in (a_ref, b_ref):
        ref[24:48, 0:128] = leaf_part
        ref[24:48, 128:256] = none
        ref[48:72, 0:128] = block_row
        ref[48:72, 128:256] = none
    build_features(wx, wy, g, ox, oy, stage_t, stage_s, stage_w, t_ref, s_ref, w_ref, 0, True)


def pack_slab(part_ref, ra_ref, rb_ref, m_ref, f_ref, after_ref, m_out, f_out, near_ref, far_ref):
    info = position()
    even = info[2] == 0
    leaf_even = info[3] == 0
    for c in range(3):
        ra = ra_ref[8 * c : 8 * c + 8]
        rb = rb_ref[8 * c : 8 * c + 8]
        before = jnp.where(even, rb, ra)
        after = jnp.where(even, ra, rb)
        rows = [before[0:4], before[4:8]] + [part_ref[c, i] for i in range(SIDE)] + [after[0:4], after[4:8]]
        left = jnp.concatenate([r[0:2] for r in rows], axis=0)
        right = jnp.concatenate([r[2:4] for r in rows], axis=0)
        near_ref[16 * c : 16 * c + 16] = jnp.where(leaf_even, right, left)
        far_ref[16 * c : 16 * c + 16] = jnp.where(leaf_even, left, right)
    ma = ra_ref[24:48, 0:16]
    mb = rb_ref[24:48, 0:16]
    window = jnp.concatenate(
        [m_ref[:, 0:16], jnp.where(even, mb, ma), jnp.where(even, ma, mb), jnp.zeros((24, 80), F32)], axis=1
    )
    blocks = f_ref[...] + ra_ref[48:72, 0:128]
    m_out[...] = window
    f_out[...] = blocks
    none = jnp.zeros((24, 128), F32)
    near_ref[48:72, 0:128] = jnp.concatenate([none[:, 0:48], window[:, 0:48], none[:, 0:32]], axis=1)
    near_ref[48:72, 128:256] = none
    far_ref[48:72, 0:128] = window
    far_ref[48:72, 128:256] = none
    near_ref[72:96, 0:128] = blocks
    near_ref[72:96, 128:256] = none


def slab_halo(ra_ref, rb_ref, s_ref, w_ref, stage_s, stage_w):
    even = position()[2] == 0
    halo = []
    for c in range(3):
        ra = ra_ref[8 * c : 8 * c + 8]
        rb = rb_ref[8 * c : 8 * c + 8]
        halo.append(jnp.concatenate([jnp.where(even, rb, ra), jnp.where(even, ra, rb)], axis=0))
    n = row_of(LEAVES)
    i = (n >> 2) - 2
    ox = jnp.where(i >= 0, i + 4, i).astype(F32) - 1.5
    oy = (n & 3).astype(F32) - 1.5
    build_features(halo[0], halo[1], halo[2], ox, oy, None, stage_s, stage_w, None, s_ref, w_ref, 0, False)


def leaf_halo(which, r_ref, s_ref, w_ref, stage_s, stage_w):
    info = position()
    leaf_even = info[3] == 0
    to_right = leaf_even if which == 0 else jnp.logical_not(leaf_even)
    valid = jnp.float32(1.0) if which == 0 else info[4].astype(F32)
    n = row_of(LEAVES)
    ox = (n >> 1).astype(F32) - 3.5
    side = (n & 1).astype(F32)
    oy = jnp.where(to_right, side + 4.0, side - 2.0) - 1.5
    build_features(
        r_ref[0:16], r_ref[16:32], r_ref[32:48] * valid, ox, oy, None, stage_s, stage_w, None, s_ref, w_ref, 0, False
    )


def near_halo(r_ref, s_ref, w_ref, stage_s, stage_w):
    leaf_halo(0, r_ref, s_ref, w_ref, stage_s, stage_w)


def far_halo(r_ref, s_ref, w_ref, stage_s, stage_w):
    leaf_halo(1, r_ref, s_ref, w_ref, stage_s, stage_w)


def pack_near(r_ref, f_ref, send_ref, after_ref, f_out, send_out):
    blocks = f_ref[...] + r_ref[72:96, 0:128]
    f_out[...] = blocks
    send_out[0:72] = send_ref[...]
    send_out[72:96, 0:128] = blocks
    send_out[72:96, 128:256] = jnp.zeros((24, 128), F32)


def chosen(index, values):
    if all(v == values[0] for v in values):
        return values[0]
    out = values[-1]
    for n in range(len(values) - 2, -1, -1):
        out = jnp.where(index == n, values[n], out)
    return out


HEAD_START = (
    ((85, 80, 81, 70), (0, -14, -15, -6), (0, -12, -18, -6)),
    ((86, 58, 39, 47), (0, -13, -20, -11), (0, -14, -26, -11)),
)
FLEX_STEPS = (22, 43, 65, 83)


def early_bodies():
    slab, leaf, core, unused, unused = position()
    ahead = [
        chosen((slab >> 1) & 3, by_z) + chosen(slab >> 3, by_x) + chosen(leaf, by_y)
        for by_z, by_x, by_y in HEAD_START
    ]
    ahead = jnp.where(core == 0, ahead[0], ahead[1])
    return sum((ahead >= step).astype(jnp.int32) for step in FLEX_STEPS)


def direct(tables, mode, zero, extra, extra_in, mask_ref, t_ref, s_ref, w_ref, *refs):
    if zero:
        acc_ref, rows_ref = refs
        acc_ref[...] = jnp.zeros_like(acc_ref)
        near_mask = jnp.concatenate([mask_ref[i] for i in range(SIDE)], axis=0).astype(F32)
        for o in range(16):
            rows_ref[o, :, 0, :] = jnp.broadcast_to(near_mask[:, o : o + 1], (LEAVES, SIZE))
        rows_ref[16, :, 0, :] = jnp.ones((LEAVES, SIZE), F32)
        mask_ref = rows_ref
    else:
        acc_ref = refs[extra_in + 1]
        acc_ref[...] = refs[0][...]
        others = refs[1 : extra_in + 1] + refs[extra_in + 2 :]
    count = tables.shape[1]

    def step(index, unused):
        for n in range(count):
            t, s, o = (chosen(index, [int(v) for v in tables[:, n, c]]) for c in range(3))
            distance = jnp.dot(s_ref[s], t_ref[t], preferred_element_type=F32)
            kernel = 1.0 / distance
            high = kernel.astype(BF16)
            low = (kernel - high.astype(F32)).astype(BF16)
            w = w_ref[s]
            total = jnp.dot(w, high, preferred_element_type=F32) + jnp.dot(w, low, preferred_element_type=F32)
            if isinstance(o, int) and o == 16:
                acc_ref[t] = acc_ref[t] + total
            else:
                acc_ref[t] = acc_ref[t] + mask_ref[o, t] * total
        return 0

    if mode == "side":
        step(position()[3], 0)
    elif mode == "early":
        lax.fori_loop(0, early_bodies(), step, 0)
    elif mode == "late":
        lax.fori_loop(early_bodies(), tables.shape[0], step, 0)
    else:
        step(0, 0)
    if extra is not None:
        extra(*others)


def pair_table(kind, to_right=False):
    out = []
    for t in range(LEAVES):
        i, j = divmod(t, SIDE)
        for a, b in near_steps:
            o = cycle_steps.index((a, b)) if max(abs(a), abs(b)) == 2 else 16
            si, sj = i + a, j + b
            in_row, in_column = 0 <= si < SIDE, 0 <= sj < SIDE
            if kind == "own" and in_row and in_column:
                out.append((t, si * SIDE + sj, o))
            if kind == "slab" and not in_row and in_column:
                out.append((t, ((si + 2) if si < 0 else (si - 2)) * SIDE + sj, o))
            if kind == "leaf" and not in_column and (sj >= SIDE) == to_right:
                out.append((t, (si + 2) * 2 + (sj - SIDE if to_right else sj + 2), o))
    return np.array(out, np.int32)


def translate(groups, h_ref, a_ref, out_ref):
    for group, (tx, ty, weight) in enumerate(groups):
        span = slice(128 * group, 128 * group + 128)
        square = tx * tx + ty * ty
        inv_x = tx / square
        inv_y = -ty / square
        re = weight * inv_x
        im = weight * inv_y
        h_ref[0, :, span] = re
        h_ref[1, :, span] = im
        for order in range(1, 2 * ORDER - 1):
            re, im = (re * inv_x - im * inv_y) * float(order), (re * inv_y + im * inv_x) * float(order)
            h_ref[2 * order, :, span] = re
            h_ref[2 * order + 1, :, span] = im
    lane = lax.broadcasted_iota(jnp.int32, (LEAVES, 128), 1)
    table = jnp.zeros((LEAVES, 128), F32)
    half = ORDER // 2
    for first in (0, half):
        sums_re = [None] * half
        sums_im = [None] * half
        for group in range(len(groups)):
            span = slice(128 * group, 128 * group + 128)
            for k_ in range(ORDER):
                a_re = a_ref[k_ : k_ + 1, span]
                a_im = a_ref[ORDER + k_ : ORDER + k_ + 1, span]
                for m in range(half):
                    at = first + m + k_
                    h_re = h_ref[2 * at, :, span]
                    h_im = h_ref[2 * at + 1, :, span]
                    term_re = h_re * a_re - h_im * a_im
                    term_im = h_re * a_im + h_im * a_re
                    sums_re[m] = term_re if sums_re[m] is None else sums_re[m] + term_re
                    sums_im[m] = term_im if sums_im[m] is None else sums_im[m] + term_im
        for m in range(half):
            factor = 1.0 / math.factorial(first + m)
            table = jnp.where(lane == first + m, jnp.sum(sums_re[m], 1, keepdims=True) * factor, table)
            table = jnp.where(lane == 64 + first + m, jnp.sum(sums_im[m], 1, keepdims=True) * factor, table)
    out_ref[...] = table


def source_scale():
    row = row_of(24)
    which = jnp.where(row >= ORDER, row - ORDER, row)
    scale = jnp.zeros((24, 1), F32)
    for k_ in range(ORDER):
        scale = jnp.where(which == k_, (-1.0) ** (k_ + 1) / math.factorial(k_), scale)
    return scale


def leaf_field(nm_ref, m_ref, r1_ref, r2_ref, out_ref, h_ref, a_ref):
    info = position()
    leaf_even = info[3] == 0
    valid = info[4].astype(F32)
    n = row_of(LEAVES)
    ti = n >> 2
    tj = n & 3
    lane = lax.broadcasted_iota(jnp.int32, (LEAVES, 128), 1)
    near_mask = jnp.concatenate([nm_ref[i] for i in range(SIDE)], axis=0).astype(F32)
    near_shift = jnp.where(leaf_even, 4, -4)
    second = lane >= 48
    place = jnp.where(second, lane - 48, lane)
    k = place >> 4
    r = place & 15
    si = jnp.where(k == 0, r >> 2, jnp.where(k == 1, (r >> 2) - 4, (r >> 2) + 4))
    groups = []
    for column, lanes in ((jnp.where(second, near_shift, 0), 96), (-near_shift, 48)):
        dx = si - ti
        dy = (r & 3) + column - tj
        reach = jnp.maximum(jnp.abs(dx), jnp.abs(dy))
        weight = jnp.where(reach >= 3, 1.0, 0.0).astype(F32)
        for o, (a, b) in enumerate(cycle_steps):
            hit = jnp.logical_and(dx == a, dy == b)
            weight = jnp.where(hit, 1.0 - near_mask[:, o : o + 1], weight)
        inside = lane < lanes
        used = jnp.logical_and(reach >= 2, inside)
        groups.append(
            (
                jnp.where(used, dx.astype(F32), 1.0),
                jnp.where(used, dy.astype(F32), 1.0),
                jnp.where(inside, weight, 0.0),
            )
        )
    scale = source_scale()
    a_ref[:, 0:128] = (m_ref[...] + r1_ref[48:72, 0:128]) * scale
    a_ref[:, 128:256] = r2_ref[48:72, 0:128] * (valid * scale)
    translate(groups, h_ref, a_ref, out_ref)


def finish(part_ref, acc_ref, near_ref, f_ref, got_ref, out_ref, h_ref, a_ref, l_ref):
    info = position()
    n = row_of(LEAVES)
    ti = n >> 2
    tj = n & 3
    lane = lax.broadcasted_iota(jnp.int32, (LEAVES, 128), 1)
    bx = (lane >> 2) - info[0]
    by = (lane & 3) - info[1]
    remote = jnp.maximum(jnp.abs(bx), jnp.abs(by)) >= 2
    tx = jnp.where(remote, (bx * SIDE - ti).astype(F32) + 1.5, 1.0)
    ty = jnp.where(remote, (by * SIDE - tj).astype(F32) + 1.5, 1.0)
    weight = jnp.where(remote, 1.0, 0.0).astype(F32)
    a_ref[...] = (f_ref[...] + got_ref[...]) * source_scale()
    translate([(tx, ty, weight)], h_ref, a_ref, l_ref)
    local = l_ref[...] + near_ref[...]
    wx = own_rows(part_ref, 0)
    wy = own_rows(part_ref, 1)
    ox, oy = leaf_offsets()
    x = wx + ox
    y = wy + oy
    rows = lambda at: acc_ref[:, at, :] + acc_ref[:, at + 1, :] + acc_ref[:, at + 2, :]
    total = rows(0)
    sum_re = x * total - rows(3)
    sum_im = rows(6) - y * total
    p_re = jnp.ones_like(wx)
    p_im = jnp.zeros_like(wx)
    for m in range(ORDER):
        if m:
            p_re, p_im = p_re * wx - p_im * wy, p_re * wy + p_im * wx
        l_re = local[:, m : m + 1]
        l_im = local[:, 64 + m : 65 + m]
        sum_re = sum_re + (l_re * p_re - l_im * p_im)
        sum_im = sum_im + (l_re * p_im + l_im * p_re)
    sum_re = sum_re * (1.0 / TWO_PI)
    sum_im = sum_im * (1.0 / TWO_PI)
    for i in range(SIDE):
        out_ref[0, i] = sum_im[4 * i : 4 * i + 4]
        out_ref[1, i] = sum_re[4 * i : 4 * i + 4]


V = pl.BlockSpec(memory_space=pltpu.VMEM)
S = pl.BlockSpec(memory_space=pltpu.SMEM)
A = pl.BlockSpec(memory_space=pl.ANY)


def shaped(*shape, dtype=F32):
    return jax.ShapeDtypeStruct(shape, dtype)


def call(kernel, name, in_specs, outs, scratch, cost, aliases=None):
    return pl.pallas_call(
        kernel,
        out_shape=outs,
        in_specs=in_specs,
        out_specs=jax.tree.map(lambda unused: V, outs),
        scratch_shapes=scratch,
        name=name,
        input_output_aliases=aliases or {},
        cost_estimate=pl.CostEstimate(flops=cost, bytes_accessed=1 << 20, transcendentals=0),
        compiler_params=pltpu.CompilerParams(vmem_limit_bytes=VMEM_LIMIT),
    )


def features_out(count):
    return [shaped(count, SIZE, FEATURES, dtype=BF16), shaped(count, 16, SIZE, dtype=BF16)]


def stages(with_target):
    out = [pltpu.VMEM((LEAVES, FEATURES, SIZE), F32), pltpu.VMEM((LEAVES, 16, SIZE), F32)]
    return ([pltpu.VMEM((LEAVES, FEATURES, SIZE), F32)] if with_target else []) + out


SMALL = 4_000_000
PAIR = 400_000_000


def run_direct(name, tables, mask, feats, acc, mode="", extra=None, ins=(), outs=(), scratch=()):
    zero = acc is None
    args = [mask, *feats] + ([] if zero else [acc]) + list(ins)
    got = call(
        functools.partial(direct, tables, mode, zero, extra, len(ins)),
        name,
        [V] * len(args),
        [shaped(LEAVES, 16, SIZE), *outs],
        list(scratch),
        PAIR * tables.shape[1],
        {} if zero else {4: 0},
    )(*args)
    return got if outs else got[0]


def far_scratch(width):
    return [pltpu.VMEM((4 * ORDER - 2, LEAVES, width), F32), pltpu.VMEM((24, width), F32)]


def body(particles, near_mask):
    turned = near_mask.transpose(1, 2, 0)
    t0, s0, w0, m0, f0, send_a, send_b = call(
        prepare_own,
        "prepare_own",
        [V],
        [shaped(LEAVES, FEATURES, SIZE, dtype=BF16), *features_out(LEAVES), shaped(24, 128), shaped(24, 128)]
        + [shaped(SLAB_ROWS, SIZE)] * 2,
        stages(True),
        SMALL,
    )(particles)
    own = pair_table("own")
    flex = own[:112].reshape(4, 28, 3)
    feats = (t0, s0, w0)
    acc, mask = run_direct(
        "direct_early", flex, turned, feats, None, "early", outs=[shaped(17, LEAVES, 1, SIZE)]
    )
    send_a, send_b, acc = lax.optimization_barrier((send_a, send_b, acc))
    recv_a = swap(send_a, "core")
    recv_b = swap(send_b, "slab")
    acc = run_direct("direct_own_0", own[None, 112:140], mask, feats, acc)
    m1, f1, send_near, send_far = call(
        pack_slab,
        "pack_slab",
        [V, V, V, V, V, A],
        [shaped(24, 128), shaped(24, 128), shaped(LEAF_ROWS, SIZE), shaped(72, SIZE)],
        [],
        SMALL,
    )(particles, recv_a, recv_b, m0, f0, acc)
    send_near, acc = lax.optimization_barrier((send_near, acc))
    recv_near = swap(send_near, "leaf_near")
    built = dict(outs=features_out(LEAVES), scratch=stages(False))
    acc, s1, w1 = run_direct(
        "direct_own_1", own[None, 140:168], mask, feats, acc, extra=slab_halo, ins=(recv_a, recv_b), **built
    )
    f2, send_far = call(
        pack_near, "pack_near", [V, V, V, A], [shaped(24, 128), shaped(LEAF_ROWS, SIZE)], [], SMALL
    )(recv_near, f1, send_far, acc)
    send_far, acc = lax.optimization_barrier((send_far, acc))
    recv_far = swap(send_far, "leaf_far")
    acc, s2, w2 = run_direct(
        "direct_own_2", own[None, 168:], mask, feats, acc, extra=near_halo, ins=(recv_near,), **built
    )
    recv_far, acc = lax.optimization_barrier((recv_far, acc))
    blocks = f2 + recv_far[72:96, 0:128]
    slab_pairs = pair_table("slab").reshape(3, 1, 28, 3)
    for number, axis in enumerate(("z_near", "z_far", "x_near")):
        blocks, acc = lax.optimization_barrier((blocks, acc))
        got = swap(blocks, axis)
        name = f"direct_slab_{number}"
        slab_feats = (t0, s1, w1)
        if number == 0:
            acc, s3, w3 = run_direct(
                name, slab_pairs[number], mask, slab_feats, acc, extra=far_halo, ins=(recv_far,), **built
            )
        else:
            acc = run_direct(name, slab_pairs[number], mask, slab_feats, acc)
        got, acc = lax.optimization_barrier((got, acc))
        blocks = blocks + got
    blocks, acc = lax.optimization_barrier((blocks, acc))
    got = swap(blocks, "x_far")
    right = pair_table("leaf", True)
    left = pair_table("leaf", False)
    acc, local = run_direct(
        "direct_leaf_near",
        np.stack([right, left]),
        mask,
        (t0, s2, w2),
        acc,
        "side",
        extra=leaf_field,
        ins=(turned, m1, recv_near, recv_far),
        outs=[shaped(LEAVES, 128)],
        scratch=far_scratch(256),
    )
    acc = run_direct("direct_leaf_far", np.stack([left, right]), mask, (t0, s3, w3), acc, "side")
    acc = run_direct("direct_late", flex, mask, feats, acc, "late")
    got, acc = lax.optimization_barrier((got, acc))
    return call(
        finish,
        "finish",
        [V] * 5,
        shaped(2, SIDE, SIDE, SIZE),
        far_scratch(128) + [pltpu.VMEM((LEAVES, 128), F32)],
        SMALL,
    )(particles, acc, local, blocks, got)


def solution(mesh):
    finer = Mesh(mesh.devices.reshape(4, 4, 2, mesh.shape["leaf"]), ALL)
    in_specs = (P(None, SLAB, "leaf", None), P(None, SLAB, "leaf"))
    out_specs = P(None, SLAB, "leaf", None)
    run = jax.shard_map(body, mesh=finer, in_specs=in_specs, out_specs=out_specs, check_vma=False)

    def whole(particles, near_mask):
        with jax.sharding.use_abstract_mesh(mesh.abstract_mesh):
            return run(particles, near_mask)

    return run
```

```python
import functools
import math

import jax
import jax.numpy as jnp
import numpy as np
from jax import lax
from jax.experimental import pallas as pl
from jax.experimental.pallas import tpu as pltpu
from jax.sharding import Mesh
from jax.sharding import PartitionSpec as P

ORDER = 10
SIDE = 4
LEAVES = 16
SIZE = 256
FEATURES = 32
FLEX = 3
DELTA_SQUARED = 0.0025
TWO_PI = 2.0 * math.pi
SLAB = ("slab_0", "slab_1", "slab_2")
ALL = ("slab_0", "slab_1", "slab_2", "leaf")
F32 = jnp.float32
BF16 = jnp.bfloat16
VMEM_LIMIT = 6 << 20
cycle_steps = [(a, b) for a in range(-2, 3) for b in range(-2, 3) if max(abs(a), abs(b)) == 2]
near_steps = [(a, b) for a in range(-2, 3) for b in range(-2, 3)]


def exchange_pairs(partner):
    pairs = []
    for x in range(4):
        for z in range(4):
            for c in range(2):
                for y in range(4):
                    other = partner(x, z, c, y)
                    if other is not None:
                        a, b, d, e = other
                        pairs.append((((x * 4 + z) * 2 + c) * 4 + y, ((a * 4 + b) * 2 + d) * 4 + e))
    return pairs


def slab_between_chips(x, z, c, y):
    slab = (x * 4 + z) * 2 + c
    other = slab + 1 if c == 1 else slab - 1
    if not 0 <= other < 32:
        return None
    return (other // 8, (other // 2) % 4, other % 2, y)


def near_side(k):
    return k ^ 1


def far_side(k):
    return 3 - k


SWAPS = {
    "core": exchange_pairs(lambda x, z, c, y: (x, z, 1 - c, y)),
    "slab": exchange_pairs(slab_between_chips),
    "leaf_near": exchange_pairs(lambda x, z, c, y: (x, z, c, near_side(y))),
    "leaf_far": exchange_pairs(lambda x, z, c, y: (x, z, c, far_side(y))),
    "z_near": exchange_pairs(lambda x, z, c, y: (x, near_side(z), c, y)),
    "z_far": exchange_pairs(lambda x, z, c, y: (x, far_side(z), c, y)),
    "x_near": exchange_pairs(lambda x, z, c, y: (near_side(x), z, c, y)),
    "x_far": exchange_pairs(lambda x, z, c, y: (far_side(x), z, c, y)),
}


def swap(value, name):
    return lax.ppermute(value, ALL, SWAPS[name])


def pieces(value, count):
    parts = []
    for unused in range(count):
        part = value.astype(BF16).astype(F32)
        parts.append(part)
        value = value - part
    return parts


def build_features(wx, wy, g, ox, oy, stage_t, stage_s, stage_w, t_ref, s_ref, w_ref, first, with_target):
    count = wx.shape[0]
    one = jnp.ones_like(wx)
    zero = jnp.zeros_like(wx)
    coarse_x = jnp.round(wx * 32.0) * (1.0 / 32.0)
    coarse_y = jnp.round(wy * 32.0) * (1.0 / 32.0)
    fine_x = wx - coarse_x
    fine_y = wy - coarse_y
    big_x = coarse_x + ox
    big_y = coarse_y + oy
    big = pieces(big_x * big_x + big_y * big_y, 2)
    rest = 2.0 * (big_x * fine_x + big_y * fine_y) + fine_x * fine_x + fine_y * fine_y
    px = pieces(fine_x, 2)
    py = pieces(fine_y, 2)
    if with_target:
        rows = [big_x, big_y, big[0], big[1], one, one, zero, zero]
        rows += [big_x, big_x, big_y, big_y, px[0], px[1], py[0], py[1]]
        rows += [px[0], px[0], px[1], py[0], py[0], py[1]]
        rows += pieces(rest + DELTA_SQUARED, 3) + [one, one, one]
        rows += [zero] * (FEATURES - len(rows))
        for f, row in enumerate(rows):
            stage_t[:count, f, :] = row
    twice = lambda v: -2.0 * v
    rows = [twice(big_x), twice(big_y), one, one, big[0], big[1], zero, zero]
    rows += [twice(px[0]), twice(px[1]), twice(py[0]), twice(py[1])]
    rows += [twice(big_x), twice(big_x), twice(big_y), twice(big_y)]
    rows += [twice(px[0]), twice(px[1]), twice(px[0]), twice(py[0]), twice(py[1]), twice(py[0])]
    rows += [one, one, one] + pieces(rest, 3)
    rows += [zero] * (FEATURES - len(rows))
    for f, row in enumerate(rows):
        stage_s[:count, f, :] = row
    rows = pieces(g, 3) + pieces(g * (wx + ox), 3) + pieces(g * (wy + oy), 3)
    rows += [zero] * (16 - len(rows))
    for f, row in enumerate(rows):
        stage_w[:count, f, :] = row
    for n in range(count):
        if with_target:
            t_ref[first + n] = stage_t[n].astype(BF16)
        s_ref[first + n] = jnp.transpose(stage_s[n]).astype(BF16)
        w_ref[first + n] = stage_w[n].astype(BF16)


def power_list(base_re, base_im, count):
    re = [jnp.ones_like(base_re)]
    im = [jnp.zeros_like(base_im)]
    for unused in range(1, count):
        a, b = re[-1], im[-1]
        re.append(a * base_re - b * base_im)
        im.append(a * base_im + b * base_re)
    return re, im


def row_of(n):
    return lax.broadcasted_iota(jnp.int32, (n, 1), 0)


def leaf_offsets():
    n = row_of(LEAVES)
    ox = (n >> 2).astype(F32) - 1.5
    oy = (n & 3).astype(F32) - 1.5
    return ox, oy


def own_rows(ref, part):
    return jnp.concatenate([ref[part, i] for i in range(SIDE)], axis=0)


def position():
    slab = lax.axis_index(SLAB)
    leaf = lax.axis_index("leaf")
    between = jnp.logical_and(leaf > 0, leaf < 3).astype(jnp.int32)
    return slab, leaf, slab & 1, leaf & 1, between


SLAB_ROWS = 72
LEAF_ROWS = 96


def prepare_own(part_ref, t_ref, s_ref, w_ref, m_ref, f_ref, a_ref, b_ref, stage_t, stage_s, stage_w):
    info = position()
    wx = own_rows(part_ref, 0)
    wy = own_rows(part_ref, 1)
    g = own_rows(part_ref, 2)
    ox, oy = leaf_offsets()
    lane = lax.broadcasted_iota(jnp.int32, (LEAVES, 128), 1)
    table = jnp.zeros((LEAVES, 128), F32)
    for start, base_re, base_im in ((0, wx, wy), (32, wx + ox, wy + oy)):
        re, im = power_list(base_re, base_im, ORDER)
        for k in range(ORDER):
            table = jnp.where(lane == start + k, jnp.sum(g * re[k], 1, keepdims=True), table)
            if k:
                table = jnp.where(lane == start + ORDER + k, jnp.sum(g * im[k], 1, keepdims=True), table)
    turned = jnp.transpose(table)
    leaf_part = jnp.concatenate([turned[0:24], jnp.zeros((24, 112), F32)], axis=1)
    block_part = jnp.sum(turned[32:56], axis=1, keepdims=True)
    me = info[0] * 4 + info[1]
    wide = lax.broadcasted_iota(jnp.int32, (24, 128), 1)
    block_row = jnp.where(wide == me, block_part, 0.0)
    m_ref[...] = leaf_part
    f_ref[...] = block_row
    even = info[2] == 0
    for c in range(3):
        first = jnp.concatenate([part_ref[c, 0], part_ref[c, 1]], axis=0)
        last = jnp.concatenate([part_ref[c, 2], part_ref[c, 3]], axis=0)
        a_ref[8 * c : 8 * c + 8] = jnp.where(even, last, first)
        b_ref[8 * c : 8 * c + 8] = jnp.where(even, first, last)
    none = jnp.zeros((24, 128), F32)
    for ref in (a_ref, b_ref):
        ref[24:48, 0:128] = leaf_part
        ref[24:48, 128:256] = none
        ref[48:72, 0:128] = block_row
        ref[48:72, 128:256] = none
    build_features(wx, wy, g, ox, oy, stage_t, stage_s, stage_w, t_ref, s_ref, w_ref, 0, True)


def pack_slab(part_ref, ra_ref, rb_ref, m_ref, f_ref, after_ref, m_out, f_out, near_ref, far_ref):
    info = position()
    even = info[2] == 0
    leaf_even = info[3] == 0
    for c in range(3):
        ra = ra_ref[8 * c : 8 * c + 8]
        rb = rb_ref[8 * c : 8 * c + 8]
        before = jnp.where(even, rb, ra)
        after = jnp.where(even, ra, rb)
        rows = [before[0:4], before[4:8]] + [part_ref[c, i] for i in range(SIDE)] + [after[0:4], after[4:8]]
        left = jnp.concatenate([r[0:2] for r in rows], axis=0)
        right = jnp.concatenate([r[2:4] for r in rows], axis=0)
        near_ref[16 * c : 16 * c + 16] = jnp.where(leaf_even, right, left)
        far_ref[16 * c : 16 * c + 16] = jnp.where(leaf_even, left, right)
    ma = ra_ref[24:48, 0:16]
    mb = rb_ref[24:48, 0:16]
    window = jnp.concatenate(
        [m_ref[:, 0:16], jnp.where(even, mb, ma), jnp.where(even, ma, mb), jnp.zeros((24, 80), F32)], axis=1
    )
    blocks = f_ref[...] + ra_ref[48:72, 0:128]
    m_out[...] = window
    f_out[...] = blocks
    none = jnp.zeros((24, 128), F32)
    near_ref[48:72, 0:128] = jnp.concatenate([none[:, 0:48], window[:, 0:48], none[:, 0:32]], axis=1)
    near_ref[48:72, 128:256] = none
    far_ref[48:72, 0:128] = window
    far_ref[48:72, 128:256] = none
    near_ref[72:96, 0:128] = blocks
    near_ref[72:96, 128:256] = none


def slab_halo(ra_ref, rb_ref, s_ref, w_ref, stage_s, stage_w):
    even = position()[2] == 0
    halo = []
    for c in range(3):
        ra = ra_ref[8 * c : 8 * c + 8]
        rb = rb_ref[8 * c : 8 * c + 8]
        halo.append(jnp.concatenate([jnp.where(even, rb, ra), jnp.where(even, ra, rb)], axis=0))
    n = row_of(LEAVES)
    i = (n >> 2) - 2
    ox = jnp.where(i >= 0, i + 4, i).astype(F32) - 1.5
    oy = (n & 3).astype(F32) - 1.5
    build_features(halo[0], halo[1], halo[2], ox, oy, None, stage_s, stage_w, None, s_ref, w_ref, 0, False)


def leaf_halo(which, r_ref, s_ref, w_ref, stage_s, stage_w):
    info = position()
    leaf_even = info[3] == 0
    to_right = leaf_even if which == 0 else jnp.logical_not(leaf_even)
    valid = jnp.float32(1.0) if which == 0 else info[4].astype(F32)
    n = row_of(LEAVES)
    ox = (n >> 1).astype(F32) - 3.5
    side = (n & 1).astype(F32)
    oy = jnp.where(to_right, side + 4.0, side - 2.0) - 1.5
    build_features(
        r_ref[0:16], r_ref[16:32], r_ref[32:48] * valid, ox, oy, None, stage_s, stage_w, None, s_ref, w_ref, 0, False
    )


def near_halo(r_ref, s_ref, w_ref, stage_s, stage_w):
    leaf_halo(0, r_ref, s_ref, w_ref, stage_s, stage_w)


def far_halo(r_ref, s_ref, w_ref, stage_s, stage_w):
    leaf_halo(1, r_ref, s_ref, w_ref, stage_s, stage_w)


def pack_near(r_ref, f_ref, send_ref, after_ref, f_out, send_out):
    blocks = f_ref[...] + r_ref[72:96, 0:128]
    f_out[...] = blocks
    send_out[0:72] = send_ref[...]
    send_out[72:96, 0:128] = blocks
    send_out[72:96, 128:256] = jnp.zeros((24, 128), F32)


def chosen(index, values):
    if all(v == values[0] for v in values):
        return values[0]
    out = values[-1]
    for n in range(len(values) - 2, -1, -1):
        out = jnp.where(index == n, values[n], out)
    return out


RELEASE = ((0, 10, 20, 25), (0, 14, 27, 35), (0, 11, 22, 24))
LAST_RELEASE = 80
BODY_TIME = 22


def early_bodies():
    slab, leaf, core, unused, unused = position()
    places = (slab >> 3, (slab >> 1) & 3, leaf)
    ahead = LAST_RELEASE + 6 * core - sum(chosen(place, term) for place, term in zip(places, RELEASE))
    return sum((ahead >= BODY_TIME * (n + 1)).astype(jnp.int32) for n in range(FLEX))


def direct(tables, mode, zero, extra, extra_in, mask_ref, t_ref, s_ref, w_ref, *refs):
    if zero:
        acc_ref, rows_ref = refs
        acc_ref[...] = jnp.zeros_like(acc_ref)
        near_mask = jnp.concatenate([mask_ref[i] for i in range(SIDE)], axis=0).astype(F32)
        for o in range(16):
            rows_ref[o, :, 0, :] = jnp.broadcast_to(near_mask[:, o : o + 1], (LEAVES, SIZE))
        rows_ref[16, :, 0, :] = jnp.ones((LEAVES, SIZE), F32)
        mask_ref = rows_ref
    else:
        acc_ref = refs[extra_in + 1]
        acc_ref[...] = refs[0][...]
        others = refs[1 : extra_in + 1] + refs[extra_in + 2 :]
    count = tables.shape[1]

    def step(index, unused):
        for n in range(count):
            t, s, o = (chosen(index, [int(v) for v in tables[:, n, c]]) for c in range(3))
            distance = jnp.dot(s_ref[s], t_ref[t], preferred_element_type=F32)
            kernel = 1.0 / distance
            high = kernel.astype(BF16)
            low = (kernel - high.astype(F32)).astype(BF16)
            w = w_ref[s]
            total = jnp.dot(w, high, preferred_element_type=F32) + jnp.dot(w, low, preferred_element_type=F32)
            if isinstance(o, int) and o == 16:
                acc_ref[t] = acc_ref[t] + total
            else:
                acc_ref[t] = acc_ref[t] + mask_ref[o, t] * total
        return 0

    if mode == "side":
        step(position()[3], 0)
    elif mode == "early":
        lax.fori_loop(0, early_bodies(), step, 0)
    elif mode == "late":
        lax.fori_loop(early_bodies(), tables.shape[0], step, 0)
    else:
        step(0, 0)
    if extra is not None:
        extra(*others)


def pair_table(kind, to_right=False):
    out = []
    for t in range(LEAVES):
        i, j = divmod(t, SIDE)
        for a, b in near_steps:
            o = cycle_steps.index((a, b)) if max(abs(a), abs(b)) == 2 else 16
            si, sj = i + a, j + b
            in_row, in_column = 0 <= si < SIDE, 0 <= sj < SIDE
            if kind == "own" and in_row and in_column:
                out.append((t, si * SIDE + sj, o))
            if kind == "slab" and not in_row and in_column:
                out.append((t, ((si + 2) if si < 0 else (si - 2)) * SIDE + sj, o))
            if kind == "leaf" and not in_column and (sj >= SIDE) == to_right:
                out.append((t, (si + 2) * 2 + (sj - SIDE if to_right else sj + 2), o))
    return np.array(out, np.int32)


def translate(groups, h_ref, a_ref, out_ref):
    for group, (tx, ty, weight) in enumerate(groups):
        span = slice(128 * group, 128 * group + 128)
        square = tx * tx + ty * ty
        inv_x = tx / square
        inv_y = -ty / square
        re = weight * inv_x
        im = weight * inv_y
        h_ref[0, :, span] = re
        h_ref[1, :, span] = im
        for order in range(1, 2 * ORDER - 1):
            re, im = (re * inv_x - im * inv_y) * float(order), (re * inv_y + im * inv_x) * float(order)
            h_ref[2 * order, :, span] = re
            h_ref[2 * order + 1, :, span] = im
    lane = lax.broadcasted_iota(jnp.int32, (LEAVES, 128), 1)
    table = jnp.zeros((LEAVES, 128), F32)
    half = ORDER // 2
    for first in (0, half):
        sums_re = [None] * half
        sums_im = [None] * half
        for group in range(len(groups)):
            span = slice(128 * group, 128 * group + 128)
            for k_ in range(ORDER):
                a_re = a_ref[k_ : k_ + 1, span]
                a_im = a_ref[ORDER + k_ : ORDER + k_ + 1, span]
                for m in range(half):
                    at = first + m + k_
                    h_re = h_ref[2 * at, :, span]
                    h_im = h_ref[2 * at + 1, :, span]
                    term_re = h_re * a_re - h_im * a_im
                    term_im = h_re * a_im + h_im * a_re
                    sums_re[m] = term_re if sums_re[m] is None else sums_re[m] + term_re
                    sums_im[m] = term_im if sums_im[m] is None else sums_im[m] + term_im
        for m in range(half):
            factor = 1.0 / math.factorial(first + m)
            table = jnp.where(lane == first + m, jnp.sum(sums_re[m], 1, keepdims=True) * factor, table)
            table = jnp.where(lane == 64 + first + m, jnp.sum(sums_im[m], 1, keepdims=True) * factor, table)
    out_ref[...] = table


def source_scale():
    row = row_of(24)
    which = jnp.where(row >= ORDER, row - ORDER, row)
    scale = jnp.zeros((24, 1), F32)
    for k_ in range(ORDER):
        scale = jnp.where(which == k_, (-1.0) ** (k_ + 1) / math.factorial(k_), scale)
    return scale


def leaf_field(nm_ref, m_ref, r1_ref, r2_ref, out_ref, h_ref, a_ref):
    info = position()
    leaf_even = info[3] == 0
    valid = info[4].astype(F32)
    n = row_of(LEAVES)
    ti = n >> 2
    tj = n & 3
    lane = lax.broadcasted_iota(jnp.int32, (LEAVES, 128), 1)
    near_mask = jnp.concatenate([nm_ref[i] for i in range(SIDE)], axis=0).astype(F32)
    near_shift = jnp.where(leaf_even, 4, -4)
    second = lane >= 48
    place = jnp.where(second, lane - 48, lane)
    k = place >> 4
    r = place & 15
    si = jnp.where(k == 0, r >> 2, jnp.where(k == 1, (r >> 2) - 4, (r >> 2) + 4))
    groups = []
    for column, lanes in ((jnp.where(second, near_shift, 0), 96), (-near_shift, 48)):
        dx = si - ti
        dy = (r & 3) + column - tj
        reach = jnp.maximum(jnp.abs(dx), jnp.abs(dy))
        weight = jnp.where(reach >= 3, 1.0, 0.0).astype(F32)
        for o, (a, b) in enumerate(cycle_steps):
            hit = jnp.logical_and(dx == a, dy == b)
            weight = jnp.where(hit, 1.0 - near_mask[:, o : o + 1], weight)
        inside = lane < lanes
        used = jnp.logical_and(reach >= 2, inside)
        groups.append(
            (
                jnp.where(used, dx.astype(F32), 1.0),
                jnp.where(used, dy.astype(F32), 1.0),
                jnp.where(inside, weight, 0.0),
            )
        )
    scale = source_scale()
    a_ref[:, 0:128] = (m_ref[...] + r1_ref[48:72, 0:128]) * scale
    a_ref[:, 128:256] = r2_ref[48:72, 0:128] * (valid * scale)
    translate(groups, h_ref, a_ref, out_ref)


def finish(part_ref, acc_ref, near_ref, f_ref, got_ref, out_ref, h_ref, a_ref, l_ref):
    info = position()
    n = row_of(LEAVES)
    ti = n >> 2
    tj = n & 3
    lane = lax.broadcasted_iota(jnp.int32, (LEAVES, 128), 1)
    bx = (lane >> 2) - info[0]
    by = (lane & 3) - info[1]
    remote = jnp.maximum(jnp.abs(bx), jnp.abs(by)) >= 2
    tx = jnp.where(remote, (bx * SIDE - ti).astype(F32) + 1.5, 1.0)
    ty = jnp.where(remote, (by * SIDE - tj).astype(F32) + 1.5, 1.0)
    weight = jnp.where(remote, 1.0, 0.0).astype(F32)
    a_ref[...] = (f_ref[...] + got_ref[...]) * source_scale()
    translate([(tx, ty, weight)], h_ref, a_ref, l_ref)
    local = l_ref[...] + near_ref[...]
    wx = own_rows(part_ref, 0)
    wy = own_rows(part_ref, 1)
    ox, oy = leaf_offsets()
    x = wx + ox
    y = wy + oy
    rows = lambda at: acc_ref[:, at, :] + acc_ref[:, at + 1, :] + acc_ref[:, at + 2, :]
    total = rows(0)
    sum_re = x * total - rows(3)
    sum_im = rows(6) - y * total
    p_re = jnp.ones_like(wx)
    p_im = jnp.zeros_like(wx)
    for m in range(ORDER):
        if m:
            p_re, p_im = p_re * wx - p_im * wy, p_re * wy + p_im * wx
        l_re = local[:, m : m + 1]
        l_im = local[:, 64 + m : 65 + m]
        sum_re = sum_re + (l_re * p_re - l_im * p_im)
        sum_im = sum_im + (l_re * p_im + l_im * p_re)
    sum_re = sum_re * (1.0 / TWO_PI)
    sum_im = sum_im * (1.0 / TWO_PI)
    for i in range(SIDE):
        out_ref[0, i] = sum_im[4 * i : 4 * i + 4]
        out_ref[1, i] = sum_re[4 * i : 4 * i + 4]


V = pl.BlockSpec(memory_space=pltpu.VMEM)
S = pl.BlockSpec(memory_space=pltpu.SMEM)
A = pl.BlockSpec(memory_space=pl.ANY)


def shaped(*shape, dtype=F32):
    return jax.ShapeDtypeStruct(shape, dtype)


def call(kernel, name, in_specs, outs, scratch, cost, aliases=None):
    return pl.pallas_call(
        kernel,
        out_shape=outs,
        in_specs=in_specs,
        out_specs=jax.tree.map(lambda unused: V, outs),
        scratch_shapes=scratch,
        name=name,
        input_output_aliases=aliases or {},
        cost_estimate=pl.CostEstimate(flops=cost, bytes_accessed=1 << 20, transcendentals=0),
        compiler_params=pltpu.CompilerParams(vmem_limit_bytes=VMEM_LIMIT),
    )


def features_out(count):
    return [shaped(count, SIZE, FEATURES, dtype=BF16), shaped(count, 16, SIZE, dtype=BF16)]


def stages(with_target):
    out = [pltpu.VMEM((LEAVES, FEATURES, SIZE), F32), pltpu.VMEM((LEAVES, 16, SIZE), F32)]
    return ([pltpu.VMEM((LEAVES, FEATURES, SIZE), F32)] if with_target else []) + out


SMALL = 4_000_000
PAIR = 400_000_000


def run_direct(name, tables, mask, feats, acc, mode="", extra=None, ins=(), outs=(), scratch=()):
    zero = acc is None
    args = [mask, *feats] + ([] if zero else [acc]) + list(ins)
    got = call(
        functools.partial(direct, tables, mode, zero, extra, len(ins)),
        name,
        [V] * len(args),
        [shaped(LEAVES, 16, SIZE), *outs],
        list(scratch),
        PAIR * tables.shape[1],
        {} if zero else {4: 0},
    )(*args)
    return got if outs else got[0]


def far_scratch(width):
    return [pltpu.VMEM((4 * ORDER - 2, LEAVES, width), F32), pltpu.VMEM((24, width), F32)]


def body(particles, near_mask):
    turned = near_mask.transpose(1, 2, 0)
    t0, s0, w0, m0, f0, send_a, send_b = call(
        prepare_own,
        "prepare_own",
        [V],
        [shaped(LEAVES, FEATURES, SIZE, dtype=BF16), *features_out(LEAVES), shaped(24, 128), shaped(24, 128)]
        + [shaped(SLAB_ROWS, SIZE)] * 2,
        stages(True),
        SMALL,
    )(particles)
    own = pair_table("own")
    flex = own[: 28 * FLEX].reshape(FLEX, 28, 3)
    feats = (t0, s0, w0)
    acc, mask = run_direct(
        "direct_early", flex, turned, feats, None, "early", outs=[shaped(17, LEAVES, 1, SIZE)]
    )
    send_a, send_b, acc = lax.optimization_barrier((send_a, send_b, acc))
    recv_a = swap(send_a, "core")
    recv_b = swap(send_b, "slab")
    acc = run_direct("direct_own_0", own[None, 84:112], mask, feats, acc)
    m1, f1, send_near, send_far = call(
        pack_slab,
        "pack_slab",
        [V, V, V, V, V, A],
        [shaped(24, 128), shaped(24, 128), shaped(LEAF_ROWS, SIZE), shaped(72, SIZE)],
        [],
        SMALL,
    )(particles, recv_a, recv_b, m0, f0, acc)
    send_near, acc = lax.optimization_barrier((send_near, acc))
    recv_near = swap(send_near, "leaf_near")
    built = dict(outs=features_out(LEAVES), scratch=stages(False))
    acc, s1, w1 = run_direct(
        "direct_own_1", own[None, 112:154], mask, feats, acc, extra=slab_halo, ins=(recv_a, recv_b), **built
    )
    f2, send_far = call(
        pack_near, "pack_near", [V, V, V, A], [shaped(24, 128), shaped(LEAF_ROWS, SIZE)], [], SMALL
    )(recv_near, f1, send_far, acc)
    send_far, acc = lax.optimization_barrier((send_far, acc))
    recv_far = swap(send_far, "leaf_far")
    acc, s2, w2 = run_direct(
        "direct_own_2", own[None, 154:], mask, feats, acc, extra=near_halo, ins=(recv_near,), **built
    )
    recv_far, acc = lax.optimization_barrier((recv_far, acc))
    blocks = f2 + recv_far[72:96, 0:128]
    slab_pairs = pair_table("slab").reshape(3, 1, 28, 3)
    for number, axis in enumerate(("z_near", "z_far", "x_near")):
        blocks, acc = lax.optimization_barrier((blocks, acc))
        got = swap(blocks, axis)
        name = f"direct_slab_{number}"
        slab_feats = (t0, s1, w1)
        if number == 0:
            acc, s3, w3 = run_direct(
                name, slab_pairs[number], mask, slab_feats, acc, extra=far_halo, ins=(recv_far,), **built
            )
        else:
            acc = run_direct(name, slab_pairs[number], mask, slab_feats, acc)
        got, acc = lax.optimization_barrier((got, acc))
        blocks = blocks + got
    blocks, acc = lax.optimization_barrier((blocks, acc))
    got = swap(blocks, "x_far")
    right = pair_table("leaf", True)
    left = pair_table("leaf", False)
    acc, local = run_direct(
        "direct_leaf_near",
        np.stack([right, left]),
        mask,
        (t0, s2, w2),
        acc,
        "side",
        extra=leaf_field,
        ins=(turned, m1, recv_near, recv_far),
        outs=[shaped(LEAVES, 128)],
        scratch=far_scratch(256),
    )
    acc = run_direct("direct_leaf_far", np.stack([left, right]), mask, (t0, s3, w3), acc, "side")
    acc = run_direct("direct_late", flex, mask, feats, acc, "late")
    got, acc = lax.optimization_barrier((got, acc))
    return call(
        finish,
        "finish",
        [V] * 5,
        shaped(2, SIDE, SIDE, SIZE),
        far_scratch(128) + [pltpu.VMEM((LEAVES, 128), F32)],
        SMALL,
    )(particles, acc, local, blocks, got)


def solution(mesh):
    finer = Mesh(mesh.devices.reshape(4, 4, 2, mesh.shape["leaf"]), ALL)
    in_specs = (P(None, SLAB, "leaf", None), P(None, SLAB, "leaf"))
    out_specs = P(None, SLAB, "leaf", None)
    run = jax.shard_map(body, mesh=finer, in_specs=in_specs, out_specs=out_specs, check_vma=False)

    def whole(particles, near_mask):
        with jax.sharding.use_abstract_mesh(mesh.abstract_mesh):
            return run(particles, near_mask)

    return run
```

```python
import functools
import math

import jax
import jax.numpy as jnp
import numpy as np
from jax import lax
from jax.experimental import pallas as pl
from jax.experimental.pallas import tpu as pltpu
from jax.sharding import Mesh
from jax.sharding import PartitionSpec as P

ORDER = 10
SIDE = 4
LEAVES = 16
SIZE = 256
FEATURES = 32
FLEX = 2
DELTA_SQUARED = 0.0025
TWO_PI = 2.0 * math.pi
SLAB = ("slab_0", "slab_1", "slab_2")
ALL = ("slab_0", "slab_1", "slab_2", "leaf")
F32 = jnp.float32
BF16 = jnp.bfloat16
VMEM_LIMIT = 6 << 20
cycle_steps = [(a, b) for a in range(-2, 3) for b in range(-2, 3) if max(abs(a), abs(b)) == 2]
near_steps = [(a, b) for a in range(-2, 3) for b in range(-2, 3)]


def exchange_pairs(partner):
    pairs = []
    for x in range(4):
        for z in range(4):
            for c in range(2):
                for y in range(4):
                    other = partner(x, z, c, y)
                    if other is not None:
                        a, b, d, e = other
                        pairs.append((((x * 4 + z) * 2 + c) * 4 + y, ((a * 4 + b) * 2 + d) * 4 + e))
    return pairs


def slab_between_chips(x, z, c, y):
    slab = (x * 4 + z) * 2 + c
    other = slab + 1 if c == 1 else slab - 1
    if not 0 <= other < 32:
        return None
    return (other // 8, (other // 2) % 4, other % 2, y)


def near_side(k):
    return k ^ 1


def far_side(k):
    return 3 - k


SWAPS = {
    "core": exchange_pairs(lambda x, z, c, y: (x, z, 1 - c, y)),
    "slab": exchange_pairs(slab_between_chips),
    "leaf_near": exchange_pairs(lambda x, z, c, y: (x, z, c, near_side(y))),
    "leaf_far": exchange_pairs(lambda x, z, c, y: (x, z, c, far_side(y))),
    "z_near": exchange_pairs(lambda x, z, c, y: (x, near_side(z), c, y) if c == 1 else None),
    "z_far": exchange_pairs(lambda x, z, c, y: (x, far_side(z), c, y) if c == 1 else None),
    "x_near": exchange_pairs(lambda x, z, c, y: (near_side(x), z, c, y) if c == 1 else None),
    "x_far": exchange_pairs(lambda x, z, c, y: (far_side(x), z, c, y) if c == 1 else None),
}


def swap(value, name):
    return lax.ppermute(value, ALL, SWAPS[name])


def pieces(value, count):
    parts = []
    for unused in range(count):
        part = value.astype(BF16).astype(F32)
        parts.append(part)
        value = value - part
    return parts


def build_features(wx, wy, g, ox, oy, stage_t, stage_s, stage_w, t_ref, s_ref, w_ref, first, with_target):
    count = wx.shape[0]
    one = jnp.ones_like(wx)
    zero = jnp.zeros_like(wx)
    coarse_x = jnp.round(wx * 32.0) * (1.0 / 32.0)
    coarse_y = jnp.round(wy * 32.0) * (1.0 / 32.0)
    fine_x = wx - coarse_x
    fine_y = wy - coarse_y
    big_x = coarse_x + ox
    big_y = coarse_y + oy
    big = pieces(big_x * big_x + big_y * big_y, 2)
    rest = 2.0 * (big_x * fine_x + big_y * fine_y) + fine_x * fine_x + fine_y * fine_y
    px = pieces(fine_x, 2)
    py = pieces(fine_y, 2)
    if with_target:
        rows = [big_x, big_y, big[0], big[1], one, one, zero, zero]
        rows += [big_x, big_x, big_y, big_y, px[0], px[1], py[0], py[1]]
        rows += [px[0], px[0], px[1], py[0], py[0], py[1]]
        rows += pieces(rest + DELTA_SQUARED, 3) + [one, one, one]
        rows += [zero] * (FEATURES - len(rows))
        for f, row in enumerate(rows):
            stage_t[:count, f, :] = row
    twice = lambda v: -2.0 * v
    rows = [twice(big_x), twice(big_y), one, one, big[0], big[1], zero, zero]
    rows += [twice(px[0]), twice(px[1]), twice(py[0]), twice(py[1])]
    rows += [twice(big_x), twice(big_x), twice(big_y), twice(big_y)]
    rows += [twice(px[0]), twice(px[1]), twice(px[0]), twice(py[0]), twice(py[1]), twice(py[0])]
    rows += [one, one, one] + pieces(rest, 3)
    rows += [zero] * (FEATURES - len(rows))
    for f, row in enumerate(rows):
        stage_s[:count, f, :] = row
    rows = pieces(g, 3) + pieces(g * (wx + ox), 3) + pieces(g * (wy + oy), 3)
    rows += [zero] * (16 - len(rows))
    for f, row in enumerate(rows):
        stage_w[:count, f, :] = row
    for n in range(count):
        if with_target:
            t_ref[first + n] = stage_t[n].astype(BF16)
        s_ref[first + n] = jnp.transpose(stage_s[n]).astype(BF16)
        w_ref[first + n] = stage_w[n].astype(BF16)


def power_list(base_re, base_im, count):
    re = [jnp.ones_like(base_re)]
    im = [jnp.zeros_like(base_im)]
    for unused in range(1, count):
        a, b = re[-1], im[-1]
        re.append(a * base_re - b * base_im)
        im.append(a * base_im + b * base_re)
    return re, im


def row_of(n):
    return lax.broadcasted_iota(jnp.int32, (n, 1), 0)


def leaf_offsets():
    n = row_of(LEAVES)
    ox = (n >> 2).astype(F32) - 1.5
    oy = (n & 3).astype(F32) - 1.5
    return ox, oy


def own_rows(ref, part):
    return jnp.concatenate([ref[part, i] for i in range(SIDE)], axis=0)


def position():
    slab = lax.axis_index(SLAB)
    leaf = lax.axis_index("leaf")
    between = jnp.logical_and(leaf > 0, leaf < 3).astype(jnp.int32)
    return slab, leaf, slab & 1, leaf & 1, between


SLAB_ROWS = 72
LEAF_ROWS = 96


def prepare_own(part_ref, t_ref, s_ref, w_ref, m_ref, f_ref, a_ref, b_ref, stage_t, stage_s, stage_w):
    info = position()
    wx = own_rows(part_ref, 0)
    wy = own_rows(part_ref, 1)
    g = own_rows(part_ref, 2)
    ox, oy = leaf_offsets()
    lane = lax.broadcasted_iota(jnp.int32, (LEAVES, 128), 1)
    table = jnp.zeros((LEAVES, 128), F32)
    for start, base_re, base_im in ((0, wx, wy), (32, wx + ox, wy + oy)):
        re, im = power_list(base_re, base_im, ORDER)
        for k in range(ORDER):
            table = jnp.where(lane == start + k, jnp.sum(g * re[k], 1, keepdims=True), table)
            if k:
                table = jnp.where(lane == start + ORDER + k, jnp.sum(g * im[k], 1, keepdims=True), table)
    turned = jnp.transpose(table)
    leaf_part = jnp.concatenate([turned[0:24], jnp.zeros((24, 112), F32)], axis=1)
    block_part = jnp.sum(turned[32:56], axis=1, keepdims=True)
    me = info[0] * 4 + info[1]
    wide = lax.broadcasted_iota(jnp.int32, (24, 128), 1)
    block_row = jnp.where(wide == me, block_part, 0.0)
    m_ref[...] = leaf_part
    f_ref[...] = block_row
    even = info[2] == 0
    for c in range(3):
        first = jnp.concatenate([part_ref[c, 0], part_ref[c, 1]], axis=0)
        last = jnp.concatenate([part_ref[c, 2], part_ref[c, 3]], axis=0)
        a_ref[8 * c : 8 * c + 8] = jnp.where(even, last, first)
        b_ref[8 * c : 8 * c + 8] = jnp.where(even, first, last)
    none = jnp.zeros((24, 128), F32)
    for ref in (a_ref, b_ref):
        ref[24:48, 0:128] = leaf_part
        ref[24:48, 128:256] = none
        ref[48:72, 0:128] = block_row
        ref[48:72, 128:256] = none
    build_features(wx, wy, g, ox, oy, stage_t, stage_s, stage_w, t_ref, s_ref, w_ref, 0, True)


def pack_slab(part_ref, ra_ref, rb_ref, m_ref, f_ref, after_ref, m_out, f_out, near_ref, far_ref):
    info = position()
    even = info[2] == 0
    leaf_even = info[3] == 0
    for c in range(3):
        ra = ra_ref[8 * c : 8 * c + 8]
        rb = rb_ref[8 * c : 8 * c + 8]
        before = jnp.where(even, rb, ra)
        after = jnp.where(even, ra, rb)
        rows = [before[0:4], before[4:8]] + [part_ref[c, i] for i in range(SIDE)] + [after[0:4], after[4:8]]
        left = jnp.concatenate([r[0:2] for r in rows], axis=0)
        right = jnp.concatenate([r[2:4] for r in rows], axis=0)
        near_ref[16 * c : 16 * c + 16] = jnp.where(leaf_even, right, left)
        far_ref[16 * c : 16 * c + 16] = jnp.where(leaf_even, left, right)
    ma = ra_ref[24:48, 0:16]
    mb = rb_ref[24:48, 0:16]
    window = jnp.concatenate(
        [m_ref[:, 0:16], jnp.where(even, mb, ma), jnp.where(even, ma, mb), jnp.zeros((24, 80), F32)], axis=1
    )
    blocks = f_ref[...] + ra_ref[48:72, 0:128]
    m_out[...] = window
    f_out[...] = blocks
    none = jnp.zeros((24, 128), F32)
    near_ref[48:72, 0:128] = jnp.concatenate([none[:, 0:48], window[:, 0:48], none[:, 0:32]], axis=1)
    near_ref[48:72, 128:256] = none
    far_ref[48:72, 0:128] = window
    far_ref[48:72, 128:256] = none
    near_ref[72:96, 0:128] = blocks
    near_ref[72:96, 128:256] = none


def slab_halo(ra_ref, rb_ref, s_ref, w_ref, stage_s, stage_w):
    even = position()[2] == 0
    halo = []
    for c in range(3):
        ra = ra_ref[8 * c : 8 * c + 8]
        rb = rb_ref[8 * c : 8 * c + 8]
        halo.append(jnp.concatenate([jnp.where(even, rb, ra), jnp.where(even, ra, rb)], axis=0))
    n = row_of(LEAVES)
    i = (n >> 2) - 2
    ox = jnp.where(i >= 0, i + 4, i).astype(F32) - 1.5
    oy = (n & 3).astype(F32) - 1.5
    build_features(halo[0], halo[1], halo[2], ox, oy, None, stage_s, stage_w, None, s_ref, w_ref, 0, False)


def leaf_halo(which, r_ref, s_ref, w_ref, stage_s, stage_w):
    info = position()
    leaf_even = info[3] == 0
    to_right = leaf_even if which == 0 else jnp.logical_not(leaf_even)
    valid = jnp.float32(1.0) if which == 0 else info[4].astype(F32)
    n = row_of(LEAVES)
    ox = (n >> 1).astype(F32) - 3.5
    side = (n & 1).astype(F32)
    oy = jnp.where(to_right, side + 4.0, side - 2.0) - 1.5
    build_features(
        r_ref[0:16], r_ref[16:32], r_ref[32:48] * valid, ox, oy, None, stage_s, stage_w, None, s_ref, w_ref, 0, False
    )


def near_halo(r_ref, s_ref, w_ref, stage_s, stage_w):
    leaf_halo(0, r_ref, s_ref, w_ref, stage_s, stage_w)


def far_halo(r_ref, s_ref, w_ref, stage_s, stage_w):
    leaf_halo(1, r_ref, s_ref, w_ref, stage_s, stage_w)


def pack_near(r_ref, f_ref, send_ref, after_ref, f_out, send_out):
    blocks = f_ref[...] + r_ref[72:96, 0:128]
    f_out[...] = blocks
    send_out[0:72] = send_ref[...]
    send_out[72:96, 0:128] = blocks
    send_out[72:96, 128:256] = jnp.zeros((24, 128), F32)


def chosen(index, values):
    if all(v == values[0] for v in values):
        return values[0]
    out = values[-1]
    for n in range(len(values) - 2, -1, -1):
        out = jnp.where(index == n, values[n], out)
    return out


RELEASE = ((0, 8, 15, 12), (0, 18, 30, 30), (0, 8, 15, 12))
FIRST_STEPS = (18, 40)
LAST_RELEASE = 60


def early_bodies():
    slab, leaf = position()[:2]
    places = (slab >> 3, (slab >> 1) & 3, leaf)
    ahead = LAST_RELEASE - sum(chosen(place, term) for place, term in zip(places, RELEASE))
    return sum((ahead >= step).astype(jnp.int32) for step in FIRST_STEPS)


def direct(tables, mode, zero, extra, extra_in, mask_ref, t_ref, s_ref, w_ref, *refs):
    if zero:
        acc_ref, rows_ref = refs
        acc_ref[...] = jnp.zeros_like(acc_ref)
        near_mask = jnp.concatenate([mask_ref[i] for i in range(SIDE)], axis=0).astype(F32)
        for o in range(16):
            rows_ref[o, :, 0, :] = jnp.broadcast_to(near_mask[:, o : o + 1], (LEAVES, SIZE))
        rows_ref[16, :, 0, :] = jnp.ones((LEAVES, SIZE), F32)
        mask_ref = rows_ref
    else:
        acc_ref = refs[extra_in + 1]
        acc_ref[...] = refs[0][...]
        others = refs[1 : extra_in + 1] + refs[extra_in + 2 :]
    count = tables.shape[1]

    def step(index, unused):
        for n in range(count):
            t, s, o = (chosen(index, [int(v) for v in tables[:, n, c]]) for c in range(3))
            distance = jnp.dot(s_ref[s], t_ref[t], preferred_element_type=F32)
            kernel = 1.0 / distance
            high = kernel.astype(BF16)
            low = (kernel - high.astype(F32)).astype(BF16)
            w = w_ref[s]
            total = jnp.dot(w, high, preferred_element_type=F32) + jnp.dot(w, low, preferred_element_type=F32)
            if isinstance(o, int) and o == 16:
                acc_ref[t] = acc_ref[t] + total
            else:
                acc_ref[t] = acc_ref[t] + mask_ref[o, t] * total
        return 0

    if mode == "side":
        step(position()[3], 0)
    elif mode == "early":
        lax.fori_loop(0, early_bodies(), step, 0)
    elif mode == "late":
        lax.fori_loop(early_bodies(), tables.shape[0], step, 0)
    else:
        step(0, 0)
    if extra is not None:
        extra(*others)


def pair_table(kind, to_right=False):
    out = []
    for t in range(LEAVES):
        i, j = divmod(t, SIDE)
        for a, b in near_steps:
            o = cycle_steps.index((a, b)) if max(abs(a), abs(b)) == 2 else 16
            si, sj = i + a, j + b
            in_row, in_column = 0 <= si < SIDE, 0 <= sj < SIDE
            if kind == "own" and in_row and in_column:
                out.append((t, si * SIDE + sj, o))
            if kind == "slab" and not in_row and in_column:
                out.append((t, ((si + 2) if si < 0 else (si - 2)) * SIDE + sj, o))
            if kind == "leaf" and not in_column and (sj >= SIDE) == to_right:
                out.append((t, (si + 2) * 2 + (sj - SIDE if to_right else sj + 2), o))
    return np.array(out, np.int32)


def translate(groups, h_ref, a_ref, out_ref):
    for group, (tx, ty, weight) in enumerate(groups):
        span = slice(128 * group, 128 * group + 128)
        square = tx * tx + ty * ty
        inv_x = tx / square
        inv_y = -ty / square
        re = weight * inv_x
        im = weight * inv_y
        h_ref[0, :, span] = re
        h_ref[1, :, span] = im
        for order in range(1, 2 * ORDER - 1):
            re, im = (re * inv_x - im * inv_y) * float(order), (re * inv_y + im * inv_x) * float(order)
            h_ref[2 * order, :, span] = re
            h_ref[2 * order + 1, :, span] = im
    lane = lax.broadcasted_iota(jnp.int32, (LEAVES, 128), 1)
    table = jnp.zeros((LEAVES, 128), F32)
    half = ORDER // 2
    for first in (0, half):
        sums_re = [None] * half
        sums_im = [None] * half
        for group in range(len(groups)):
            span = slice(128 * group, 128 * group + 128)
            for k_ in range(ORDER):
                a_re = a_ref[k_ : k_ + 1, span]
                a_im = a_ref[ORDER + k_ : ORDER + k_ + 1, span]
                for m in range(half):
                    at = first + m + k_
                    h_re = h_ref[2 * at, :, span]
                    h_im = h_ref[2 * at + 1, :, span]
                    term_re = h_re * a_re - h_im * a_im
                    term_im = h_re * a_im + h_im * a_re
                    sums_re[m] = term_re if sums_re[m] is None else sums_re[m] + term_re
                    sums_im[m] = term_im if sums_im[m] is None else sums_im[m] + term_im
        for m in range(half):
            factor = 1.0 / math.factorial(first + m)
            table = jnp.where(lane == first + m, jnp.sum(sums_re[m], 1, keepdims=True) * factor, table)
            table = jnp.where(lane == 64 + first + m, jnp.sum(sums_im[m], 1, keepdims=True) * factor, table)
    out_ref[...] = table


def source_scale():
    row = row_of(24)
    which = jnp.where(row >= ORDER, row - ORDER, row)
    scale = jnp.zeros((24, 1), F32)
    for k_ in range(ORDER):
        scale = jnp.where(which == k_, (-1.0) ** (k_ + 1) / math.factorial(k_), scale)
    return scale


def leaf_field(nm_ref, m_ref, r1_ref, r2_ref, out_ref, h_ref, a_ref):
    info = position()
    leaf_even = info[3] == 0
    valid = info[4].astype(F32)
    n = row_of(LEAVES)
    ti = n >> 2
    tj = n & 3
    lane = lax.broadcasted_iota(jnp.int32, (LEAVES, 128), 1)
    near_mask = jnp.concatenate([nm_ref[i] for i in range(SIDE)], axis=0).astype(F32)
    near_shift = jnp.where(leaf_even, 4, -4)
    second = lane >= 48
    place = jnp.where(second, lane - 48, lane)
    k = place >> 4
    r = place & 15
    si = jnp.where(k == 0, r >> 2, jnp.where(k == 1, (r >> 2) - 4, (r >> 2) + 4))
    groups = []
    for column, lanes in ((jnp.where(second, near_shift, 0), 96), (-near_shift, 48)):
        dx = si - ti
        dy = (r & 3) + column - tj
        reach = jnp.maximum(jnp.abs(dx), jnp.abs(dy))
        weight = jnp.where(reach >= 3, 1.0, 0.0).astype(F32)
        for o, (a, b) in enumerate(cycle_steps):
            hit = jnp.logical_and(dx == a, dy == b)
            weight = jnp.where(hit, 1.0 - near_mask[:, o : o + 1], weight)
        inside = lane < lanes
        used = jnp.logical_and(reach >= 2, inside)
        groups.append(
            (
                jnp.where(used, dx.astype(F32), 1.0),
                jnp.where(used, dy.astype(F32), 1.0),
                jnp.where(inside, weight, 0.0),
            )
        )
    scale = source_scale()
    a_ref[:, 0:128] = (m_ref[...] + r1_ref[48:72, 0:128]) * scale
    a_ref[:, 128:256] = r2_ref[48:72, 0:128] * (valid * scale)
    translate(groups, h_ref, a_ref, out_ref)


def finish(part_ref, acc_ref, near_ref, f_ref, got_ref, out_ref, h_ref, a_ref, l_ref):
    info = position()
    n = row_of(LEAVES)
    ti = n >> 2
    tj = n & 3
    lane = lax.broadcasted_iota(jnp.int32, (LEAVES, 128), 1)
    bx = (lane >> 2) - info[0]
    by = (lane & 3) - info[1]
    remote = jnp.maximum(jnp.abs(bx), jnp.abs(by)) >= 2
    tx = jnp.where(remote, (bx * SIDE - ti).astype(F32) + 1.5, 1.0)
    ty = jnp.where(remote, (by * SIDE - tj).astype(F32) + 1.5, 1.0)
    weight = jnp.where(remote, 1.0, 0.0).astype(F32)
    a_ref[...] = jnp.where(info[2] == 1, f_ref[...], got_ref[...]) * source_scale()
    translate([(tx, ty, weight)], h_ref, a_ref, l_ref)
    local = l_ref[...] + near_ref[...]
    wx = own_rows(part_ref, 0)
    wy = own_rows(part_ref, 1)
    ox, oy = leaf_offsets()
    x = wx + ox
    y = wy + oy
    rows = lambda at: acc_ref[:, at, :] + acc_ref[:, at + 1, :] + acc_ref[:, at + 2, :]
    total = rows(0)
    sum_re = x * total - rows(3)
    sum_im = rows(6) - y * total
    p_re = jnp.ones_like(wx)
    p_im = jnp.zeros_like(wx)
    for m in range(ORDER):
        if m:
            p_re, p_im = p_re * wx - p_im * wy, p_re * wy + p_im * wx
        l_re = local[:, m : m + 1]
        l_im = local[:, 64 + m : 65 + m]
        sum_re = sum_re + (l_re * p_re - l_im * p_im)
        sum_im = sum_im + (l_re * p_im + l_im * p_re)
    sum_re = sum_re * (1.0 / TWO_PI)
    sum_im = sum_im * (1.0 / TWO_PI)
    for i in range(SIDE):
        out_ref[0, i] = sum_im[4 * i : 4 * i + 4]
        out_ref[1, i] = sum_re[4 * i : 4 * i + 4]


V = pl.BlockSpec(memory_space=pltpu.VMEM)
S = pl.BlockSpec(memory_space=pltpu.SMEM)
A = pl.BlockSpec(memory_space=pl.ANY)


def shaped(*shape, dtype=F32):
    return jax.ShapeDtypeStruct(shape, dtype)


def call(kernel, name, in_specs, outs, scratch, cost, aliases=None):
    return pl.pallas_call(
        kernel,
        out_shape=outs,
        in_specs=in_specs,
        out_specs=jax.tree.map(lambda unused: V, outs),
        scratch_shapes=scratch,
        name=name,
        input_output_aliases=aliases or {},
        cost_estimate=pl.CostEstimate(flops=cost, bytes_accessed=1 << 20, transcendentals=0),
        compiler_params=pltpu.CompilerParams(vmem_limit_bytes=VMEM_LIMIT),
    )


def features_out(count):
    return [shaped(count, SIZE, FEATURES, dtype=BF16), shaped(count, 16, SIZE, dtype=BF16)]


def stages(with_target):
    out = [pltpu.VMEM((LEAVES, FEATURES, SIZE), F32), pltpu.VMEM((LEAVES, 16, SIZE), F32)]
    return ([pltpu.VMEM((LEAVES, FEATURES, SIZE), F32)] if with_target else []) + out


SMALL = 4_000_000
PAIR = 400_000_000


def run_direct(name, tables, mask, feats, acc, mode="", extra=None, ins=(), outs=(), scratch=()):
    zero = acc is None
    args = [mask, *feats] + ([] if zero else [acc]) + list(ins)
    got = call(
        functools.partial(direct, tables, mode, zero, extra, len(ins)),
        name,
        [V] * len(args),
        [shaped(LEAVES, 16, SIZE), *outs],
        list(scratch),
        PAIR * tables.shape[1],
        {} if zero else {4: 0},
    )(*args)
    return got if outs else got[0]


def far_scratch(width):
    return [pltpu.VMEM((4 * ORDER - 2, LEAVES, width), F32), pltpu.VMEM((24, width), F32)]


def body(particles, near_mask):
    turned = near_mask.transpose(1, 2, 0)
    t0, s0, w0, m0, f0, send_a, send_b = call(
        prepare_own,
        "prepare_own",
        [V],
        [shaped(LEAVES, FEATURES, SIZE, dtype=BF16), *features_out(LEAVES), shaped(24, 128), shaped(24, 128)]
        + [shaped(SLAB_ROWS, SIZE)] * 2,
        stages(True),
        SMALL,
    )(particles)
    own = pair_table("own")
    flex = own[: 28 * FLEX].reshape(FLEX, 28, 3)
    feats = (t0, s0, w0)
    acc, mask = run_direct(
        "direct_early", flex, turned, feats, None, "early", outs=[shaped(17, LEAVES, 1, SIZE)]
    )
    send_a, send_b, acc = lax.optimization_barrier((send_a, send_b, acc))
    recv_a = swap(send_a, "core")
    recv_b = swap(send_b, "slab")
    acc = run_direct("direct_own_0", own[None, 56:98], mask, feats, acc)
    m1, f1, send_near, send_far = call(
        pack_slab,
        "pack_slab",
        [V, V, V, V, V, A],
        [shaped(24, 128), shaped(24, 128), shaped(LEAF_ROWS, SIZE), shaped(72, SIZE)],
        [],
        SMALL,
    )(particles, recv_a, recv_b, m0, f0, acc)
    send_near, acc = lax.optimization_barrier((send_near, acc))
    recv_near = swap(send_near, "leaf_near")
    built = dict(outs=features_out(LEAVES), scratch=stages(False))
    acc, s1, w1 = run_direct(
        "direct_own_1", own[None, 98:147], mask, feats, acc, extra=slab_halo, ins=(recv_a, recv_b), **built
    )
    f2, send_far = call(
        pack_near, "pack_near", [V, V, V, A], [shaped(24, 128), shaped(LEAF_ROWS, SIZE)], [], SMALL
    )(recv_near, f1, send_far, acc)
    send_far, acc = lax.optimization_barrier((send_far, acc))
    recv_far = swap(send_far, "leaf_far")
    acc, s2, w2 = run_direct(
        "direct_own_2", own[None, 147:], mask, feats, acc, extra=near_halo, ins=(recv_near,), **built
    )
    recv_far, acc = lax.optimization_barrier((recv_far, acc))
    blocks = f2 + recv_far[72:96, 0:128]
    slab_pairs = pair_table("slab").reshape(2, 1, 42, 3)
    right = pair_table("leaf", True)
    left = pair_table("leaf", False)
    far_pairs = np.stack([left, right])
    slab_feats = (t0, s1, w1)
    blocks, acc = lax.optimization_barrier((blocks, acc))
    got = swap(blocks, "z_near")
    acc, s3, w3 = run_direct(
        "direct_slab_0", slab_pairs[0], mask, slab_feats, acc, extra=far_halo, ins=(recv_far,), **built
    )
    got, acc = lax.optimization_barrier((got, acc))
    blocks, acc = lax.optimization_barrier((blocks + got, acc))
    got = swap(blocks, "z_far")
    acc = run_direct("direct_slab_1", slab_pairs[1], mask, slab_feats, acc)
    got, acc = lax.optimization_barrier((got, acc))
    blocks, acc = lax.optimization_barrier((blocks + got, acc))
    got = swap(blocks, "x_near")
    acc, local = run_direct(
        "direct_leaf_near",
        np.stack([right, left]),
        mask,
        (t0, s2, w2),
        acc,
        "side",
        extra=leaf_field,
        ins=(turned, m1, recv_near, recv_far),
        outs=[shaped(LEAVES, 128)],
        scratch=far_scratch(256),
    )
    got, acc = lax.optimization_barrier((got, acc))
    blocks, acc = lax.optimization_barrier((blocks + got, acc))
    got = swap(blocks, "x_far")
    acc = run_direct("direct_leaf_far_0", far_pairs[:, :30], mask, (t0, s3, w3), acc, "side")
    got, acc = lax.optimization_barrier((got, acc))
    blocks, acc = lax.optimization_barrier((blocks + got, acc))
    got = swap(blocks, "core")
    acc = run_direct("direct_leaf_far_1", far_pairs[:, 30:], mask, (t0, s3, w3), acc, "side")
    acc = run_direct("direct_late", flex, mask, feats, acc, "late")
    got, acc = lax.optimization_barrier((got, acc))
    return call(
        finish,
        "finish",
        [V] * 5,
        shaped(2, SIDE, SIDE, SIZE),
        far_scratch(128) + [pltpu.VMEM((LEAVES, 128), F32)],
        SMALL,
    )(particles, acc, local, blocks, got)


def solution(mesh):
    finer = Mesh(mesh.devices.reshape(4, 4, 2, mesh.shape["leaf"]), ALL)
    in_specs = (P(None, SLAB, "leaf", None), P(None, SLAB, "leaf"))
    out_specs = P(None, SLAB, "leaf", None)
    run = jax.shard_map(body, mesh=finer, in_specs=in_specs, out_specs=out_specs, check_vma=False)

    def whole(particles, near_mask):
        with jax.sharding.use_abstract_mesh(mesh.abstract_mesh):
            return run(particles, near_mask)

    return run
```

```python
import functools
import math

import jax
import jax.numpy as jnp
import numpy as np
from jax import lax
from jax.experimental import pallas as pl
from jax.experimental.pallas import tpu as pltpu
from jax.sharding import Mesh
from jax.sharding import PartitionSpec as P

ORDER = 10
SIDE = 4
LEAVES = 16
SIZE = 256
FEATURES = 32
DELTA_SQUARED = 0.0025
TWO_PI = 2.0 * math.pi
SLAB = ("slab_0", "slab_1", "slab_2")
ALL = ("slab_0", "slab_1", "slab_2", "leaf")
F32 = jnp.float32
BF16 = jnp.bfloat16
VMEM_LIMIT = 6 << 20
cycle_steps = [(a, b) for a in range(-2, 3) for b in range(-2, 3) if max(abs(a), abs(b)) == 2]
near_steps = [(a, b) for a in range(-2, 3) for b in range(-2, 3)]


def exchange_pairs(partner):
    pairs = []
    for x in range(4):
        for z in range(4):
            for c in range(2):
                for y in range(4):
                    other = partner(x, z, c, y)
                    if other is not None:
                        a, b, d, e = other
                        pairs.append((((x * 4 + z) * 2 + c) * 4 + y, ((a * 4 + b) * 2 + d) * 4 + e))
    return pairs


def inner_slab(slab):
    return jnp.logical_and(slab > 0, slab < 31).astype(F32)


def slab_between_chips(x, z, c, y):
    slab = (x * 4 + z) * 2 + c
    other = (slab + 1 if c == 1 else slab - 1) % 32
    return (other // 8, (other // 2) % 4, other % 2, y)


def near_side(k):
    return k ^ 1


def far_side(k):
    return 3 - k


SWAPS = {
    "core": exchange_pairs(lambda x, z, c, y: (x, z, 1 - c, y)),
    "slab": exchange_pairs(slab_between_chips),
    "leaf_near": exchange_pairs(lambda x, z, c, y: (x, z, c, near_side(y))),
    "leaf_far": exchange_pairs(lambda x, z, c, y: (x, z, c, far_side(y))),
    "z_near": exchange_pairs(lambda x, z, c, y: (x, near_side(z), c, y)),
    "z_far": exchange_pairs(lambda x, z, c, y: (x, far_side(z), c, y)),
    "x_near": exchange_pairs(lambda x, z, c, y: (near_side(x), z, c, y)),
    "x_far": exchange_pairs(lambda x, z, c, y: (far_side(x), z, c, y)),
}


def swap(value, name):
    return lax.ppermute(value, ALL, SWAPS[name])


def pieces(value, count):
    parts = []
    for unused in range(count):
        part = value.astype(BF16).astype(F32)
        parts.append(part)
        value = value - part
    return parts


def build_features(wx, wy, g, ox, oy, stage_t, stage_s, stage_w, t_ref, s_ref, w_ref, first, with_target):
    count = wx.shape[0]
    one = jnp.ones_like(wx)
    zero = jnp.zeros_like(wx)
    coarse_x = jnp.round(wx * 32.0) * (1.0 / 32.0)
    coarse_y = jnp.round(wy * 32.0) * (1.0 / 32.0)
    fine_x = wx - coarse_x
    fine_y = wy - coarse_y
    big_x = coarse_x + ox
    big_y = coarse_y + oy
    big = pieces(big_x * big_x + big_y * big_y, 2)
    rest = 2.0 * (big_x * fine_x + big_y * fine_y) + fine_x * fine_x + fine_y * fine_y
    px = pieces(fine_x, 2)
    py = pieces(fine_y, 2)
    if with_target:
        rows = [big_x, big_y, big[0], big[1], one, one, zero, zero]
        rows += [big_x, big_x, big_y, big_y, px[0], px[1], py[0], py[1]]
        rows += [px[0], px[0], px[1], py[0], py[0], py[1]]
        rows += pieces(rest + DELTA_SQUARED, 3) + [one, one, one]
        rows += [zero] * (FEATURES - len(rows))
        for f, row in enumerate(rows):
            stage_t[:count, f, :] = row
    twice = lambda v: -2.0 * v
    rows = [twice(big_x), twice(big_y), one, one, big[0], big[1], zero, zero]
    rows += [twice(px[0]), twice(px[1]), twice(py[0]), twice(py[1])]
    rows += [twice(big_x), twice(big_x), twice(big_y), twice(big_y)]
    rows += [twice(px[0]), twice(px[1]), twice(px[0]), twice(py[0]), twice(py[1]), twice(py[0])]
    rows += [one, one, one] + pieces(rest, 3)
    rows += [zero] * (FEATURES - len(rows))
    for f, row in enumerate(rows):
        stage_s[:count, f, :] = row
    rows = pieces(g, 3) + pieces(g * (wx + ox), 3) + pieces(g * (wy + oy), 3)
    rows += [zero] * (16 - len(rows))
    for f, row in enumerate(rows):
        stage_w[:count, f, :] = row
    for n in range(count):
        if with_target:
            t_ref[first + n] = stage_t[n].astype(BF16)
        s_ref[first + n] = jnp.transpose(stage_s[n]).astype(BF16)
        w_ref[first + n] = stage_w[n].astype(BF16)


def power_list(base_re, base_im, count):
    re = [jnp.ones_like(base_re)]
    im = [jnp.zeros_like(base_im)]
    for unused in range(1, count):
        a, b = re[-1], im[-1]
        re.append(a * base_re - b * base_im)
        im.append(a * base_im + b * base_re)
    return re, im


def row_of(n):
    return lax.broadcasted_iota(jnp.int32, (n, 1), 0)


def leaf_offsets():
    n = row_of(LEAVES)
    ox = (n >> 2).astype(F32) - 1.5
    oy = (n & 3).astype(F32) - 1.5
    return ox, oy


def own_rows(ref, part):
    return jnp.concatenate([ref[part, i] for i in range(SIDE)], axis=0)


def position():
    slab = lax.axis_index(SLAB)
    leaf = lax.axis_index("leaf")
    between = jnp.logical_and(leaf > 0, leaf < 3).astype(jnp.int32)
    return slab, leaf, slab & 1, leaf & 1, between


SLAB_ROWS = 72
LEAF_ROWS = 96


def prepare_own(part_ref, t_ref, s_ref, w_ref, m_ref, f_ref, a_ref, b_ref, stage_t, stage_s, stage_w):
    info = position()
    wx = own_rows(part_ref, 0)
    wy = own_rows(part_ref, 1)
    g = own_rows(part_ref, 2)
    ox, oy = leaf_offsets()
    lane = lax.broadcasted_iota(jnp.int32, (LEAVES, 128), 1)
    table = jnp.zeros((LEAVES, 128), F32)
    for start, base_re, base_im in ((0, wx, wy), (32, wx + ox, wy + oy)):
        re, im = power_list(base_re, base_im, ORDER)
        for k in range(ORDER):
            table = jnp.where(lane == start + k, jnp.sum(g * re[k], 1, keepdims=True), table)
            if k:
                table = jnp.where(lane == start + ORDER + k, jnp.sum(g * im[k], 1, keepdims=True), table)
    turned = jnp.transpose(table)
    leaf_part = jnp.concatenate([turned[0:24], jnp.zeros((24, 112), F32)], axis=1)
    block_part = jnp.sum(turned[32:56], axis=1, keepdims=True)
    me = info[0] * 4 + info[1]
    wide = lax.broadcasted_iota(jnp.int32, (24, 128), 1)
    block_row = jnp.where(wide == me, block_part, 0.0)
    m_ref[...] = leaf_part
    f_ref[...] = block_row
    even = info[2] == 0
    for c in range(3):
        first = jnp.concatenate([part_ref[c, 0], part_ref[c, 1]], axis=0)
        last = jnp.concatenate([part_ref[c, 2], part_ref[c, 3]], axis=0)
        a_ref[8 * c : 8 * c + 8] = jnp.where(even, last, first)
        b_ref[8 * c : 8 * c + 8] = jnp.where(even, first, last)
    none = jnp.zeros((24, 128), F32)
    for ref in (a_ref, b_ref):
        ref[24:48, 0:128] = leaf_part
        ref[24:48, 128:256] = none
        ref[48:72, 0:128] = block_row
        ref[48:72, 128:256] = none
    build_features(wx, wy, g, ox, oy, stage_t, stage_s, stage_w, t_ref, s_ref, w_ref, 0, True)


def pack_slab(part_ref, ra_ref, rb_ref, m_ref, f_ref, after_ref, m_out, f_out, near_ref, far_ref):
    info = position()
    even = info[2] == 0
    leaf_even = info[3] == 0
    inner = inner_slab(info[0])
    for c in range(3):
        ra = ra_ref[8 * c : 8 * c + 8]
        rb = rb_ref[8 * c : 8 * c + 8]
        if c == 2:
            rb = rb * inner
        before = jnp.where(even, rb, ra)
        after = jnp.where(even, ra, rb)
        rows = [before[0:4], before[4:8]] + [part_ref[c, i] for i in range(SIDE)] + [after[0:4], after[4:8]]
        left = jnp.concatenate([r[0:2] for r in rows], axis=0)
        right = jnp.concatenate([r[2:4] for r in rows], axis=0)
        near_ref[16 * c : 16 * c + 16] = jnp.where(leaf_even, right, left)
        far_ref[16 * c : 16 * c + 16] = jnp.where(leaf_even, left, right)
    ma = ra_ref[24:48, 0:16]
    mb = rb_ref[24:48, 0:16] * inner
    window = jnp.concatenate(
        [m_ref[:, 0:16], jnp.where(even, mb, ma), jnp.where(even, ma, mb), jnp.zeros((24, 80), F32)], axis=1
    )
    blocks = f_ref[...] + ra_ref[48:72, 0:128]
    m_out[...] = window
    f_out[...] = blocks
    none = jnp.zeros((24, 128), F32)
    near_ref[48:72, 0:128] = jnp.concatenate([none[:, 0:48], window[:, 0:48], none[:, 0:32]], axis=1)
    near_ref[48:72, 128:256] = none
    far_ref[48:72, 0:128] = window
    far_ref[48:72, 128:256] = none
    near_ref[72:96, 0:128] = blocks
    near_ref[72:96, 128:256] = none


def slab_halo(ra_ref, rb_ref, s_ref, w_ref, stage_s, stage_w):
    even = position()[2] == 0
    inner = inner_slab(position()[0])
    halo = []
    for c in range(3):
        ra = ra_ref[8 * c : 8 * c + 8]
        rb = rb_ref[8 * c : 8 * c + 8]
        if c == 2:
            rb = rb * inner
        halo.append(jnp.concatenate([jnp.where(even, rb, ra), jnp.where(even, ra, rb)], axis=0))
    n = row_of(LEAVES)
    i = (n >> 2) - 2
    ox = jnp.where(i >= 0, i + 4, i).astype(F32) - 1.5
    oy = (n & 3).astype(F32) - 1.5
    build_features(halo[0], halo[1], halo[2], ox, oy, None, stage_s, stage_w, None, s_ref, w_ref, 0, False)


def leaf_halo(which, r_ref, s_ref, w_ref, stage_s, stage_w):
    info = position()
    leaf_even = info[3] == 0
    to_right = leaf_even if which == 0 else jnp.logical_not(leaf_even)
    valid = jnp.float32(1.0) if which == 0 else info[4].astype(F32)
    n = row_of(LEAVES)
    ox = (n >> 1).astype(F32) - 3.5
    side = (n & 1).astype(F32)
    oy = jnp.where(to_right, side + 4.0, side - 2.0) - 1.5
    build_features(
        r_ref[0:16], r_ref[16:32], r_ref[32:48] * valid, ox, oy, None, stage_s, stage_w, None, s_ref, w_ref, 0, False
    )


def near_halo(r_ref, s_ref, w_ref, stage_s, stage_w):
    leaf_halo(0, r_ref, s_ref, w_ref, stage_s, stage_w)


def far_halo(r_ref, s_ref, w_ref, stage_s, stage_w):
    leaf_halo(1, r_ref, s_ref, w_ref, stage_s, stage_w)


def pack_near(r_ref, f_ref, send_ref, after_ref, f_out, send_out):
    blocks = f_ref[...] + r_ref[72:96, 0:128]
    f_out[...] = blocks
    send_out[0:72] = send_ref[...]
    send_out[72:96, 0:128] = blocks
    send_out[72:96, 128:256] = jnp.zeros((24, 128), F32)


def chosen(index, values):
    if all(v == values[0] for v in values):
        return values[0]
    out = values[-1]
    for n in range(len(values) - 2, -1, -1):
        out = jnp.where(index == n, values[n], out)
    return out


def direct(tables, by_side, zero, extra, extra_in, mask_ref, t_ref, s_ref, w_ref, *refs):
    if zero:
        acc_ref, rows_ref = refs
        acc_ref[...] = jnp.zeros_like(acc_ref)
        near_mask = jnp.concatenate([mask_ref[i] for i in range(SIDE)], axis=0).astype(F32)
        for o in range(16):
            rows_ref[o, :, 0, :] = jnp.broadcast_to(near_mask[:, o : o + 1], (LEAVES, SIZE))
        rows_ref[16, :, 0, :] = jnp.ones((LEAVES, SIZE), F32)
        mask_ref = rows_ref
    else:
        acc_ref = refs[extra_in + 1]
        acc_ref[...] = refs[0][...]
        others = refs[1 : extra_in + 1] + refs[extra_in + 2 :]
    count = tables.shape[1]

    def step(index, unused):
        for n in range(count):
            t, s, o = (chosen(index, [int(v) for v in tables[:, n, c]]) for c in range(3))
            distance = jnp.dot(s_ref[s], t_ref[t], preferred_element_type=F32)
            kernel = 1.0 / distance
            high = kernel.astype(BF16)
            low = (kernel - high.astype(F32)).astype(BF16)
            w = w_ref[s]
            total = jnp.dot(w, high, preferred_element_type=F32) + jnp.dot(w, low, preferred_element_type=F32)
            if isinstance(o, int) and o == 16:
                acc_ref[t] = acc_ref[t] + total
            else:
                acc_ref[t] = acc_ref[t] + mask_ref[o, t] * total
        return 0

    if by_side:
        step(position()[3], 0)
    elif tables.shape[0] == 1:
        step(0, 0)
    else:
        lax.fori_loop(0, tables.shape[0], step, 0)
    if extra is not None:
        extra(*others)


def pair_table(kind, to_right=False):
    out = []
    for t in range(LEAVES):
        i, j = divmod(t, SIDE)
        for a, b in near_steps:
            o = cycle_steps.index((a, b)) if max(abs(a), abs(b)) == 2 else 16
            si, sj = i + a, j + b
            in_row, in_column = 0 <= si < SIDE, 0 <= sj < SIDE
            if kind == "own" and in_row and in_column:
                out.append((t, si * SIDE + sj, o))
            if kind == "slab" and not in_row and in_column:
                out.append((t, ((si + 2) if si < 0 else (si - 2)) * SIDE + sj, o))
            if kind == "leaf" and not in_column and (sj >= SIDE) == to_right:
                out.append((t, (si + 2) * 2 + (sj - SIDE if to_right else sj + 2), o))
    return np.array(out, np.int32)


def translate(groups, h_ref, a_ref, out_ref):
    for group, (tx, ty, weight) in enumerate(groups):
        span = slice(128 * group, 128 * group + 128)
        square = tx * tx + ty * ty
        inv_x = tx / square
        inv_y = -ty / square
        re = weight * inv_x
        im = weight * inv_y
        h_ref[0, :, span] = re
        h_ref[1, :, span] = im
        for order in range(1, 2 * ORDER - 1):
            re, im = (re * inv_x - im * inv_y) * float(order), (re * inv_y + im * inv_x) * float(order)
            h_ref[2 * order, :, span] = re
            h_ref[2 * order + 1, :, span] = im
    lane = lax.broadcasted_iota(jnp.int32, (LEAVES, 128), 1)
    table = jnp.zeros((LEAVES, 128), F32)
    half = ORDER // 2
    for first in (0, half):
        sums_re = [None] * half
        sums_im = [None] * half
        for group in range(len(groups)):
            span = slice(128 * group, 128 * group + 128)
            for k_ in range(ORDER):
                a_re = a_ref[k_ : k_ + 1, span]
                a_im = a_ref[ORDER + k_ : ORDER + k_ + 1, span]
                for m in range(half):
                    at = first + m + k_
                    h_re = h_ref[2 * at, :, span]
                    h_im = h_ref[2 * at + 1, :, span]
                    term_re = h_re * a_re - h_im * a_im
                    term_im = h_re * a_im + h_im * a_re
                    sums_re[m] = term_re if sums_re[m] is None else sums_re[m] + term_re
                    sums_im[m] = term_im if sums_im[m] is None else sums_im[m] + term_im
        for m in range(half):
            factor = 1.0 / math.factorial(first + m)
            table = jnp.where(lane == first + m, jnp.sum(sums_re[m], 1, keepdims=True) * factor, table)
            table = jnp.where(lane == 64 + first + m, jnp.sum(sums_im[m], 1, keepdims=True) * factor, table)
    out_ref[...] = table


def source_scale():
    row = row_of(24)
    which = jnp.where(row >= ORDER, row - ORDER, row)
    scale = jnp.zeros((24, 1), F32)
    for k_ in range(ORDER):
        scale = jnp.where(which == k_, (-1.0) ** (k_ + 1) / math.factorial(k_), scale)
    return scale


def leaf_field(nm_ref, m_ref, r1_ref, r2_ref, out_ref, h_ref, a_ref):
    info = position()
    leaf_even = info[3] == 0
    valid = info[4].astype(F32)
    n = row_of(LEAVES)
    ti = n >> 2
    tj = n & 3
    lane = lax.broadcasted_iota(jnp.int32, (LEAVES, 128), 1)
    near_mask = jnp.concatenate([nm_ref[i] for i in range(SIDE)], axis=0).astype(F32)
    near_shift = jnp.where(leaf_even, 4, -4)
    second = lane >= 48
    place = jnp.where(second, lane - 48, lane)
    k = place >> 4
    r = place & 15
    si = jnp.where(k == 0, r >> 2, jnp.where(k == 1, (r >> 2) - 4, (r >> 2) + 4))
    groups = []
    for column, lanes in ((jnp.where(second, near_shift, 0), 96), (-near_shift, 48)):
        dx = si - ti
        dy = (r & 3) + column - tj
        reach = jnp.maximum(jnp.abs(dx), jnp.abs(dy))
        weight = jnp.where(reach >= 3, 1.0, 0.0).astype(F32)
        for o, (a, b) in enumerate(cycle_steps):
            hit = jnp.logical_and(dx == a, dy == b)
            weight = jnp.where(hit, 1.0 - near_mask[:, o : o + 1], weight)
        inside = lane < lanes
        used = jnp.logical_and(reach >= 2, inside)
        groups.append(
            (
                jnp.where(used, dx.astype(F32), 1.0),
                jnp.where(used, dy.astype(F32), 1.0),
                jnp.where(inside, weight, 0.0),
            )
        )
    scale = source_scale()
    a_ref[:, 0:128] = (m_ref[...] + r1_ref[48:72, 0:128]) * scale
    a_ref[:, 128:256] = r2_ref[48:72, 0:128] * (valid * scale)
    translate(groups, h_ref, a_ref, out_ref)


def finish(part_ref, acc_ref, near_ref, f_ref, got_ref, out_ref, h_ref, a_ref, l_ref):
    info = position()
    n = row_of(LEAVES)
    ti = n >> 2
    tj = n & 3
    lane = lax.broadcasted_iota(jnp.int32, (LEAVES, 128), 1)
    bx = (lane >> 2) - info[0]
    by = (lane & 3) - info[1]
    remote = jnp.maximum(jnp.abs(bx), jnp.abs(by)) >= 2
    tx = jnp.where(remote, (bx * SIDE - ti).astype(F32) + 1.5, 1.0)
    ty = jnp.where(remote, (by * SIDE - tj).astype(F32) + 1.5, 1.0)
    weight = jnp.where(remote, 1.0, 0.0).astype(F32)
    a_ref[...] = (f_ref[...] + got_ref[...]) * source_scale()
    translate([(tx, ty, weight)], h_ref, a_ref, l_ref)
    local = l_ref[...] + near_ref[...]
    wx = own_rows(part_ref, 0)
    wy = own_rows(part_ref, 1)
    ox, oy = leaf_offsets()
    x = wx + ox
    y = wy + oy
    rows = lambda at: acc_ref[:, at, :] + acc_ref[:, at + 1, :] + acc_ref[:, at + 2, :]
    total = rows(0)
    sum_re = x * total - rows(3)
    sum_im = rows(6) - y * total
    p_re = jnp.ones_like(wx)
    p_im = jnp.zeros_like(wx)
    for m in range(ORDER):
        if m:
            p_re, p_im = p_re * wx - p_im * wy, p_re * wy + p_im * wx
        l_re = local[:, m : m + 1]
        l_im = local[:, 64 + m : 65 + m]
        sum_re = sum_re + (l_re * p_re - l_im * p_im)
        sum_im = sum_im + (l_re * p_im + l_im * p_re)
    sum_re = sum_re * (1.0 / TWO_PI)
    sum_im = sum_im * (1.0 / TWO_PI)
    for i in range(SIDE):
        out_ref[0, i] = sum_im[4 * i : 4 * i + 4]
        out_ref[1, i] = sum_re[4 * i : 4 * i + 4]


V = pl.BlockSpec(memory_space=pltpu.VMEM)
S = pl.BlockSpec(memory_space=pltpu.SMEM)
A = pl.BlockSpec(memory_space=pl.ANY)


def shaped(*shape, dtype=F32):
    return jax.ShapeDtypeStruct(shape, dtype)


def call(kernel, name, in_specs, outs, scratch, cost, aliases=None):
    return pl.pallas_call(
        kernel,
        out_shape=outs,
        in_specs=in_specs,
        out_specs=jax.tree.map(lambda unused: V, outs),
        scratch_shapes=scratch,
        name=name,
        input_output_aliases=aliases or {},
        cost_estimate=pl.CostEstimate(flops=cost, bytes_accessed=1 << 20, transcendentals=0),
        compiler_params=pltpu.CompilerParams(vmem_limit_bytes=VMEM_LIMIT),
    )


def features_out(count):
    return [shaped(count, SIZE, FEATURES, dtype=BF16), shaped(count, 16, SIZE, dtype=BF16)]


def stages(with_target):
    out = [pltpu.VMEM((LEAVES, FEATURES, SIZE), F32), pltpu.VMEM((LEAVES, 16, SIZE), F32)]
    return ([pltpu.VMEM((LEAVES, FEATURES, SIZE), F32)] if with_target else []) + out


SMALL = 4_000_000
PAIR = 400_000_000


def run_direct(name, tables, mask, feats, acc, by_side=False, extra=None, ins=(), outs=(), scratch=()):
    zero = acc is None
    args = [mask, *feats] + ([] if zero else [acc]) + list(ins)
    got = call(
        functools.partial(direct, tables, by_side, zero, extra, len(ins)),
        name,
        [V] * len(args),
        [shaped(LEAVES, 16, SIZE), *outs],
        list(scratch),
        PAIR * (1 if by_side else tables.shape[0]) * tables.shape[1],
        {} if zero else {4: 0},
    )(*args)
    return got if outs else got[0]


def far_scratch(width):
    return [pltpu.VMEM((4 * ORDER - 2, LEAVES, width), F32), pltpu.VMEM((24, width), F32)]


def body(particles, near_mask):
    turned = near_mask.transpose(1, 2, 0)
    t0, s0, w0, m0, f0, send_a, send_b = call(
        prepare_own,
        "prepare_own",
        [V],
        [shaped(LEAVES, FEATURES, SIZE, dtype=BF16), *features_out(LEAVES), shaped(24, 128), shaped(24, 128)]
        + [shaped(SLAB_ROWS, SIZE)] * 2,
        stages(True),
        SMALL,
    )(particles)
    recv_a = swap(send_a, "core")
    recv_b = swap(send_b, "slab")
    own = pair_table("own")
    feats = (t0, s0, w0)
    acc, mask = run_direct(
        "direct_own_0", own[:98].reshape(2, 49, 3), turned, feats, None, outs=[shaped(17, LEAVES, 1, SIZE)]
    )
    m1, f1, send_near, send_far = call(
        pack_slab,
        "pack_slab",
        [V, V, V, V, V, A],
        [shaped(24, 128), shaped(24, 128), shaped(LEAF_ROWS, SIZE), shaped(72, SIZE)],
        [],
        SMALL,
    )(particles, recv_a, recv_b, m0, f0, acc)
    send_near, acc = lax.optimization_barrier((send_near, acc))
    recv_near = swap(send_near, "leaf_near")
    built = dict(outs=features_out(LEAVES), scratch=stages(False))
    acc, s1, w1 = run_direct(
        "direct_own_1", own[None, 98:147], mask, feats, acc, extra=slab_halo, ins=(recv_a, recv_b), **built
    )
    f2, send_far = call(
        pack_near, "pack_near", [V, V, V, A], [shaped(24, 128), shaped(LEAF_ROWS, SIZE)], [], SMALL
    )(recv_near, f1, send_far, acc)
    send_far, acc = lax.optimization_barrier((send_far, acc))
    recv_far = swap(send_far, "leaf_far")
    acc, s2, w2 = run_direct(
        "direct_own_2", own[None, 147:], mask, feats, acc, extra=near_halo, ins=(recv_near,), **built
    )
    recv_far, acc = lax.optimization_barrier((recv_far, acc))
    f3 = f2 + recv_far[72:96, 0:128]
    f3, acc = lax.optimization_barrier((f3, acc))
    got = swap(f3, "z_near")
    acc, s3, w3 = run_direct(
        "direct_slab",
        pair_table("slab").reshape(2, 42, 3),
        mask,
        (t0, s1, w1),
        acc,
        extra=far_halo,
        ins=(recv_far,),
        **built,
    )
    got, acc = lax.optimization_barrier((got, acc))
    f4 = f3 + got
    f4, acc = lax.optimization_barrier((f4, acc))
    got = swap(f4, "z_far")
    right = pair_table("leaf", True)
    left = pair_table("leaf", False)
    near_pairs = np.stack([right, left])
    far_pairs = np.stack([left, right])
    acc, local = run_direct(
        "direct_leaf_near",
        near_pairs,
        mask,
        (t0, s2, w2),
        acc,
        True,
        extra=leaf_field,
        ins=(turned, m1, recv_near, recv_far),
        outs=[shaped(LEAVES, 128)],
        scratch=far_scratch(256),
    )
    got, acc = lax.optimization_barrier((got, acc))
    f5 = f4 + got
    f5, acc = lax.optimization_barrier((f5, acc))
    got = swap(f5, "x_near")
    acc = run_direct("direct_leaf_far_0", far_pairs[:, :30], mask, (t0, s3, w3), acc, True)
    got, acc = lax.optimization_barrier((got, acc))
    f6 = f5 + got
    f6, acc = lax.optimization_barrier((f6, acc))
    got = swap(f6, "x_far")
    acc = run_direct("direct_leaf_far_1", far_pairs[:, 30:], mask, (t0, s3, w3), acc, True)
    got, acc = lax.optimization_barrier((got, acc))
    return call(
        finish,
        "finish",
        [V] * 5,
        shaped(2, SIDE, SIDE, SIZE),
        far_scratch(128) + [pltpu.VMEM((LEAVES, 128), F32)],
        SMALL,
    )(particles, acc, local, f6, got)


def solution(mesh):
    finer = Mesh(mesh.devices.reshape(4, 4, 2, mesh.shape["leaf"]), ALL)
    in_specs = (P(None, SLAB, "leaf", None), P(None, SLAB, "leaf"))
    out_specs = P(None, SLAB, "leaf", None)
    run = jax.shard_map(body, mesh=finer, in_specs=in_specs, out_specs=out_specs, check_vma=False)

    def whole(particles, near_mask):
        with jax.sharding.use_abstract_mesh(mesh.abstract_mesh):
            return run(particles, near_mask)

    return run
```

```python
import functools
import math

import jax
import jax.numpy as jnp
import numpy as np
from jax import lax
from jax.experimental import pallas as pl
from jax.experimental.pallas import tpu as pltpu
from jax.sharding import Mesh
from jax.sharding import PartitionSpec as P

ORDER = 10
SIDE = 4
LEAVES = 16
SIZE = 256
FEATURES = 32
DELTA_SQUARED = 0.0025
TWO_PI = 2.0 * math.pi
SLAB = ("slab_0", "slab_1", "slab_2")
ALL = ("slab_0", "slab_1", "slab_2", "leaf")
F32 = jnp.float32
BF16 = jnp.bfloat16
VMEM_LIMIT = 6 << 20
cycle_steps = [(a, b) for a in range(-2, 3) for b in range(-2, 3) if max(abs(a), abs(b)) == 2]
near_steps = [(a, b) for a in range(-2, 3) for b in range(-2, 3)]


def exchange_pairs(partner):
    pairs = []
    for x in range(4):
        for z in range(4):
            for c in range(2):
                for y in range(4):
                    other = partner(x, z, c, y)
                    if other is not None:
                        a, b, d, e = other
                        pairs.append((((x * 4 + z) * 2 + c) * 4 + y, ((a * 4 + b) * 2 + d) * 4 + e))
    return pairs


def inner_slab(slab):
    return jnp.logical_and(slab > 0, slab < 31).astype(F32)


def slab_between_chips(x, z, c, y):
    slab = (x * 4 + z) * 2 + c
    other = (slab + 1 if c == 1 else slab - 1) % 32
    return (other // 8, (other // 2) % 4, other % 2, y)


def near_side(k):
    return k ^ 1


def far_side(k):
    return 3 - k


SWAPS = {
    "core": exchange_pairs(lambda x, z, c, y: (x, z, 1 - c, y)),
    "slab": exchange_pairs(slab_between_chips),
    "leaf_near": exchange_pairs(lambda x, z, c, y: (x, z, c, near_side(y))),
    "leaf_far": exchange_pairs(lambda x, z, c, y: (x, z, c, far_side(y))),
    "z_near": exchange_pairs(lambda x, z, c, y: (x, near_side(z), c, y)),
    "z_far": exchange_pairs(lambda x, z, c, y: (x, far_side(z), c, y)),
    "x_near": exchange_pairs(lambda x, z, c, y: (near_side(x), z, c, y)),
    "x_far": exchange_pairs(lambda x, z, c, y: (far_side(x), z, c, y)),
}


def swap(value, name):
    return lax.ppermute(value, ALL, SWAPS[name])


def pieces(value, count):
    parts = []
    for unused in range(count):
        part = value.astype(BF16).astype(F32)
        parts.append(part)
        value = value - part
    return parts


def build_features(wx, wy, g, ox, oy, stage_t, stage_s, stage_w, t_ref, s_ref, w_ref, first, with_target):
    count = wx.shape[0]
    one = jnp.ones_like(wx)
    zero = jnp.zeros_like(wx)
    coarse_x = jnp.round(wx * 32.0) * (1.0 / 32.0)
    coarse_y = jnp.round(wy * 32.0) * (1.0 / 32.0)
    fine_x = wx - coarse_x
    fine_y = wy - coarse_y
    big_x = coarse_x + ox
    big_y = coarse_y + oy
    big = pieces(big_x * big_x + big_y * big_y, 2)
    rest = 2.0 * (big_x * fine_x + big_y * fine_y) + fine_x * fine_x + fine_y * fine_y
    px = pieces(fine_x, 2)
    py = pieces(fine_y, 2)
    if with_target:
        rows = [big_x, big_y, big[0], big[1], one, one, zero, zero]
        rows += [big_x, big_x, big_y, big_y, px[0], px[1], py[0], py[1]]
        rows += [px[0], px[0], px[1], py[0], py[0], py[1]]
        rows += pieces(rest + DELTA_SQUARED, 3) + [one, one, one]
        rows += [zero] * (FEATURES - len(rows))
        for f, row in enumerate(rows):
            stage_t[:count, f, :] = row
    twice = lambda v: -2.0 * v
    rows = [twice(big_x), twice(big_y), one, one, big[0], big[1], zero, zero]
    rows += [twice(px[0]), twice(px[1]), twice(py[0]), twice(py[1])]
    rows += [twice(big_x), twice(big_x), twice(big_y), twice(big_y)]
    rows += [twice(px[0]), twice(px[1]), twice(px[0]), twice(py[0]), twice(py[1]), twice(py[0])]
    rows += [one, one, one] + pieces(rest, 3)
    rows += [zero] * (FEATURES - len(rows))
    for f, row in enumerate(rows):
        stage_s[:count, f, :] = row
    rows = pieces(g, 3) + pieces(g * (wx + ox), 3) + pieces(g * (wy + oy), 3)
    rows += [zero] * (16 - len(rows))
    for f, row in enumerate(rows):
        stage_w[:count, f, :] = row
    for n in range(count):
        if with_target:
            t_ref[first + n] = stage_t[n].astype(BF16)
        s_ref[first + n] = jnp.transpose(stage_s[n]).astype(BF16)
        w_ref[first + n] = stage_w[n].astype(BF16)


def power_list(base_re, base_im, count):
    re = [jnp.ones_like(base_re)]
    im = [jnp.zeros_like(base_im)]
    for unused in range(1, count):
        a, b = re[-1], im[-1]
        re.append(a * base_re - b * base_im)
        im.append(a * base_im + b * base_re)
    return re, im


def row_of(n):
    return lax.broadcasted_iota(jnp.int32, (n, 1), 0)


def leaf_offsets():
    n = row_of(LEAVES)
    ox = (n >> 2).astype(F32) - 1.5
    oy = (n & 3).astype(F32) - 1.5
    return ox, oy


def own_rows(ref, part):
    return jnp.concatenate([ref[part, i] for i in range(SIDE)], axis=0)


def position():
    slab = lax.axis_index(SLAB)
    leaf = lax.axis_index("leaf")
    between = jnp.logical_and(leaf > 0, leaf < 3).astype(jnp.int32)
    return slab, leaf, slab & 1, leaf & 1, between


SLAB_ROWS = 72
LEAF_ROWS = 96


def prepare_own(part_ref, t_ref, s_ref, w_ref, m_ref, f_ref, a_ref, b_ref, stage_t, stage_s, stage_w):
    info = position()
    wx = own_rows(part_ref, 0)
    wy = own_rows(part_ref, 1)
    g = own_rows(part_ref, 2)
    ox, oy = leaf_offsets()
    lane = lax.broadcasted_iota(jnp.int32, (LEAVES, 128), 1)
    table = jnp.zeros((LEAVES, 128), F32)
    for start, base_re, base_im in ((0, wx, wy), (32, wx + ox, wy + oy)):
        re, im = power_list(base_re, base_im, ORDER)
        for k in range(ORDER):
            table = jnp.where(lane == start + k, jnp.sum(g * re[k], 1, keepdims=True), table)
            if k:
                table = jnp.where(lane == start + ORDER + k, jnp.sum(g * im[k], 1, keepdims=True), table)
    turned = jnp.transpose(table)
    leaf_part = jnp.concatenate([turned[0:24], jnp.zeros((24, 112), F32)], axis=1)
    block_part = jnp.sum(turned[32:56], axis=1, keepdims=True)
    me = info[0] * 4 + info[1]
    wide = lax.broadcasted_iota(jnp.int32, (24, 128), 1)
    block_row = jnp.where(wide == me, block_part, 0.0)
    m_ref[...] = leaf_part
    f_ref[...] = block_row
    even = info[2] == 0
    for c in range(3):
        first = jnp.concatenate([part_ref[c, 0], part_ref[c, 1]], axis=0)
        last = jnp.concatenate([part_ref[c, 2], part_ref[c, 3]], axis=0)
        a_ref[8 * c : 8 * c + 8] = jnp.where(even, last, first)
        b_ref[8 * c : 8 * c + 8] = jnp.where(even, first, last)
    none = jnp.zeros((24, 128), F32)
    for ref in (a_ref, b_ref):
        ref[24:48, 0:128] = leaf_part
        ref[24:48, 128:256] = none
        ref[48:72, 0:128] = block_row
        ref[48:72, 128:256] = none
    build_features(wx, wy, g, ox, oy, stage_t, stage_s, stage_w, t_ref, s_ref, w_ref, 0, True)


def pack_slab(part_ref, ra_ref, rb_ref, m_ref, f_ref, after_ref, m_out, f_out, near_ref, far_ref):
    info = position()
    even = info[2] == 0
    leaf_even = info[3] == 0
    inner = inner_slab(info[0])
    for c in range(3):
        ra = ra_ref[8 * c : 8 * c + 8]
        rb = rb_ref[8 * c : 8 * c + 8]
        if c == 2:
            rb = rb * inner
        before = jnp.where(even, rb, ra)
        after = jnp.where(even, ra, rb)
        rows = [before[0:4], before[4:8]] + [part_ref[c, i] for i in range(SIDE)] + [after[0:4], after[4:8]]
        left = jnp.concatenate([r[0:2] for r in rows], axis=0)
        right = jnp.concatenate([r[2:4] for r in rows], axis=0)
        near_ref[16 * c : 16 * c + 16] = jnp.where(leaf_even, right, left)
        far_ref[16 * c : 16 * c + 16] = jnp.where(leaf_even, left, right)
    ma = ra_ref[24:48, 0:16]
    mb = rb_ref[24:48, 0:16] * inner
    window = jnp.concatenate(
        [m_ref[:, 0:16], jnp.where(even, mb, ma), jnp.where(even, ma, mb), jnp.zeros((24, 80), F32)], axis=1
    )
    blocks = f_ref[...] + ra_ref[48:72, 0:128]
    m_out[...] = window
    f_out[...] = blocks
    none = jnp.zeros((24, 128), F32)
    near_ref[48:72, 0:128] = jnp.concatenate([none[:, 0:48], window[:, 0:48], none[:, 0:32]], axis=1)
    near_ref[48:72, 128:256] = none
    far_ref[48:72, 0:128] = window
    far_ref[48:72, 128:256] = none
    near_ref[72:96, 0:128] = blocks
    near_ref[72:96, 128:256] = none


def slab_halo(ra_ref, rb_ref, s_ref, w_ref, stage_s, stage_w):
    even = position()[2] == 0
    inner = inner_slab(position()[0])
    halo = []
    for c in range(3):
        ra = ra_ref[8 * c : 8 * c + 8]
        rb = rb_ref[8 * c : 8 * c + 8]
        if c == 2:
            rb = rb * inner
        halo.append(jnp.concatenate([jnp.where(even, rb, ra), jnp.where(even, ra, rb)], axis=0))
    n = row_of(LEAVES)
    i = (n >> 2) - 2
    ox = jnp.where(i >= 0, i + 4, i).astype(F32) - 1.5
    oy = (n & 3).astype(F32) - 1.5
    build_features(halo[0], halo[1], halo[2], ox, oy, None, stage_s, stage_w, None, s_ref, w_ref, 0, False)


def leaf_halo(which, r_ref, s_ref, w_ref, stage_s, stage_w):
    info = position()
    leaf_even = info[3] == 0
    to_right = leaf_even if which == 0 else jnp.logical_not(leaf_even)
    valid = jnp.float32(1.0) if which == 0 else info[4].astype(F32)
    n = row_of(LEAVES)
    ox = (n >> 1).astype(F32) - 3.5
    side = (n & 1).astype(F32)
    oy = jnp.where(to_right, side + 4.0, side - 2.0) - 1.5
    build_features(
        r_ref[0:16], r_ref[16:32], r_ref[32:48] * valid, ox, oy, None, stage_s, stage_w, None, s_ref, w_ref, 0, False
    )


def near_halo(r_ref, s_ref, w_ref, stage_s, stage_w):
    leaf_halo(0, r_ref, s_ref, w_ref, stage_s, stage_w)


def far_halo(r_ref, s_ref, w_ref, stage_s, stage_w):
    leaf_halo(1, r_ref, s_ref, w_ref, stage_s, stage_w)


def pack_near(r_ref, f_ref, send_ref, after_ref, f_out, send_out):
    blocks = f_ref[...] + r_ref[72:96, 0:128]
    f_out[...] = blocks
    send_out[0:72] = send_ref[...]
    send_out[72:96, 0:128] = blocks
    send_out[72:96, 128:256] = jnp.zeros((24, 128), F32)


def chosen(index, values):
    if all(v == values[0] for v in values):
        return values[0]
    out = values[-1]
    for n in range(len(values) - 2, -1, -1):
        out = jnp.where(index == n, values[n], out)
    return out


def direct(tables, by_side, zero, extra, extra_in, mask_ref, t_ref, s_ref, w_ref, *refs):
    if zero:
        acc_ref, rows_ref = refs
        acc_ref[...] = jnp.zeros_like(acc_ref)
        near_mask = jnp.concatenate([mask_ref[i] for i in range(SIDE)], axis=0).astype(F32)
        for o in range(16):
            rows_ref[o, :, 0, :] = jnp.broadcast_to(near_mask[:, o : o + 1], (LEAVES, SIZE))
        rows_ref[16, :, 0, :] = jnp.ones((LEAVES, SIZE), F32)
        mask_ref = rows_ref
    else:
        acc_ref = refs[extra_in + 1]
        acc_ref[...] = refs[0][...]
        others = refs[1 : extra_in + 1] + refs[extra_in + 2 :]
    count = tables.shape[1]

    def step(index, unused):
        for n in range(count):
            t, s, o = (chosen(index, [int(v) for v in tables[:, n, c]]) for c in range(3))
            distance = jnp.dot(s_ref[s], t_ref[t], preferred_element_type=F32)
            kernel = 1.0 / distance
            high = kernel.astype(BF16)
            low = (kernel - high.astype(F32)).astype(BF16)
            w = w_ref[s]
            total = jnp.dot(w, high, preferred_element_type=F32) + jnp.dot(w, low, preferred_element_type=F32)
            if isinstance(o, int) and o == 16:
                acc_ref[t] = acc_ref[t] + total
            else:
                acc_ref[t] = acc_ref[t] + mask_ref[o, t] * total
        return 0

    if by_side == "far":
        @pl.when(position()[4] == 1)
        def _():
            step(position()[3], 0)

    elif by_side:
        step(position()[3], 0)
    elif tables.shape[0] == 1:
        step(0, 0)
    else:
        lax.fori_loop(0, tables.shape[0], step, 0)
    if extra is not None:
        extra(*others)


def pair_table(kind, to_right=False):
    out = []
    for t in range(LEAVES):
        i, j = divmod(t, SIDE)
        for a, b in near_steps:
            o = cycle_steps.index((a, b)) if max(abs(a), abs(b)) == 2 else 16
            si, sj = i + a, j + b
            in_row, in_column = 0 <= si < SIDE, 0 <= sj < SIDE
            if kind == "own" and in_row and in_column:
                out.append((t, si * SIDE + sj, o))
            if kind == "slab" and not in_row and in_column:
                out.append((t, ((si + 2) if si < 0 else (si - 2)) * SIDE + sj, o))
            if kind == "leaf" and not in_column and (sj >= SIDE) == to_right:
                out.append((t, (si + 2) * 2 + (sj - SIDE if to_right else sj + 2), o))
    return np.array(out, np.int32)


def translate(groups, h_ref, a_ref, out_ref):
    for group, (tx, ty, weight) in enumerate(groups):
        span = slice(128 * group, 128 * group + 128)
        square = tx * tx + ty * ty
        inv_x = tx / square
        inv_y = -ty / square
        re = weight * inv_x
        im = weight * inv_y
        h_ref[0, :, span] = re
        h_ref[1, :, span] = im
        for order in range(1, 2 * ORDER - 1):
            re, im = (re * inv_x - im * inv_y) * float(order), (re * inv_y + im * inv_x) * float(order)
            h_ref[2 * order, :, span] = re
            h_ref[2 * order + 1, :, span] = im
    lane = lax.broadcasted_iota(jnp.int32, (LEAVES, 128), 1)
    table = jnp.zeros((LEAVES, 128), F32)
    half = ORDER // 2
    for first in (0, half):
        sums_re = [None] * half
        sums_im = [None] * half
        for group in range(len(groups)):
            span = slice(128 * group, 128 * group + 128)
            for k_ in range(ORDER):
                a_re = a_ref[k_ : k_ + 1, span]
                a_im = a_ref[ORDER + k_ : ORDER + k_ + 1, span]
                for m in range(half):
                    at = first + m + k_
                    h_re = h_ref[2 * at, :, span]
                    h_im = h_ref[2 * at + 1, :, span]
                    term_re = h_re * a_re - h_im * a_im
                    term_im = h_re * a_im + h_im * a_re
                    sums_re[m] = term_re if sums_re[m] is None else sums_re[m] + term_re
                    sums_im[m] = term_im if sums_im[m] is None else sums_im[m] + term_im
        for m in range(half):
            factor = 1.0 / math.factorial(first + m)
            table = jnp.where(lane == first + m, jnp.sum(sums_re[m], 1, keepdims=True) * factor, table)
            table = jnp.where(lane == 64 + first + m, jnp.sum(sums_im[m], 1, keepdims=True) * factor, table)
    out_ref[...] = table


def source_scale():
    row = row_of(24)
    which = jnp.where(row >= ORDER, row - ORDER, row)
    scale = jnp.zeros((24, 1), F32)
    for k_ in range(ORDER):
        scale = jnp.where(which == k_, (-1.0) ** (k_ + 1) / math.factorial(k_), scale)
    return scale


def leaf_field(nm_ref, m_ref, r1_ref, r2_ref, out_ref, h_ref, a_ref):
    info = position()
    leaf_even = info[3] == 0
    valid = info[4].astype(F32)
    n = row_of(LEAVES)
    ti = n >> 2
    tj = n & 3
    lane = lax.broadcasted_iota(jnp.int32, (LEAVES, 128), 1)
    near_mask = jnp.concatenate([nm_ref[i] for i in range(SIDE)], axis=0).astype(F32)
    near_shift = jnp.where(leaf_even, 4, -4)
    second = lane >= 48
    place = jnp.where(second, lane - 48, lane)
    k = place >> 4
    r = place & 15
    si = jnp.where(k == 0, r >> 2, jnp.where(k == 1, (r >> 2) - 4, (r >> 2) + 4))
    groups = []
    for column, lanes in ((jnp.where(second, near_shift, 0), 96), (-near_shift, 48)):
        dx = si - ti
        dy = (r & 3) + column - tj
        reach = jnp.maximum(jnp.abs(dx), jnp.abs(dy))
        weight = jnp.where(reach >= 3, 1.0, 0.0).astype(F32)
        for o, (a, b) in enumerate(cycle_steps):
            hit = jnp.logical_and(dx == a, dy == b)
            weight = jnp.where(hit, 1.0 - near_mask[:, o : o + 1], weight)
        inside = lane < lanes
        used = jnp.logical_and(reach >= 2, inside)
        groups.append(
            (
                jnp.where(used, dx.astype(F32), 1.0),
                jnp.where(used, dy.astype(F32), 1.0),
                jnp.where(inside, weight, 0.0),
            )
        )
    scale = source_scale()
    a_ref[:, 0:128] = (m_ref[...] + r1_ref[48:72, 0:128]) * scale
    a_ref[:, 128:256] = r2_ref[48:72, 0:128] * (valid * scale)
    translate(groups, h_ref, a_ref, out_ref)


def finish(part_ref, acc_ref, near_ref, f_ref, got_ref, out_ref, h_ref, a_ref, l_ref):
    info = position()
    n = row_of(LEAVES)
    ti = n >> 2
    tj = n & 3
    lane = lax.broadcasted_iota(jnp.int32, (LEAVES, 128), 1)
    bx = (lane >> 2) - info[0]
    by = (lane & 3) - info[1]
    remote = jnp.maximum(jnp.abs(bx), jnp.abs(by)) >= 2
    tx = jnp.where(remote, (bx * SIDE - ti).astype(F32) + 1.5, 1.0)
    ty = jnp.where(remote, (by * SIDE - tj).astype(F32) + 1.5, 1.0)
    weight = jnp.where(remote, 1.0, 0.0).astype(F32)
    a_ref[...] = (f_ref[...] + got_ref[...]) * source_scale()
    translate([(tx, ty, weight)], h_ref, a_ref, l_ref)
    local = l_ref[...] + near_ref[...]
    wx = own_rows(part_ref, 0)
    wy = own_rows(part_ref, 1)
    ox, oy = leaf_offsets()
    x = wx + ox
    y = wy + oy
    rows = lambda at: acc_ref[:, at, :] + acc_ref[:, at + 1, :] + acc_ref[:, at + 2, :]
    total = rows(0)
    sum_re = x * total - rows(3)
    sum_im = rows(6) - y * total
    p_re = jnp.ones_like(wx)
    p_im = jnp.zeros_like(wx)
    for m in range(ORDER):
        if m:
            p_re, p_im = p_re * wx - p_im * wy, p_re * wy + p_im * wx
        l_re = local[:, m : m + 1]
        l_im = local[:, 64 + m : 65 + m]
        sum_re = sum_re + (l_re * p_re - l_im * p_im)
        sum_im = sum_im + (l_re * p_im + l_im * p_re)
    sum_re = sum_re * (1.0 / TWO_PI)
    sum_im = sum_im * (1.0 / TWO_PI)
    for i in range(SIDE):
        out_ref[0, i] = sum_im[4 * i : 4 * i + 4]
        out_ref[1, i] = sum_re[4 * i : 4 * i + 4]


V = pl.BlockSpec(memory_space=pltpu.VMEM)
S = pl.BlockSpec(memory_space=pltpu.SMEM)
A = pl.BlockSpec(memory_space=pl.ANY)


def shaped(*shape, dtype=F32):
    return jax.ShapeDtypeStruct(shape, dtype)


def call(kernel, name, in_specs, outs, scratch, cost, aliases=None):
    return pl.pallas_call(
        kernel,
        out_shape=outs,
        in_specs=in_specs,
        out_specs=jax.tree.map(lambda unused: V, outs),
        scratch_shapes=scratch,
        name=name,
        input_output_aliases=aliases or {},
        cost_estimate=pl.CostEstimate(flops=cost, bytes_accessed=1 << 20, transcendentals=0),
        compiler_params=pltpu.CompilerParams(vmem_limit_bytes=VMEM_LIMIT),
    )


def features_out(count):
    return [shaped(count, SIZE, FEATURES, dtype=BF16), shaped(count, 16, SIZE, dtype=BF16)]


def stages(with_target):
    out = [pltpu.VMEM((LEAVES, FEATURES, SIZE), F32), pltpu.VMEM((LEAVES, 16, SIZE), F32)]
    return ([pltpu.VMEM((LEAVES, FEATURES, SIZE), F32)] if with_target else []) + out


SMALL = 4_000_000
PAIR = 400_000_000


def run_direct(name, tables, mask, feats, acc, by_side=False, extra=None, ins=(), outs=(), scratch=()):
    zero = acc is None
    args = [mask, *feats] + ([] if zero else [acc]) + list(ins)
    got = call(
        functools.partial(direct, tables, by_side, zero, extra, len(ins)),
        name,
        [V] * len(args),
        [shaped(LEAVES, 16, SIZE), *outs],
        list(scratch),
        PAIR * (1 if by_side else tables.shape[0]) * tables.shape[1],
        {} if zero else {4: 0},
    )(*args)
    return got if outs else got[0]


def far_scratch(width):
    return [pltpu.VMEM((4 * ORDER - 2, LEAVES, width), F32), pltpu.VMEM((24, width), F32)]


def body(particles, near_mask):
    turned = near_mask.transpose(1, 2, 0)
    t0, s0, w0, m0, f0, send_a, send_b = call(
        prepare_own,
        "prepare_own",
        [V],
        [shaped(LEAVES, FEATURES, SIZE, dtype=BF16), *features_out(LEAVES), shaped(24, 128), shaped(24, 128)]
        + [shaped(SLAB_ROWS, SIZE)] * 2,
        stages(True),
        SMALL,
    )(particles)
    recv_a = swap(send_a, "core")
    recv_b = swap(send_b, "slab")
    own = pair_table("own")
    feats = (t0, s0, w0)
    acc, mask = run_direct(
        "direct_own_0", own[None, :98], turned, feats, None, outs=[shaped(17, LEAVES, 1, SIZE)]
    )
    m1, f1, send_near, send_far = call(
        pack_slab,
        "pack_slab",
        [V, V, V, V, V, A],
        [shaped(24, 128), shaped(24, 128), shaped(LEAF_ROWS, SIZE), shaped(72, SIZE)],
        [],
        SMALL,
    )(particles, recv_a, recv_b, m0, f0, acc)
    send_near, acc = lax.optimization_barrier((send_near, acc))
    recv_near = swap(send_near, "leaf_near")
    built = dict(outs=features_out(LEAVES), scratch=stages(False))
    acc, s1, w1 = run_direct(
        "direct_own_1", own[None, 98:147], mask, feats, acc, extra=slab_halo, ins=(recv_a, recv_b), **built
    )
    f2, send_far = call(
        pack_near, "pack_near", [V, V, V, A], [shaped(24, 128), shaped(LEAF_ROWS, SIZE)], [], SMALL
    )(recv_near, f1, send_far, acc)
    send_far, acc = lax.optimization_barrier((send_far, acc))
    recv_far = swap(send_far, "leaf_far")
    acc, s2, w2 = run_direct(
        "direct_own_2", own[None, 147:], mask, feats, acc, extra=near_halo, ins=(recv_near,), **built
    )
    recv_far, acc = lax.optimization_barrier((recv_far, acc))
    f3 = f2 + recv_far[72:96, 0:128]
    f3, acc = lax.optimization_barrier((f3, acc))
    got = swap(f3, "z_near")
    acc, s3, w3 = run_direct(
        "direct_slab",
        pair_table("slab").reshape(2, 42, 3),
        mask,
        (t0, s1, w1),
        acc,
        extra=far_halo,
        ins=(recv_far,),
        **built,
    )
    got, acc = lax.optimization_barrier((got, acc))
    f4 = f3 + got
    f4, acc = lax.optimization_barrier((f4, acc))
    got = swap(f4, "z_far")
    right = pair_table("leaf", True)
    left = pair_table("leaf", False)
    near_pairs = np.stack([right, left])
    far_pairs = np.stack([left, right])
    acc, local = run_direct(
        "direct_leaf_near",
        near_pairs,
        mask,
        (t0, s2, w2),
        acc,
        True,
        extra=leaf_field,
        ins=(turned, m1, recv_near, recv_far),
        outs=[shaped(LEAVES, 128)],
        scratch=far_scratch(256),
    )
    got, acc = lax.optimization_barrier((got, acc))
    f5 = f4 + got
    f5, acc = lax.optimization_barrier((f5, acc))
    got = swap(f5, "x_near")
    acc = run_direct("direct_leaf_far_0", far_pairs[:, :30], mask, (t0, s3, w3), acc, "far")
    got, acc = lax.optimization_barrier((got, acc))
    f6 = f5 + got
    f6, acc = lax.optimization_barrier((f6, acc))
    got = swap(f6, "x_far")
    acc = run_direct("direct_leaf_far_1", far_pairs[:, 30:], mask, (t0, s3, w3), acc, "far")
    got, acc = lax.optimization_barrier((got, acc))
    return call(
        finish,
        "finish",
        [V] * 5,
        shaped(2, SIDE, SIDE, SIZE),
        far_scratch(128) + [pltpu.VMEM((LEAVES, 128), F32)],
        SMALL,
    )(particles, acc, local, f6, got)


def solution(mesh):
    finer = Mesh(mesh.devices.reshape(4, 4, 2, mesh.shape["leaf"]), ALL)
    in_specs = (P(None, SLAB, "leaf", None), P(None, SLAB, "leaf"))
    out_specs = P(None, SLAB, "leaf", None)
    run = jax.shard_map(body, mesh=finer, in_specs=in_specs, out_specs=out_specs, check_vma=False)

    def whole(particles, near_mask):
        with jax.sharding.use_abstract_mesh(mesh.abstract_mesh):
            return run(particles, near_mask)

    return run
```

```python
import functools
import math

import jax
import jax.numpy as jnp
import numpy as np
from jax import lax
from jax.experimental import pallas as pl
from jax.experimental.pallas import tpu as pltpu
from jax.sharding import Mesh
from jax.sharding import PartitionSpec as P

ORDER = 10
SIDE = 4
LEAVES = 16
SIZE = 256
FEATURES = 32
DELTA_SQUARED = 0.0025
TWO_PI = 2.0 * math.pi
SLAB = ("slab_0", "slab_1", "slab_2")
ALL = ("slab_0", "slab_1", "slab_2", "leaf")
F32 = jnp.float32
BF16 = jnp.bfloat16
VMEM_LIMIT = 6 << 20
cycle_steps = [(a, b) for a in range(-2, 3) for b in range(-2, 3) if max(abs(a), abs(b)) == 2]
near_steps = [(a, b) for a in range(-2, 3) for b in range(-2, 3)]


def exchange_pairs(partner):
    pairs = []
    for x in range(4):
        for z in range(4):
            for c in range(2):
                for y in range(4):
                    other = partner(x, z, c, y)
                    if other is not None:
                        a, b, d, e = other
                        pairs.append((((x * 4 + z) * 2 + c) * 4 + y, ((a * 4 + b) * 2 + d) * 4 + e))
    return pairs


def inner_slab(slab):
    return jnp.logical_and(slab > 0, slab < 31).astype(F32)


def slab_between_chips(x, z, c, y):
    slab = (x * 4 + z) * 2 + c
    other = (slab + 1 if c == 1 else slab - 1) % 32
    return (other // 8, (other // 2) % 4, other % 2, y)


def near_side(k):
    return k ^ 1


def far_side(k):
    return 3 - k


SWAPS = {
    "core": exchange_pairs(lambda x, z, c, y: (x, z, 1 - c, y)),
    "slab": exchange_pairs(slab_between_chips),
    "leaf_near": exchange_pairs(lambda x, z, c, y: (x, z, c, near_side(y))),
    "leaf_far": exchange_pairs(lambda x, z, c, y: (x, z, c, far_side(y))),
    "z_near": exchange_pairs(lambda x, z, c, y: (x, near_side(z), c, y)),
    "z_far": exchange_pairs(lambda x, z, c, y: (x, far_side(z), c, y)),
    "x_near": exchange_pairs(lambda x, z, c, y: (near_side(x), z, c, y)),
    "x_far": exchange_pairs(lambda x, z, c, y: (far_side(x), z, c, y)),
}


def swap(value, name):
    return lax.ppermute(value, ALL, SWAPS[name])


def pieces(value, count):
    parts = []
    for unused in range(count):
        part = value.astype(BF16).astype(F32)
        parts.append(part)
        value = value - part
    return parts


def build_features(wx, wy, g, ox, oy, stage_t, stage_s, stage_w, t_ref, s_ref, w_ref, first, with_target):
    count = wx.shape[0]
    one = jnp.ones_like(wx)
    zero = jnp.zeros_like(wx)
    coarse_x = jnp.round(wx * 32.0) * (1.0 / 32.0)
    coarse_y = jnp.round(wy * 32.0) * (1.0 / 32.0)
    fine_x = wx - coarse_x
    fine_y = wy - coarse_y
    big_x = coarse_x + ox
    big_y = coarse_y + oy
    big = pieces(big_x * big_x + big_y * big_y, 2)
    rest = 2.0 * (big_x * fine_x + big_y * fine_y) + fine_x * fine_x + fine_y * fine_y
    px = pieces(fine_x, 2)
    py = pieces(fine_y, 2)
    if with_target:
        rows = [big_x, big_y, big[0], big[1], one, one, zero, zero]
        rows += [big_x, big_x, big_y, big_y, px[0], px[1], py[0], py[1]]
        rows += [px[0], px[0], px[1], py[0], py[0], py[1]]
        rows += pieces(rest + DELTA_SQUARED, 3) + [one, one, one]
        rows += [zero] * (FEATURES - len(rows))
        for f, row in enumerate(rows):
            stage_t[:count, f, :] = row
    twice = lambda v: -2.0 * v
    rows = [twice(big_x), twice(big_y), one, one, big[0], big[1], zero, zero]
    rows += [twice(px[0]), twice(px[1]), twice(py[0]), twice(py[1])]
    rows += [twice(big_x), twice(big_x), twice(big_y), twice(big_y)]
    rows += [twice(px[0]), twice(px[1]), twice(px[0]), twice(py[0]), twice(py[1]), twice(py[0])]
    rows += [one, one, one] + pieces(rest, 3)
    rows += [zero] * (FEATURES - len(rows))
    for f, row in enumerate(rows):
        stage_s[:count, f, :] = row
    rows = pieces(g, 3) + pieces(g * (wx + ox), 3) + pieces(g * (wy + oy), 3)
    rows += [zero] * (16 - len(rows))
    for f, row in enumerate(rows):
        stage_w[:count, f, :] = row
    for n in range(count):
        if with_target:
            t_ref[first + n] = stage_t[n].astype(BF16)
        s_ref[first + n] = jnp.transpose(stage_s[n]).astype(BF16)
        w_ref[first + n] = stage_w[n].astype(BF16)


def power_list(base_re, base_im, count):
    re = [jnp.ones_like(base_re)]
    im = [jnp.zeros_like(base_im)]
    for unused in range(1, count):
        a, b = re[-1], im[-1]
        re.append(a * base_re - b * base_im)
        im.append(a * base_im + b * base_re)
    return re, im


def row_of(n):
    return lax.broadcasted_iota(jnp.int32, (n, 1), 0)


def leaf_offsets():
    n = row_of(LEAVES)
    ox = (n >> 2).astype(F32) - 1.5
    oy = (n & 3).astype(F32) - 1.5
    return ox, oy


def own_rows(ref, part):
    return jnp.concatenate([ref[part, i] for i in range(SIDE)], axis=0)


def position():
    slab = lax.axis_index(SLAB)
    leaf = lax.axis_index("leaf")
    between = jnp.logical_and(leaf > 0, leaf < 3).astype(jnp.int32)
    return slab, leaf, slab & 1, leaf & 1, between


SLAB_ROWS = 72
LEAF_ROWS = 96


def prepare_own(part_ref, t_ref, s_ref, w_ref, m_ref, f_ref, a_ref, b_ref, stage_t, stage_s, stage_w):
    info = position()
    wx = own_rows(part_ref, 0)
    wy = own_rows(part_ref, 1)
    g = own_rows(part_ref, 2)
    ox, oy = leaf_offsets()
    lane = lax.broadcasted_iota(jnp.int32, (LEAVES, 128), 1)
    table = jnp.zeros((LEAVES, 128), F32)
    for start, base_re, base_im in ((0, wx, wy), (32, wx + ox, wy + oy)):
        re, im = power_list(base_re, base_im, ORDER)
        for k in range(ORDER):
            table = jnp.where(lane == start + k, jnp.sum(g * re[k], 1, keepdims=True), table)
            if k:
                table = jnp.where(lane == start + ORDER + k, jnp.sum(g * im[k], 1, keepdims=True), table)
    turned = jnp.transpose(table)
    leaf_part = jnp.concatenate([turned[0:24], jnp.zeros((24, 112), F32)], axis=1)
    block_part = jnp.sum(turned[32:56], axis=1, keepdims=True)
    me = info[0] * 4 + info[1]
    wide = lax.broadcasted_iota(jnp.int32, (24, 128), 1)
    block_row = jnp.where(wide == me, block_part, 0.0)
    m_ref[...] = leaf_part
    f_ref[...] = block_row
    even = info[2] == 0
    for c in range(3):
        first = jnp.concatenate([part_ref[c, 0], part_ref[c, 1]], axis=0)
        last = jnp.concatenate([part_ref[c, 2], part_ref[c, 3]], axis=0)
        a_ref[8 * c : 8 * c + 8] = jnp.where(even, last, first)
        b_ref[8 * c : 8 * c + 8] = jnp.where(even, first, last)
    none = jnp.zeros((24, 128), F32)
    for ref in (a_ref, b_ref):
        ref[24:48, 0:128] = leaf_part
        ref[24:48, 128:256] = none
        ref[48:72, 0:128] = block_row
        ref[48:72, 128:256] = none
    build_features(wx, wy, g, ox, oy, stage_t, stage_s, stage_w, t_ref, s_ref, w_ref, 0, True)


def pack_slab(part_ref, ra_ref, rb_ref, m_ref, f_ref, after_ref, m_out, f_out, near_ref, far_ref):
    info = position()
    even = info[2] == 0
    leaf_even = info[3] == 0
    inner = inner_slab(info[0])
    for c in range(3):
        ra = ra_ref[8 * c : 8 * c + 8]
        rb = rb_ref[8 * c : 8 * c + 8]
        if c == 2:
            rb = rb * inner
        before = jnp.where(even, rb, ra)
        after = jnp.where(even, ra, rb)
        rows = [before[0:4], before[4:8]] + [part_ref[c, i] for i in range(SIDE)] + [after[0:4], after[4:8]]
        left = jnp.concatenate([r[0:2] for r in rows], axis=0)
        right = jnp.concatenate([r[2:4] for r in rows], axis=0)
        near_ref[16 * c : 16 * c + 16] = jnp.where(leaf_even, right, left)
        far_ref[16 * c : 16 * c + 16] = jnp.where(leaf_even, left, right)
    ma = ra_ref[24:48, 0:16]
    mb = rb_ref[24:48, 0:16] * inner
    window = jnp.concatenate(
        [m_ref[:, 0:16], jnp.where(even, mb, ma), jnp.where(even, ma, mb), jnp.zeros((24, 80), F32)], axis=1
    )
    blocks = f_ref[...] + ra_ref[48:72, 0:128]
    m_out[...] = window
    f_out[...] = blocks
    none = jnp.zeros((24, 128), F32)
    near_ref[48:72, 0:128] = jnp.concatenate([none[:, 0:48], window[:, 0:48], none[:, 0:32]], axis=1)
    near_ref[48:72, 128:256] = none
    far_ref[48:72, 0:128] = window
    far_ref[48:72, 128:256] = none
    near_ref[72:96, 0:128] = blocks
    near_ref[72:96, 128:256] = none


def slab_halo(ra_ref, rb_ref, s_ref, w_ref, stage_s, stage_w):
    even = position()[2] == 0
    inner = inner_slab(position()[0])
    halo = []
    for c in range(3):
        ra = ra_ref[8 * c : 8 * c + 8]
        rb = rb_ref[8 * c : 8 * c + 8]
        if c == 2:
            rb = rb * inner
        halo.append(jnp.concatenate([jnp.where(even, rb, ra), jnp.where(even, ra, rb)], axis=0))
    n = row_of(LEAVES)
    i = (n >> 2) - 2
    ox = jnp.where(i >= 0, i + 4, i).astype(F32) - 1.5
    oy = (n & 3).astype(F32) - 1.5
    build_features(halo[0], halo[1], halo[2], ox, oy, None, stage_s, stage_w, None, s_ref, w_ref, 0, False)


def leaf_halo(which, r_ref, s_ref, w_ref, stage_s, stage_w):
    info = position()
    leaf_even = info[3] == 0
    to_right = leaf_even if which == 0 else jnp.logical_not(leaf_even)
    valid = jnp.float32(1.0) if which == 0 else info[4].astype(F32)
    n = row_of(LEAVES)
    ox = (n >> 1).astype(F32) - 3.5
    side = (n & 1).astype(F32)
    oy = jnp.where(to_right, side + 4.0, side - 2.0) - 1.5
    build_features(
        r_ref[0:16], r_ref[16:32], r_ref[32:48] * valid, ox, oy, None, stage_s, stage_w, None, s_ref, w_ref, 0, False
    )


def near_halo(r_ref, s_ref, w_ref, stage_s, stage_w):
    leaf_halo(0, r_ref, s_ref, w_ref, stage_s, stage_w)


def far_halo(r_ref, s_ref, w_ref, stage_s, stage_w):
    leaf_halo(1, r_ref, s_ref, w_ref, stage_s, stage_w)


def pack_near(r_ref, f_ref, send_ref, after_ref, f_out, send_out):
    blocks = f_ref[...] + r_ref[72:96, 0:128]
    f_out[...] = blocks
    send_out[0:72] = send_ref[...]
    send_out[72:96, 0:128] = blocks
    send_out[72:96, 128:256] = jnp.zeros((24, 128), F32)


def chosen(index, values):
    if all(v == values[0] for v in values):
        return values[0]
    out = values[-1]
    for n in range(len(values) - 2, -1, -1):
        out = jnp.where(index == n, values[n], out)
    return out


def pairs(tables, mask_ref, t_ref, s_ref, w_ref, acc_ref, index, unused):
    for n in range(tables.shape[1]):
        t, s, o = (chosen(index, [int(v) for v in tables[:, n, c]]) for c in range(3))
        distance = jnp.dot(s_ref[s], t_ref[t], preferred_element_type=F32)
        kernel = 1.0 / distance
        high = kernel.astype(BF16)
        low = (kernel - high.astype(F32)).astype(BF16)
        w = w_ref[s]
        total = jnp.dot(w, high, preferred_element_type=F32) + jnp.dot(w, low, preferred_element_type=F32)
        if isinstance(o, int) and o == 16:
            acc_ref[t] = acc_ref[t] + total
        else:
            acc_ref[t] = acc_ref[t] + mask_ref[o, t] * total
    return 0


def direct_sides(near, far, extra, extra_in, mask_ref, t_ref, s2_ref, w2_ref, s3_ref, w3_ref, acc_in, *refs):
    acc_ref = refs[extra_in]
    acc_ref[...] = acc_in[...]
    parity = position()[3]
    pairs(near, mask_ref, t_ref, s2_ref, w2_ref, acc_ref, parity, 0)
    if extra is not None:
        extra(*refs[:extra_in], *refs[extra_in + 1 :])

    @pl.when(position()[4] == 1)
    def _():
        pairs(far, mask_ref, t_ref, s3_ref, w3_ref, acc_ref, parity, 0)


def direct(tables, zero, extra, extra_in, mask_ref, t_ref, s_ref, w_ref, *refs):
    if zero:
        acc_ref, rows_ref = refs
        acc_ref[...] = jnp.zeros_like(acc_ref)
        near_mask = jnp.concatenate([mask_ref[i] for i in range(SIDE)], axis=0).astype(F32)
        for o in range(16):
            rows_ref[o, :, 0, :] = jnp.broadcast_to(near_mask[:, o : o + 1], (LEAVES, SIZE))
        rows_ref[16, :, 0, :] = jnp.ones((LEAVES, SIZE), F32)
        mask_ref = rows_ref
    else:
        acc_ref = refs[extra_in + 1]
        acc_ref[...] = refs[0][...]
        others = refs[1 : extra_in + 1] + refs[extra_in + 2 :]
    step = functools.partial(pairs, tables, mask_ref, t_ref, s_ref, w_ref, acc_ref)
    if tables.shape[0] == 1:
        step(0, 0)
    else:
        lax.fori_loop(0, tables.shape[0], step, 0)
    if extra is not None:
        extra(*others)


def pair_table(kind, to_right=False):
    out = []
    for t in range(LEAVES):
        i, j = divmod(t, SIDE)
        for a, b in near_steps:
            o = cycle_steps.index((a, b)) if max(abs(a), abs(b)) == 2 else 16
            si, sj = i + a, j + b
            in_row, in_column = 0 <= si < SIDE, 0 <= sj < SIDE
            if kind == "own" and in_row and in_column:
                out.append((t, si * SIDE + sj, o))
            if kind == "slab" and not in_row and in_column:
                out.append((t, ((si + 2) if si < 0 else (si - 2)) * SIDE + sj, o))
            if kind == "leaf" and not in_column and (sj >= SIDE) == to_right:
                out.append((t, (si + 2) * 2 + (sj - SIDE if to_right else sj + 2), o))
    return np.array(out, np.int32)


def translate(groups, h_ref, a_ref, out_ref):
    for group, (tx, ty, weight) in enumerate(groups):
        span = slice(128 * group, 128 * group + 128)
        square = tx * tx + ty * ty
        inv_x = tx / square
        inv_y = -ty / square
        re = weight * inv_x
        im = weight * inv_y
        h_ref[0, :, span] = re
        h_ref[1, :, span] = im
        for order in range(1, 2 * ORDER - 1):
            re, im = (re * inv_x - im * inv_y) * float(order), (re * inv_y + im * inv_x) * float(order)
            h_ref[2 * order, :, span] = re
            h_ref[2 * order + 1, :, span] = im
    lane = lax.broadcasted_iota(jnp.int32, (LEAVES, 128), 1)
    table = jnp.zeros((LEAVES, 128), F32)
    half = ORDER // 2
    for first in (0, half):
        sums_re = [None] * half
        sums_im = [None] * half
        for group in range(len(groups)):
            span = slice(128 * group, 128 * group + 128)
            for k_ in range(ORDER):
                a_re = a_ref[k_ : k_ + 1, span]
                a_im = a_ref[ORDER + k_ : ORDER + k_ + 1, span]
                for m in range(half):
                    at = first + m + k_
                    h_re = h_ref[2 * at, :, span]
                    h_im = h_ref[2 * at + 1, :, span]
                    term_re = h_re * a_re - h_im * a_im
                    term_im = h_re * a_im + h_im * a_re
                    sums_re[m] = term_re if sums_re[m] is None else sums_re[m] + term_re
                    sums_im[m] = term_im if sums_im[m] is None else sums_im[m] + term_im
        for m in range(half):
            factor = 1.0 / math.factorial(first + m)
            table = jnp.where(lane == first + m, jnp.sum(sums_re[m], 1, keepdims=True) * factor, table)
            table = jnp.where(lane == 64 + first + m, jnp.sum(sums_im[m], 1, keepdims=True) * factor, table)
    out_ref[...] = table


def source_scale():
    row = row_of(24)
    which = jnp.where(row >= ORDER, row - ORDER, row)
    scale = jnp.zeros((24, 1), F32)
    for k_ in range(ORDER):
        scale = jnp.where(which == k_, (-1.0) ** (k_ + 1) / math.factorial(k_), scale)
    return scale


def leaf_field(nm_ref, m_ref, r1_ref, r2_ref, out_ref, h_ref, a_ref):
    info = position()
    leaf_even = info[3] == 0
    valid = info[4].astype(F32)
    n = row_of(LEAVES)
    ti = n >> 2
    tj = n & 3
    lane = lax.broadcasted_iota(jnp.int32, (LEAVES, 128), 1)
    near_mask = jnp.concatenate([nm_ref[i] for i in range(SIDE)], axis=0).astype(F32)
    near_shift = jnp.where(leaf_even, 4, -4)
    second = lane >= 48
    place = jnp.where(second, lane - 48, lane)
    k = place >> 4
    r = place & 15
    si = jnp.where(k == 0, r >> 2, jnp.where(k == 1, (r >> 2) - 4, (r >> 2) + 4))
    groups = []
    for column, lanes in ((jnp.where(second, near_shift, 0), 96), (-near_shift, 48)):
        dx = si - ti
        dy = (r & 3) + column - tj
        reach = jnp.maximum(jnp.abs(dx), jnp.abs(dy))
        weight = jnp.where(reach >= 3, 1.0, 0.0).astype(F32)
        for o, (a, b) in enumerate(cycle_steps):
            hit = jnp.logical_and(dx == a, dy == b)
            weight = jnp.where(hit, 1.0 - near_mask[:, o : o + 1], weight)
        inside = lane < lanes
        used = jnp.logical_and(reach >= 2, inside)
        groups.append(
            (
                jnp.where(used, dx.astype(F32), 1.0),
                jnp.where(used, dy.astype(F32), 1.0),
                jnp.where(inside, weight, 0.0),
            )
        )
    scale = source_scale()
    a_ref[:, 0:128] = (m_ref[...] + r1_ref[48:72, 0:128]) * scale
    a_ref[:, 128:256] = r2_ref[48:72, 0:128] * (valid * scale)
    translate(groups, h_ref, a_ref, out_ref)


def finish(part_ref, acc_ref, near_ref, f_ref, got_ref, out_ref, h_ref, a_ref, l_ref):
    info = position()
    n = row_of(LEAVES)
    ti = n >> 2
    tj = n & 3
    lane = lax.broadcasted_iota(jnp.int32, (LEAVES, 128), 1)
    bx = (lane >> 2) - info[0]
    by = (lane & 3) - info[1]
    remote = jnp.maximum(jnp.abs(bx), jnp.abs(by)) >= 2
    tx = jnp.where(remote, (bx * SIDE - ti).astype(F32) + 1.5, 1.0)
    ty = jnp.where(remote, (by * SIDE - tj).astype(F32) + 1.5, 1.0)
    weight = jnp.where(remote, 1.0, 0.0).astype(F32)
    a_ref[...] = (f_ref[...] + got_ref[...]) * source_scale()
    translate([(tx, ty, weight)], h_ref, a_ref, l_ref)
    local = l_ref[...] + near_ref[...]
    wx = own_rows(part_ref, 0)
    wy = own_rows(part_ref, 1)
    ox, oy = leaf_offsets()
    x = wx + ox
    y = wy + oy
    rows = lambda at: acc_ref[:, at, :] + acc_ref[:, at + 1, :] + acc_ref[:, at + 2, :]
    total = rows(0)
    sum_re = x * total - rows(3)
    sum_im = rows(6) - y * total
    p_re = jnp.ones_like(wx)
    p_im = jnp.zeros_like(wx)
    for m in range(ORDER):
        if m:
            p_re, p_im = p_re * wx - p_im * wy, p_re * wy + p_im * wx
        l_re = local[:, m : m + 1]
        l_im = local[:, 64 + m : 65 + m]
        sum_re = sum_re + (l_re * p_re - l_im * p_im)
        sum_im = sum_im + (l_re * p_im + l_im * p_re)
    sum_re = sum_re * (1.0 / TWO_PI)
    sum_im = sum_im * (1.0 / TWO_PI)
    for i in range(SIDE):
        out_ref[0, i] = sum_im[4 * i : 4 * i + 4]
        out_ref[1, i] = sum_re[4 * i : 4 * i + 4]


V = pl.BlockSpec(memory_space=pltpu.VMEM)
S = pl.BlockSpec(memory_space=pltpu.SMEM)
A = pl.BlockSpec(memory_space=pl.ANY)


def shaped(*shape, dtype=F32):
    return jax.ShapeDtypeStruct(shape, dtype)


def call(kernel, name, in_specs, outs, scratch, cost, aliases=None):
    return pl.pallas_call(
        kernel,
        out_shape=outs,
        in_specs=in_specs,
        out_specs=jax.tree.map(lambda unused: V, outs),
        scratch_shapes=scratch,
        name=name,
        input_output_aliases=aliases or {},
        cost_estimate=pl.CostEstimate(flops=cost, bytes_accessed=1 << 20, transcendentals=0),
        compiler_params=pltpu.CompilerParams(vmem_limit_bytes=VMEM_LIMIT),
    )


def features_out(count):
    return [shaped(count, SIZE, FEATURES, dtype=BF16), shaped(count, 16, SIZE, dtype=BF16)]


def stages(with_target):
    out = [pltpu.VMEM((LEAVES, FEATURES, SIZE), F32), pltpu.VMEM((LEAVES, 16, SIZE), F32)]
    return ([pltpu.VMEM((LEAVES, FEATURES, SIZE), F32)] if with_target else []) + out


SMALL = 4_000_000
PAIR = 400_000_000


def run_direct(name, tables, mask, feats, acc, extra=None, ins=(), outs=(), scratch=()):
    zero = acc is None
    args = [mask, *feats] + ([] if zero else [acc]) + list(ins)
    got = call(
        functools.partial(direct, tables, zero, extra, len(ins)),
        name,
        [V] * len(args),
        [shaped(LEAVES, 16, SIZE), *outs],
        list(scratch),
        PAIR * tables.shape[0] * tables.shape[1],
        {} if zero else {4: 0},
    )(*args)
    return got if outs else got[0]


def run_sides(name, near, far, args, extra=None, ins=(), outs=(), scratch=()):
    args = [*args, *ins]
    got = call(
        functools.partial(direct_sides, near, far, extra, len(ins)),
        name,
        [V] * len(args),
        [shaped(LEAVES, 16, SIZE), *outs],
        list(scratch),
        PAIR * 60,
        {6: 0},
    )(*args)
    return got if outs else got[0]


def far_scratch(width):
    return [pltpu.VMEM((4 * ORDER - 2, LEAVES, width), F32), pltpu.VMEM((24, width), F32)]


def body(particles, near_mask):
    turned = near_mask.transpose(1, 2, 0)
    t0, s0, w0, m0, f0, send_a, send_b = call(
        prepare_own,
        "prepare_own",
        [V],
        [shaped(LEAVES, FEATURES, SIZE, dtype=BF16), *features_out(LEAVES), shaped(24, 128), shaped(24, 128)]
        + [shaped(SLAB_ROWS, SIZE)] * 2,
        stages(True),
        SMALL,
    )(particles)
    recv_a = swap(send_a, "core")
    recv_b = swap(send_b, "slab")
    own = pair_table("own")
    feats = (t0, s0, w0)
    acc, mask = run_direct(
        "direct_own_0", own[:98].reshape(2, 49, 3), turned, feats, None, outs=[shaped(17, LEAVES, 1, SIZE)]
    )
    m1, f1, send_near, send_far = call(
        pack_slab,
        "pack_slab",
        [V, V, V, V, V, A],
        [shaped(24, 128), shaped(24, 128), shaped(LEAF_ROWS, SIZE), shaped(72, SIZE)],
        [],
        SMALL,
    )(particles, recv_a, recv_b, m0, f0, acc)
    send_near, acc = lax.optimization_barrier((send_near, acc))
    recv_near = swap(send_near, "leaf_near")
    built = dict(outs=features_out(LEAVES), scratch=stages(False))
    acc, s1, w1 = run_direct(
        "direct_own_1", own[None, 98:147], mask, feats, acc, extra=slab_halo, ins=(recv_a, recv_b), **built
    )
    f2, send_far = call(
        pack_near, "pack_near", [V, V, V, A], [shaped(24, 128), shaped(LEAF_ROWS, SIZE)], [], SMALL
    )(recv_near, f1, send_far, acc)
    send_far, acc = lax.optimization_barrier((send_far, acc))
    recv_far = swap(send_far, "leaf_far")
    acc, s2, w2 = run_direct(
        "direct_own_2", own[None, 147:], mask, feats, acc, extra=near_halo, ins=(recv_near,), **built
    )
    recv_far, acc = lax.optimization_barrier((recv_far, acc))
    f3 = f2 + recv_far[72:96, 0:128]
    f3, acc = lax.optimization_barrier((f3, acc))
    got = swap(f3, "z_near")
    slab_pairs = pair_table("slab").reshape(2, 1, 42, 3)
    acc, s3, w3 = run_direct(
        "direct_slab_0", slab_pairs[0], mask, (t0, s1, w1), acc, extra=far_halo, ins=(recv_far,), **built
    )
    got, acc = lax.optimization_barrier((got, acc))
    f4 = f3 + got
    f4, acc = lax.optimization_barrier((f4, acc))
    got = swap(f4, "z_far")
    acc = run_direct("direct_slab_1", slab_pairs[1], mask, (t0, s1, w1), acc)
    got, acc = lax.optimization_barrier((got, acc))
    f5 = f4 + got
    f5, acc = lax.optimization_barrier((f5, acc))
    got = swap(f5, "x_near")
    right = pair_table("leaf", True)
    left = pair_table("leaf", False)
    near_pairs = np.stack([right, left])
    far_pairs = np.stack([left, right])
    shared = (mask, t0, s2, w2, s3, w3)
    acc, local = run_sides(
        "direct_sides_0",
        near_pairs[:, :30],
        far_pairs[:, :30],
        (*shared, acc),
        extra=leaf_field,
        ins=(turned, m1, recv_near, recv_far),
        outs=[shaped(LEAVES, 128)],
        scratch=far_scratch(256),
    )
    got, acc = lax.optimization_barrier((got, acc))
    f6 = f5 + got
    f6, acc = lax.optimization_barrier((f6, acc))
    got = swap(f6, "x_far")
    acc = run_sides("direct_sides_1", near_pairs[:, 30:], far_pairs[:, 30:], (*shared, acc))
    got, acc = lax.optimization_barrier((got, acc))
    return call(
        finish,
        "finish",
        [V] * 5,
        shaped(2, SIDE, SIDE, SIZE),
        far_scratch(128) + [pltpu.VMEM((LEAVES, 128), F32)],
        SMALL,
    )(particles, acc, local, f6, got)


def solution(mesh):
    finer = Mesh(mesh.devices.reshape(4, 4, 2, mesh.shape["leaf"]), ALL)
    in_specs = (P(None, SLAB, "leaf", None), P(None, SLAB, "leaf"))
    out_specs = P(None, SLAB, "leaf", None)
    run = jax.shard_map(body, mesh=finer, in_specs=in_specs, out_specs=out_specs, check_vma=False)

    def whole(particles, near_mask):
        with jax.sharding.use_abstract_mesh(mesh.abstract_mesh):
            return run(particles, near_mask)

    return run
```

```python
import functools
import math

import jax
import jax.numpy as jnp
import numpy as np
from jax import lax
from jax.experimental import pallas as pl
from jax.experimental.pallas import tpu as pltpu
from jax.sharding import Mesh
from jax.sharding import PartitionSpec as P

ORDER = 10
SIDE = 4
LEAVES = 16
SIZE = 256
FEATURES = 32
DELTA_SQUARED = 0.0025
TWO_PI = 2.0 * math.pi
SLAB = ("slab_0", "slab_1", "slab_2")
ALL = ("slab_0", "slab_1", "slab_2", "leaf")
F32 = jnp.float32
BF16 = jnp.bfloat16
VMEM_LIMIT = 6 << 20
cycle_steps = [(a, b) for a in range(-2, 3) for b in range(-2, 3) if max(abs(a), abs(b)) == 2]
near_steps = [(a, b) for a in range(-2, 3) for b in range(-2, 3)]


def exchange_pairs(partner):
    pairs = []
    for x in range(4):
        for z in range(4):
            for c in range(2):
                for y in range(4):
                    other = partner(x, z, c, y)
                    if other is not None:
                        a, b, d, e = other
                        pairs.append((((x * 4 + z) * 2 + c) * 4 + y, ((a * 4 + b) * 2 + d) * 4 + e))
    return pairs


def inner_slab(slab):
    return jnp.logical_and(slab > 0, slab < 31).astype(F32)


def slab_between_chips(x, z, c, y):
    slab = (x * 4 + z) * 2 + c
    other = (slab + 1 if c == 1 else slab - 1) % 32
    return (other // 8, (other // 2) % 4, other % 2, y)


def near_side(k):
    return k ^ 1


def far_side(k):
    return 3 - k


SWAPS = {
    "core": exchange_pairs(lambda x, z, c, y: (x, z, 1 - c, y)),
    "slab": exchange_pairs(slab_between_chips),
    "leaf_near": exchange_pairs(lambda x, z, c, y: (x, z, c, near_side(y))),
    "leaf_far": exchange_pairs(lambda x, z, c, y: (x, z, c, far_side(y))),
    "z_near": exchange_pairs(lambda x, z, c, y: (x, near_side(z), c, y)),
    "z_far": exchange_pairs(lambda x, z, c, y: (x, far_side(z), c, y)),
    "x_near": exchange_pairs(lambda x, z, c, y: (near_side(x), z, c, y)),
    "x_far": exchange_pairs(lambda x, z, c, y: (far_side(x), z, c, y)),
}


def swap(value, name):
    return lax.ppermute(value, ALL, SWAPS[name])


def pieces(value, count):
    parts = []
    for unused in range(count):
        part = value.astype(BF16).astype(F32)
        parts.append(part)
        value = value - part
    return parts


def build_features(wx, wy, g, ox, oy, stage_t, stage_s, stage_w, t_ref, s_ref, w_ref, first, with_target):
    count = wx.shape[0]
    one = jnp.ones_like(wx)
    zero = jnp.zeros_like(wx)
    coarse_x = jnp.round(wx * 32.0) * (1.0 / 32.0)
    coarse_y = jnp.round(wy * 32.0) * (1.0 / 32.0)
    fine_x = wx - coarse_x
    fine_y = wy - coarse_y
    big_x = coarse_x + ox
    big_y = coarse_y + oy
    big = pieces(big_x * big_x + big_y * big_y, 2)
    rest = 2.0 * (big_x * fine_x + big_y * fine_y) + fine_x * fine_x + fine_y * fine_y
    px = pieces(fine_x, 2)
    py = pieces(fine_y, 2)
    if with_target:
        rows = [big_x, big_y, big[0], big[1], one, one, zero, zero]
        rows += [big_x, big_x, big_y, big_y, px[0], px[1], py[0], py[1]]
        rows += [px[0], px[0], px[1], py[0], py[0], py[1]]
        rows += pieces(rest + DELTA_SQUARED, 3) + [one, one, one]
        rows += [zero] * (FEATURES - len(rows))
        for f, row in enumerate(rows):
            stage_t[:count, f, :] = row
    twice = lambda v: -2.0 * v
    rows = [twice(big_x), twice(big_y), one, one, big[0], big[1], zero, zero]
    rows += [twice(px[0]), twice(px[1]), twice(py[0]), twice(py[1])]
    rows += [twice(big_x), twice(big_x), twice(big_y), twice(big_y)]
    rows += [twice(px[0]), twice(px[1]), twice(px[0]), twice(py[0]), twice(py[1]), twice(py[0])]
    rows += [one, one, one] + pieces(rest, 3)
    rows += [zero] * (FEATURES - len(rows))
    for f, row in enumerate(rows):
        stage_s[:count, f, :] = row
    rows = pieces(g, 3) + pieces(g * (wx + ox), 3) + pieces(g * (wy + oy), 3)
    rows += [zero] * (16 - len(rows))
    for f, row in enumerate(rows):
        stage_w[:count, f, :] = row
    for n in range(count):
        if with_target:
            t_ref[first + n] = stage_t[n].astype(BF16)
        s_ref[first + n] = jnp.transpose(stage_s[n]).astype(BF16)
        w_ref[first + n] = stage_w[n].astype(BF16)


def power_list(base_re, base_im, count):
    re = [jnp.ones_like(base_re)]
    im = [jnp.zeros_like(base_im)]
    for unused in range(1, count):
        a, b = re[-1], im[-1]
        re.append(a * base_re - b * base_im)
        im.append(a * base_im + b * base_re)
    return re, im


def row_of(n):
    return lax.broadcasted_iota(jnp.int32, (n, 1), 0)


def leaf_offsets():
    n = row_of(LEAVES)
    ox = (n >> 2).astype(F32) - 1.5
    oy = (n & 3).astype(F32) - 1.5
    return ox, oy


def own_rows(ref, part):
    return jnp.concatenate([ref[part, i] for i in range(SIDE)], axis=0)


def position():
    slab = lax.axis_index(SLAB)
    leaf = lax.axis_index("leaf")
    between = jnp.logical_and(leaf > 0, leaf < 3).astype(jnp.int32)
    return slab, leaf, slab & 1, leaf & 1, between


SLAB_ROWS = 72
LEAF_ROWS = 96


def prepare_own(part_ref, t_ref, s_ref, w_ref, m_ref, f_ref, a_ref, b_ref, stage_t, stage_s, stage_w):
    info = position()
    wx = own_rows(part_ref, 0)
    wy = own_rows(part_ref, 1)
    g = own_rows(part_ref, 2)
    ox, oy = leaf_offsets()
    lane = lax.broadcasted_iota(jnp.int32, (LEAVES, 128), 1)
    table = jnp.zeros((LEAVES, 128), F32)
    for start, base_re, base_im in ((0, wx, wy), (32, wx + ox, wy + oy)):
        re, im = power_list(base_re, base_im, ORDER)
        for k in range(ORDER):
            table = jnp.where(lane == start + k, jnp.sum(g * re[k], 1, keepdims=True), table)
            if k:
                table = jnp.where(lane == start + ORDER + k, jnp.sum(g * im[k], 1, keepdims=True), table)
    turned = jnp.transpose(table)
    leaf_part = jnp.concatenate([turned[0:24], jnp.zeros((24, 112), F32)], axis=1)
    block_part = jnp.sum(turned[32:56], axis=1, keepdims=True)
    me = info[0] * 4 + info[1]
    wide = lax.broadcasted_iota(jnp.int32, (24, 128), 1)
    block_row = jnp.where(wide == me, block_part, 0.0)
    m_ref[...] = leaf_part
    f_ref[...] = block_row
    even = info[2] == 0
    for c in range(3):
        first = jnp.concatenate([part_ref[c, 0], part_ref[c, 1]], axis=0)
        last = jnp.concatenate([part_ref[c, 2], part_ref[c, 3]], axis=0)
        a_ref[8 * c : 8 * c + 8] = jnp.where(even, last, first)
        b_ref[8 * c : 8 * c + 8] = jnp.where(even, first, last)
    none = jnp.zeros((24, 128), F32)
    for ref in (a_ref, b_ref):
        ref[24:48, 0:128] = leaf_part
        ref[24:48, 128:256] = none
        ref[48:72, 0:128] = block_row
        ref[48:72, 128:256] = none
    build_features(wx, wy, g, ox, oy, stage_t, stage_s, stage_w, t_ref, s_ref, w_ref, 0, True)


def pack_slab(part_ref, ra_ref, rb_ref, m_ref, f_ref, after_ref, m_out, f_out, near_ref, far_ref):
    info = position()
    even = info[2] == 0
    leaf_even = info[3] == 0
    inner = inner_slab(info[0])
    for c in range(3):
        ra = ra_ref[8 * c : 8 * c + 8]
        rb = rb_ref[8 * c : 8 * c + 8]
        if c == 2:
            rb = rb * inner
        before = jnp.where(even, rb, ra)
        after = jnp.where(even, ra, rb)
        rows = [before[0:4], before[4:8]] + [part_ref[c, i] for i in range(SIDE)] + [after[0:4], after[4:8]]
        left = jnp.concatenate([r[0:2] for r in rows], axis=0)
        right = jnp.concatenate([r[2:4] for r in rows], axis=0)
        near_ref[16 * c : 16 * c + 16] = jnp.where(leaf_even, right, left)
        far_ref[16 * c : 16 * c + 16] = jnp.where(leaf_even, left, right)
    ma = ra_ref[24:48, 0:16]
    mb = rb_ref[24:48, 0:16] * inner
    window = jnp.concatenate(
        [m_ref[:, 0:16], jnp.where(even, mb, ma), jnp.where(even, ma, mb), jnp.zeros((24, 80), F32)], axis=1
    )
    blocks = f_ref[...] + ra_ref[48:72, 0:128]
    m_out[...] = window
    f_out[...] = blocks
    none = jnp.zeros((24, 128), F32)
    near_ref[48:72, 0:128] = jnp.concatenate([none[:, 0:48], window[:, 0:48], none[:, 0:32]], axis=1)
    near_ref[48:72, 128:256] = none
    far_ref[48:72, 0:128] = window
    far_ref[48:72, 128:256] = none
    near_ref[72:96, 0:128] = blocks
    near_ref[72:96, 128:256] = none


def slab_halo(ra_ref, rb_ref, s_ref, w_ref, stage_s, stage_w):
    even = position()[2] == 0
    inner = inner_slab(position()[0])
    halo = []
    for c in range(3):
        ra = ra_ref[8 * c : 8 * c + 8]
        rb = rb_ref[8 * c : 8 * c + 8]
        if c == 2:
            rb = rb * inner
        halo.append(jnp.concatenate([jnp.where(even, rb, ra), jnp.where(even, ra, rb)], axis=0))
    n = row_of(LEAVES)
    i = (n >> 2) - 2
    ox = jnp.where(i >= 0, i + 4, i).astype(F32) - 1.5
    oy = (n & 3).astype(F32) - 1.5
    build_features(halo[0], halo[1], halo[2], ox, oy, None, stage_s, stage_w, None, s_ref, w_ref, 0, False)


def leaf_halo(which, r_ref, s_ref, w_ref, stage_s, stage_w):
    info = position()
    leaf_even = info[3] == 0
    to_right = leaf_even if which == 0 else jnp.logical_not(leaf_even)
    valid = jnp.float32(1.0) if which == 0 else info[4].astype(F32)
    n = row_of(LEAVES)
    ox = (n >> 1).astype(F32) - 3.5
    side = (n & 1).astype(F32)
    oy = jnp.where(to_right, side + 4.0, side - 2.0) - 1.5
    build_features(
        r_ref[0:16], r_ref[16:32], r_ref[32:48] * valid, ox, oy, None, stage_s, stage_w, None, s_ref, w_ref, 0, False
    )


def near_halo(r_ref, s_ref, w_ref, stage_s, stage_w):
    leaf_halo(0, r_ref, s_ref, w_ref, stage_s, stage_w)


def far_halo(r_ref, s_ref, w_ref, stage_s, stage_w):
    leaf_halo(1, r_ref, s_ref, w_ref, stage_s, stage_w)


def pack_near(r_ref, f_ref, send_ref, after_ref, f_out, send_out):
    blocks = f_ref[...] + r_ref[72:96, 0:128]
    f_out[...] = blocks
    send_out[0:72] = send_ref[...]
    send_out[72:96, 0:128] = blocks
    send_out[72:96, 128:256] = jnp.zeros((24, 128), F32)


def chosen(index, values):
    if all(v == values[0] for v in values):
        return values[0]
    out = values[-1]
    for n in range(len(values) - 2, -1, -1):
        out = jnp.where(index == n, values[n], out)
    return out


def pairs(tables, mask_ref, t_ref, s_ref, w_ref, acc_ref, index, unused):
    for n in range(tables.shape[1]):
        t, s, o = (chosen(index, [int(v) for v in tables[:, n, c]]) for c in range(3))
        distance = jnp.dot(s_ref[s], t_ref[t], preferred_element_type=F32)
        kernel = 1.0 / distance
        high = kernel.astype(BF16)
        low = (kernel - high.astype(F32)).astype(BF16)
        w = w_ref[s]
        total = jnp.dot(w, high, preferred_element_type=F32) + jnp.dot(w, low, preferred_element_type=F32)
        if isinstance(o, int) and o == 16:
            acc_ref[t] = acc_ref[t] + total
        else:
            acc_ref[t] = acc_ref[t] + mask_ref[o, t] * total
    return 0


def direct_sides(near, far, extra, extra_in, mask_ref, t_ref, s2_ref, w2_ref, s3_ref, w3_ref, acc_in, *refs):
    acc_ref = refs[extra_in]
    acc_ref[...] = acc_in[...]
    parity = position()[3]
    pairs(near, mask_ref, t_ref, s2_ref, w2_ref, acc_ref, parity, 0)
    if extra is not None:
        extra(*refs[:extra_in], *refs[extra_in + 1 :])

    @pl.when(position()[4] == 1)
    def _():
        pairs(far, mask_ref, t_ref, s3_ref, w3_ref, acc_ref, parity, 0)


RELEASE = ((0, 8, 15, 12), (0, 18, 30, 30), (0, 8, 15, 12))
LATE_STEPS = (20, 42)


def late_bodies():
    slab, leaf = position()[:2]
    places = (slab >> 3, (slab >> 1) & 3, leaf)
    late = sum(chosen(place, term) for place, term in zip(places, RELEASE))
    return sum((late >= step).astype(jnp.int32) for step in LATE_STEPS)


def direct(tables, zero, extra, extra_in, mask_ref, t_ref, s_ref, w_ref, *refs):
    if zero:
        acc_ref, rows_ref = refs
        acc_ref[...] = jnp.zeros_like(acc_ref)
        near_mask = jnp.concatenate([mask_ref[i] for i in range(SIDE)], axis=0).astype(F32)
        for o in range(16):
            rows_ref[o, :, 0, :] = jnp.broadcast_to(near_mask[:, o : o + 1], (LEAVES, SIZE))
        rows_ref[16, :, 0, :] = jnp.ones((LEAVES, SIZE), F32)
        mask_ref = rows_ref
    else:
        acc_ref = refs[extra_in + 1]
        acc_ref[...] = refs[0][...]
        others = refs[1 : extra_in + 1] + refs[extra_in + 2 :]
    step = functools.partial(pairs, tables, mask_ref, t_ref, s_ref, w_ref, acc_ref)
    split = tables.shape[0] - late_bodies()
    if tables.shape[0] == 1:
        step(0, 0)
    elif zero:
        lax.fori_loop(0, split, step, 0)
    else:
        lax.fori_loop(split, tables.shape[0], step, 0)
    if extra is not None:
        extra(*others)


def pair_table(kind, to_right=False):
    out = []
    for t in range(LEAVES):
        i, j = divmod(t, SIDE)
        for a, b in near_steps:
            o = cycle_steps.index((a, b)) if max(abs(a), abs(b)) == 2 else 16
            si, sj = i + a, j + b
            in_row, in_column = 0 <= si < SIDE, 0 <= sj < SIDE
            if kind == "own" and in_row and in_column:
                out.append((t, si * SIDE + sj, o))
            if kind == "slab" and not in_row and in_column:
                out.append((t, ((si + 2) if si < 0 else (si - 2)) * SIDE + sj, o))
            if kind == "leaf" and not in_column and (sj >= SIDE) == to_right:
                out.append((t, (si + 2) * 2 + (sj - SIDE if to_right else sj + 2), o))
    return np.array(out, np.int32)


def translate(groups, h_ref, a_ref, out_ref):
    for group, (tx, ty, weight) in enumerate(groups):
        span = slice(128 * group, 128 * group + 128)
        square = tx * tx + ty * ty
        inv_x = tx / square
        inv_y = -ty / square
        re = weight * inv_x
        im = weight * inv_y
        h_ref[0, :, span] = re
        h_ref[1, :, span] = im
        for order in range(1, 2 * ORDER - 1):
            re, im = (re * inv_x - im * inv_y) * float(order), (re * inv_y + im * inv_x) * float(order)
            h_ref[2 * order, :, span] = re
            h_ref[2 * order + 1, :, span] = im
    lane = lax.broadcasted_iota(jnp.int32, (LEAVES, 128), 1)
    table = jnp.zeros((LEAVES, 128), F32)
    half = ORDER // 2
    for first in (0, half):
        sums_re = [None] * half
        sums_im = [None] * half
        for group in range(len(groups)):
            span = slice(128 * group, 128 * group + 128)
            for k_ in range(ORDER):
                a_re = a_ref[k_ : k_ + 1, span]
                a_im = a_ref[ORDER + k_ : ORDER + k_ + 1, span]
                for m in range(half):
                    at = first + m + k_
                    h_re = h_ref[2 * at, :, span]
                    h_im = h_ref[2 * at + 1, :, span]
                    term_re = h_re * a_re - h_im * a_im
                    term_im = h_re * a_im + h_im * a_re
                    sums_re[m] = term_re if sums_re[m] is None else sums_re[m] + term_re
                    sums_im[m] = term_im if sums_im[m] is None else sums_im[m] + term_im
        for m in range(half):
            factor = 1.0 / math.factorial(first + m)
            table = jnp.where(lane == first + m, jnp.sum(sums_re[m], 1, keepdims=True) * factor, table)
            table = jnp.where(lane == 64 + first + m, jnp.sum(sums_im[m], 1, keepdims=True) * factor, table)
    out_ref[...] = table


def source_scale():
    row = row_of(24)
    which = jnp.where(row >= ORDER, row - ORDER, row)
    scale = jnp.zeros((24, 1), F32)
    for k_ in range(ORDER):
        scale = jnp.where(which == k_, (-1.0) ** (k_ + 1) / math.factorial(k_), scale)
    return scale


def leaf_field(nm_ref, m_ref, r1_ref, r2_ref, out_ref, h_ref, a_ref):
    info = position()
    leaf_even = info[3] == 0
    valid = info[4].astype(F32)
    n = row_of(LEAVES)
    ti = n >> 2
    tj = n & 3
    lane = lax.broadcasted_iota(jnp.int32, (LEAVES, 128), 1)
    near_mask = jnp.concatenate([nm_ref[i] for i in range(SIDE)], axis=0).astype(F32)
    near_shift = jnp.where(leaf_even, 4, -4)
    second = lane >= 48
    place = jnp.where(second, lane - 48, lane)
    k = place >> 4
    r = place & 15
    si = jnp.where(k == 0, r >> 2, jnp.where(k == 1, (r >> 2) - 4, (r >> 2) + 4))
    groups = []
    for column, lanes in ((jnp.where(second, near_shift, 0), 96), (-near_shift, 48)):
        dx = si - ti
        dy = (r & 3) + column - tj
        reach = jnp.maximum(jnp.abs(dx), jnp.abs(dy))
        weight = jnp.where(reach >= 3, 1.0, 0.0).astype(F32)
        for o, (a, b) in enumerate(cycle_steps):
            hit = jnp.logical_and(dx == a, dy == b)
            weight = jnp.where(hit, 1.0 - near_mask[:, o : o + 1], weight)
        inside = lane < lanes
        used = jnp.logical_and(reach >= 2, inside)
        groups.append(
            (
                jnp.where(used, dx.astype(F32), 1.0),
                jnp.where(used, dy.astype(F32), 1.0),
                jnp.where(inside, weight, 0.0),
            )
        )
    scale = source_scale()
    a_ref[:, 0:128] = (m_ref[...] + r1_ref[48:72, 0:128]) * scale
    a_ref[:, 128:256] = r2_ref[48:72, 0:128] * (valid * scale)
    translate(groups, h_ref, a_ref, out_ref)


def finish(part_ref, acc_ref, near_ref, f_ref, got_ref, out_ref, h_ref, a_ref, l_ref):
    info = position()
    n = row_of(LEAVES)
    ti = n >> 2
    tj = n & 3
    lane = lax.broadcasted_iota(jnp.int32, (LEAVES, 128), 1)
    bx = (lane >> 2) - info[0]
    by = (lane & 3) - info[1]
    remote = jnp.maximum(jnp.abs(bx), jnp.abs(by)) >= 2
    tx = jnp.where(remote, (bx * SIDE - ti).astype(F32) + 1.5, 1.0)
    ty = jnp.where(remote, (by * SIDE - tj).astype(F32) + 1.5, 1.0)
    weight = jnp.where(remote, 1.0, 0.0).astype(F32)
    a_ref[...] = (f_ref[...] + got_ref[...]) * source_scale()
    translate([(tx, ty, weight)], h_ref, a_ref, l_ref)
    local = l_ref[...] + near_ref[...]
    wx = own_rows(part_ref, 0)
    wy = own_rows(part_ref, 1)
    ox, oy = leaf_offsets()
    x = wx + ox
    y = wy + oy
    rows = lambda at: acc_ref[:, at, :] + acc_ref[:, at + 1, :] + acc_ref[:, at + 2, :]
    total = rows(0)
    sum_re = x * total - rows(3)
    sum_im = rows(6) - y * total
    p_re = jnp.ones_like(wx)
    p_im = jnp.zeros_like(wx)
    for m in range(ORDER):
        if m:
            p_re, p_im = p_re * wx - p_im * wy, p_re * wy + p_im * wx
        l_re = local[:, m : m + 1]
        l_im = local[:, 64 + m : 65 + m]
        sum_re = sum_re + (l_re * p_re - l_im * p_im)
        sum_im = sum_im + (l_re * p_im + l_im * p_re)
    sum_re = sum_re * (1.0 / TWO_PI)
    sum_im = sum_im * (1.0 / TWO_PI)
    for i in range(SIDE):
        out_ref[0, i] = sum_im[4 * i : 4 * i + 4]
        out_ref[1, i] = sum_re[4 * i : 4 * i + 4]


V = pl.BlockSpec(memory_space=pltpu.VMEM)
S = pl.BlockSpec(memory_space=pltpu.SMEM)
A = pl.BlockSpec(memory_space=pl.ANY)


def shaped(*shape, dtype=F32):
    return jax.ShapeDtypeStruct(shape, dtype)


def call(kernel, name, in_specs, outs, scratch, cost, aliases=None):
    return pl.pallas_call(
        kernel,
        out_shape=outs,
        in_specs=in_specs,
        out_specs=jax.tree.map(lambda unused: V, outs),
        scratch_shapes=scratch,
        name=name,
        input_output_aliases=aliases or {},
        cost_estimate=pl.CostEstimate(flops=cost, bytes_accessed=1 << 20, transcendentals=0),
        compiler_params=pltpu.CompilerParams(vmem_limit_bytes=VMEM_LIMIT),
    )


def features_out(count):
    return [shaped(count, SIZE, FEATURES, dtype=BF16), shaped(count, 16, SIZE, dtype=BF16)]


def stages(with_target):
    out = [pltpu.VMEM((LEAVES, FEATURES, SIZE), F32), pltpu.VMEM((LEAVES, 16, SIZE), F32)]
    return ([pltpu.VMEM((LEAVES, FEATURES, SIZE), F32)] if with_target else []) + out


SMALL = 4_000_000
PAIR = 400_000_000


def run_direct(name, tables, mask, feats, acc, extra=None, ins=(), outs=(), scratch=()):
    zero = acc is None
    args = [mask, *feats] + ([] if zero else [acc]) + list(ins)
    got = call(
        functools.partial(direct, tables, zero, extra, len(ins)),
        name,
        [V] * len(args),
        [shaped(LEAVES, 16, SIZE), *outs],
        list(scratch),
        PAIR * tables.shape[0] * tables.shape[1],
        {} if zero else {4: 0},
    )(*args)
    return got if outs else got[0]


def run_sides(name, near, far, args, extra=None, ins=(), outs=(), scratch=()):
    args = [*args, *ins]
    got = call(
        functools.partial(direct_sides, near, far, extra, len(ins)),
        name,
        [V] * len(args),
        [shaped(LEAVES, 16, SIZE), *outs],
        list(scratch),
        PAIR * 60,
        {6: 0},
    )(*args)
    return got if outs else got[0]


def far_scratch(width):
    return [pltpu.VMEM((4 * ORDER - 2, LEAVES, width), F32), pltpu.VMEM((24, width), F32)]


def body(particles, near_mask):
    turned = near_mask.transpose(1, 2, 0)
    t0, s0, w0, m0, f0, send_a, send_b = call(
        prepare_own,
        "prepare_own",
        [V],
        [shaped(LEAVES, FEATURES, SIZE, dtype=BF16), *features_out(LEAVES), shaped(24, 128), shaped(24, 128)]
        + [shaped(SLAB_ROWS, SIZE)] * 2,
        stages(True),
        SMALL,
    )(particles)
    recv_a = swap(send_a, "core")
    recv_b = swap(send_b, "slab")
    own = pair_table("own")
    split_pairs = own[:84].reshape(3, 28, 3)
    feats = (t0, s0, w0)
    acc, mask = run_direct(
        "direct_own_0", split_pairs, turned, feats, None, outs=[shaped(17, LEAVES, 1, SIZE)]
    )
    m1, f1, send_near, send_far = call(
        pack_slab,
        "pack_slab",
        [V, V, V, V, V, A],
        [shaped(24, 128), shaped(24, 128), shaped(LEAF_ROWS, SIZE), shaped(72, SIZE)],
        [],
        SMALL,
    )(particles, recv_a, recv_b, m0, f0, acc)
    send_near, acc = lax.optimization_barrier((send_near, acc))
    recv_near = swap(send_near, "leaf_near")
    built = dict(outs=features_out(LEAVES), scratch=stages(False))
    acc, s1, w1 = run_direct(
        "direct_own_1", own[None, 84:140], mask, feats, acc, extra=slab_halo, ins=(recv_a, recv_b), **built
    )
    f2, send_far = call(
        pack_near, "pack_near", [V, V, V, A], [shaped(24, 128), shaped(LEAF_ROWS, SIZE)], [], SMALL
    )(recv_near, f1, send_far, acc)
    send_far, acc = lax.optimization_barrier((send_far, acc))
    recv_far = swap(send_far, "leaf_far")
    acc, s2, w2 = run_direct(
        "direct_own_2", own[None, 140:], mask, feats, acc, extra=near_halo, ins=(recv_near,), **built
    )
    recv_far, acc = lax.optimization_barrier((recv_far, acc))
    f3 = f2 + recv_far[72:96, 0:128]
    f3, acc = lax.optimization_barrier((f3, acc))
    got = swap(f3, "z_near")
    slab_pairs = pair_table("slab").reshape(2, 1, 42, 3)
    acc, s3, w3 = run_direct(
        "direct_slab_0", slab_pairs[0], mask, (t0, s1, w1), acc, extra=far_halo, ins=(recv_far,), **built
    )
    got, acc = lax.optimization_barrier((got, acc))
    f4 = f3 + got
    f4, acc = lax.optimization_barrier((f4, acc))
    got = swap(f4, "z_far")
    acc = run_direct("direct_slab_1", slab_pairs[1], mask, (t0, s1, w1), acc)
    got, acc = lax.optimization_barrier((got, acc))
    f5 = f4 + got
    f5, acc = lax.optimization_barrier((f5, acc))
    got = swap(f5, "x_near")
    right = pair_table("leaf", True)
    left = pair_table("leaf", False)
    near_pairs = np.stack([right, left])
    far_pairs = np.stack([left, right])
    shared = (mask, t0, s2, w2, s3, w3)
    acc, local = run_sides(
        "direct_sides_0",
        near_pairs[:, :30],
        far_pairs[:, :30],
        (*shared, acc),
        extra=leaf_field,
        ins=(turned, m1, recv_near, recv_far),
        outs=[shaped(LEAVES, 128)],
        scratch=far_scratch(256),
    )
    got, acc = lax.optimization_barrier((got, acc))
    f6 = f5 + got
    f6, acc = lax.optimization_barrier((f6, acc))
    got = swap(f6, "x_far")
    acc = run_sides("direct_sides_1", near_pairs[:, 30:], far_pairs[:, 30:], (*shared, acc))
    acc = run_direct("direct_late", split_pairs, mask, feats, acc)
    got, acc = lax.optimization_barrier((got, acc))
    return call(
        finish,
        "finish",
        [V] * 5,
        shaped(2, SIDE, SIDE, SIZE),
        far_scratch(128) + [pltpu.VMEM((LEAVES, 128), F32)],
        SMALL,
    )(particles, acc, local, f6, got)


def solution(mesh):
    finer = Mesh(mesh.devices.reshape(4, 4, 2, mesh.shape["leaf"]), ALL)
    in_specs = (P(None, SLAB, "leaf", None), P(None, SLAB, "leaf"))
    out_specs = P(None, SLAB, "leaf", None)
    run = jax.shard_map(body, mesh=finer, in_specs=in_specs, out_specs=out_specs, check_vma=False)

    def whole(particles, near_mask):
        with jax.sharding.use_abstract_mesh(mesh.abstract_mesh):
            return run(particles, near_mask)

    return run
```

```python
import functools
import math

import jax
import jax.numpy as jnp
import numpy as np
from jax import lax
from jax.experimental import pallas as pl
from jax.experimental.pallas import tpu as pltpu
from jax.sharding import Mesh
from jax.sharding import PartitionSpec as P

ORDER = 10
SIDE = 4
LEAVES = 16
SIZE = 256
FEATURES = 32
DELTA_SQUARED = 0.0025
TWO_PI = 2.0 * math.pi
SLAB = ("slab_0", "slab_1", "slab_2")
ALL = ("slab_0", "slab_1", "slab_2", "leaf")
F32 = jnp.float32
BF16 = jnp.bfloat16
VMEM_LIMIT = 6 << 20
cycle_steps = [(a, b) for a in range(-2, 3) for b in range(-2, 3) if max(abs(a), abs(b)) == 2]
near_steps = [(a, b) for a in range(-2, 3) for b in range(-2, 3)]


def exchange_pairs(partner):
    pairs = []
    for x in range(4):
        for z in range(4):
            for c in range(2):
                for y in range(4):
                    other = partner(x, z, c, y)
                    if other is not None:
                        a, b, d, e = other
                        pairs.append((((x * 4 + z) * 2 + c) * 4 + y, ((a * 4 + b) * 2 + d) * 4 + e))
    return pairs


def inner_slab(slab):
    return jnp.logical_and(slab > 0, slab < 31).astype(F32)


def slab_between_chips(x, z, c, y):
    slab = (x * 4 + z) * 2 + c
    other = (slab + 1 if c == 1 else slab - 1) % 32
    return (other // 8, (other // 2) % 4, other % 2, y)


def near_side(k):
    return k ^ 1


def far_side(k):
    return 3 - k


SWAPS = {
    "core": exchange_pairs(lambda x, z, c, y: (x, z, 1 - c, y)),
    "slab": exchange_pairs(slab_between_chips),
    "leaf_near": exchange_pairs(lambda x, z, c, y: (x, z, c, near_side(y))),
    "leaf_far": exchange_pairs(lambda x, z, c, y: (x, z, c, far_side(y))),
    "z_near": exchange_pairs(lambda x, z, c, y: (x, near_side(z), c, y)),
    "z_far": exchange_pairs(lambda x, z, c, y: (x, far_side(z), c, y)),
    "x_near": exchange_pairs(lambda x, z, c, y: (near_side(x), z, c, y)),
    "x_far": exchange_pairs(lambda x, z, c, y: (far_side(x), z, c, y)),
}


def swap(value, name):
    return lax.ppermute(value, ALL, SWAPS[name])


def pieces(value, count):
    parts = []
    for unused in range(count):
        part = value.astype(BF16).astype(F32)
        parts.append(part)
        value = value - part
    return parts


def build_features(wx, wy, g, ox, oy, stage_t, stage_s, stage_w, t_ref, s_ref, w_ref, first, with_target):
    count = wx.shape[0]
    one = jnp.ones_like(wx)
    zero = jnp.zeros_like(wx)
    coarse_x = jnp.round(wx * 32.0) * (1.0 / 32.0)
    coarse_y = jnp.round(wy * 32.0) * (1.0 / 32.0)
    fine_x = wx - coarse_x
    fine_y = wy - coarse_y
    big_x = coarse_x + ox
    big_y = coarse_y + oy
    big = pieces(big_x * big_x + big_y * big_y, 2)
    rest = 2.0 * (big_x * fine_x + big_y * fine_y) + fine_x * fine_x + fine_y * fine_y
    px = pieces(fine_x, 2)
    py = pieces(fine_y, 2)
    if with_target:
        rows = [big_x, big_y, big[0], big[1], one, one, zero, zero]
        rows += [big_x, big_x, big_y, big_y, px[0], px[1], py[0], py[1]]
        rows += [px[0], px[0], px[1], py[0], py[0], py[1]]
        rows += pieces(rest + DELTA_SQUARED, 3) + [one, one, one]
        rows += [zero] * (FEATURES - len(rows))
        for f, row in enumerate(rows):
            stage_t[:count, f, :] = row
    twice = lambda v: -2.0 * v
    rows = [twice(big_x), twice(big_y), one, one, big[0], big[1], zero, zero]
    rows += [twice(px[0]), twice(px[1]), twice(py[0]), twice(py[1])]
    rows += [twice(big_x), twice(big_x), twice(big_y), twice(big_y)]
    rows += [twice(px[0]), twice(px[1]), twice(px[0]), twice(py[0]), twice(py[1]), twice(py[0])]
    rows += [one, one, one] + pieces(rest, 3)
    rows += [zero] * (FEATURES - len(rows))
    for f, row in enumerate(rows):
        stage_s[:count, f, :] = row
    rows = pieces(g, 3) + pieces(g * (wx + ox), 3) + pieces(g * (wy + oy), 3)
    rows += [zero] * (16 - len(rows))
    for f, row in enumerate(rows):
        stage_w[:count, f, :] = row
    for n in range(count):
        if with_target:
            t_ref[first + n] = stage_t[n].astype(BF16)
        s_ref[first + n] = jnp.transpose(stage_s[n]).astype(BF16)
        w_ref[first + n] = stage_w[n].astype(BF16)


def power_list(base_re, base_im, count):
    re = [jnp.ones_like(base_re)]
    im = [jnp.zeros_like(base_im)]
    for unused in range(1, count):
        a, b = re[-1], im[-1]
        re.append(a * base_re - b * base_im)
        im.append(a * base_im + b * base_re)
    return re, im


def row_of(n):
    return lax.broadcasted_iota(jnp.int32, (n, 1), 0)


def leaf_offsets():
    n = row_of(LEAVES)
    ox = (n >> 2).astype(F32) - 1.5
    oy = (n & 3).astype(F32) - 1.5
    return ox, oy


def own_rows(ref, part):
    return jnp.concatenate([ref[part, i] for i in range(SIDE)], axis=0)


def position():
    slab = lax.axis_index(SLAB)
    leaf = lax.axis_index("leaf")
    between = jnp.logical_and(leaf > 0, leaf < 3).astype(jnp.int32)
    return slab, leaf, slab & 1, leaf & 1, between


SLAB_ROWS = 72
LEAF_ROWS = 96


def prepare_own(part_ref, t_ref, s_ref, w_ref, m_ref, f_ref, a_ref, b_ref, stage_t, stage_s, stage_w):
    info = position()
    wx = own_rows(part_ref, 0)
    wy = own_rows(part_ref, 1)
    g = own_rows(part_ref, 2)
    ox, oy = leaf_offsets()
    lane = lax.broadcasted_iota(jnp.int32, (LEAVES, 128), 1)
    table = jnp.zeros((LEAVES, 128), F32)
    for start, base_re, base_im in ((0, wx, wy), (32, wx + ox, wy + oy)):
        re, im = power_list(base_re, base_im, ORDER)
        for k in range(ORDER):
            table = jnp.where(lane == start + k, jnp.sum(g * re[k], 1, keepdims=True), table)
            if k:
                table = jnp.where(lane == start + ORDER + k, jnp.sum(g * im[k], 1, keepdims=True), table)
    turned = jnp.transpose(table)
    leaf_part = jnp.concatenate([turned[0:24], jnp.zeros((24, 112), F32)], axis=1)
    block_part = jnp.sum(turned[32:56], axis=1, keepdims=True)
    me = info[0] * 4 + info[1]
    wide = lax.broadcasted_iota(jnp.int32, (24, 128), 1)
    block_row = jnp.where(wide == me, block_part, 0.0)
    m_ref[...] = leaf_part
    f_ref[...] = block_row
    even = info[2] == 0
    for c in range(3):
        first = jnp.concatenate([part_ref[c, 0], part_ref[c, 1]], axis=0)
        last = jnp.concatenate([part_ref[c, 2], part_ref[c, 3]], axis=0)
        a_ref[8 * c : 8 * c + 8] = jnp.where(even, last, first)
        b_ref[8 * c : 8 * c + 8] = jnp.where(even, first, last)
    none = jnp.zeros((24, 128), F32)
    for ref in (a_ref, b_ref):
        ref[24:48, 0:128] = leaf_part
        ref[24:48, 128:256] = none
        ref[48:72, 0:128] = block_row
        ref[48:72, 128:256] = none
    build_features(wx, wy, g, ox, oy, stage_t, stage_s, stage_w, t_ref, s_ref, w_ref, 0, True)


def pack_slab(part_ref, ra_ref, rb_ref, m_ref, f_ref, after_ref, m_out, f_out, near_ref, far_ref):
    info = position()
    even = info[2] == 0
    leaf_even = info[3] == 0
    inner = inner_slab(info[0])
    for c in range(3):
        ra = ra_ref[8 * c : 8 * c + 8]
        rb = rb_ref[8 * c : 8 * c + 8]
        if c == 2:
            rb = rb * inner
        before = jnp.where(even, rb, ra)
        after = jnp.where(even, ra, rb)
        rows = [before[0:4], before[4:8]] + [part_ref[c, i] for i in range(SIDE)] + [after[0:4], after[4:8]]
        left = jnp.concatenate([r[0:2] for r in rows], axis=0)
        right = jnp.concatenate([r[2:4] for r in rows], axis=0)
        near_ref[16 * c : 16 * c + 16] = jnp.where(leaf_even, right, left)
        far_ref[16 * c : 16 * c + 16] = jnp.where(leaf_even, left, right)
    ma = ra_ref[24:48, 0:16]
    mb = rb_ref[24:48, 0:16] * inner
    window = jnp.concatenate(
        [m_ref[:, 0:16], jnp.where(even, mb, ma), jnp.where(even, ma, mb), jnp.zeros((24, 80), F32)], axis=1
    )
    blocks = f_ref[...] + ra_ref[48:72, 0:128]
    m_out[...] = window
    f_out[...] = blocks
    none = jnp.zeros((24, 128), F32)
    near_ref[48:72, 0:128] = jnp.concatenate([none[:, 0:48], window[:, 0:48], none[:, 0:32]], axis=1)
    near_ref[48:72, 128:256] = none
    far_ref[48:72, 0:128] = window
    far_ref[48:72, 128:256] = none
    near_ref[72:96, 0:128] = blocks
    near_ref[72:96, 128:256] = none


def slab_halo(ra_ref, rb_ref, s_ref, w_ref, stage_s, stage_w):
    even = position()[2] == 0
    inner = inner_slab(position()[0])
    halo = []
    for c in range(3):
        ra = ra_ref[8 * c : 8 * c + 8]
        rb = rb_ref[8 * c : 8 * c + 8]
        if c == 2:
            rb = rb * inner
        halo.append(jnp.concatenate([jnp.where(even, rb, ra), jnp.where(even, ra, rb)], axis=0))
    n = row_of(LEAVES)
    i = (n >> 2) - 2
    ox = jnp.where(i >= 0, i + 4, i).astype(F32) - 1.5
    oy = (n & 3).astype(F32) - 1.5
    build_features(halo[0], halo[1], halo[2], ox, oy, None, stage_s, stage_w, None, s_ref, w_ref, 0, False)


def leaf_halo(which, r_ref, s_ref, w_ref, stage_s, stage_w):
    info = position()
    leaf_even = info[3] == 0
    to_right = leaf_even if which == 0 else jnp.logical_not(leaf_even)
    valid = jnp.float32(1.0) if which == 0 else info[4].astype(F32)
    n = row_of(LEAVES)
    ox = (n >> 1).astype(F32) - 3.5
    side = (n & 1).astype(F32)
    oy = jnp.where(to_right, side + 4.0, side - 2.0) - 1.5
    build_features(
        r_ref[0:16], r_ref[16:32], r_ref[32:48] * valid, ox, oy, None, stage_s, stage_w, None, s_ref, w_ref, 0, False
    )


def near_halo(r_ref, s_ref, w_ref, stage_s, stage_w):
    leaf_halo(0, r_ref, s_ref, w_ref, stage_s, stage_w)


def far_halo(r_ref, s_ref, w_ref, stage_s, stage_w):
    leaf_halo(1, r_ref, s_ref, w_ref, stage_s, stage_w)


def pack_near(r_ref, f_ref, send_ref, after_ref, f_out, send_out):
    blocks = f_ref[...] + r_ref[72:96, 0:128]
    f_out[...] = blocks
    send_out[0:72] = send_ref[...]
    send_out[72:96, 0:128] = blocks
    send_out[72:96, 128:256] = jnp.zeros((24, 128), F32)


def chosen(index, values):
    if all(v == values[0] for v in values):
        return values[0]
    out = values[-1]
    for n in range(len(values) - 2, -1, -1):
        out = jnp.where(index == n, values[n], out)
    return out


def pairs(tables, mask_ref, t_ref, s_ref, w_ref, acc_ref, index, unused):
    for n in range(tables.shape[1]):
        t, s, o = (chosen(index, [int(v) for v in tables[:, n, c]]) for c in range(3))
        distance = jnp.dot(s_ref[s], t_ref[t], preferred_element_type=F32)
        kernel = 1.0 / distance
        high = kernel.astype(BF16)
        low = (kernel - high.astype(F32)).astype(BF16)
        w = w_ref[s]
        total = jnp.dot(w, high, preferred_element_type=F32) + jnp.dot(w, low, preferred_element_type=F32)
        if isinstance(o, int) and o == 16:
            acc_ref[t] = acc_ref[t] + total
        else:
            acc_ref[t] = acc_ref[t] + mask_ref[o, t] * total
    return 0


def direct_sides(near, far, late, extra, extra_in, mask_ref, t_ref, s2_ref, w2_ref, s3_ref, w3_ref, acc_in, *refs):
    acc_ref = refs[extra_in]
    acc_ref[...] = acc_in[...]
    parity = position()[3]
    pairs(near, mask_ref, t_ref, s2_ref, w2_ref, acc_ref, parity, 0)
    if extra is not None:
        extra(*refs[:extra_in], *refs[extra_in + 1 :])

    @pl.when(position()[4] == 1)
    def _():
        pairs(far, mask_ref, t_ref, s3_ref, w3_ref, acc_ref, parity, 0)

    if late is not None:
        step = functools.partial(pairs, late, mask_ref, t_ref, refs[0], refs[1], acc_ref)
        lax.fori_loop(late.shape[0] - late_bodies(), late.shape[0], step, 0)


RELEASE = ((0, 8, 15, 12), (0, 18, 30, 30), (0, 8, 15, 12))
LATE_STEPS = (20, 42)


def late_bodies():
    slab, leaf = position()[:2]
    places = (slab >> 3, (slab >> 1) & 3, leaf)
    late = sum(chosen(place, term) for place, term in zip(places, RELEASE))
    return sum((late >= step).astype(jnp.int32) for step in LATE_STEPS)


def direct(tables, zero, extra, extra_in, mask_ref, t_ref, s_ref, w_ref, *refs):
    if zero:
        acc_ref, rows_ref = refs
        acc_ref[...] = jnp.zeros_like(acc_ref)
        near_mask = jnp.concatenate([mask_ref[i] for i in range(SIDE)], axis=0).astype(F32)
        for o in range(16):
            rows_ref[o, :, 0, :] = jnp.broadcast_to(near_mask[:, o : o + 1], (LEAVES, SIZE))
        rows_ref[16, :, 0, :] = jnp.ones((LEAVES, SIZE), F32)
        mask_ref = rows_ref
    else:
        acc_ref = refs[extra_in + 1]
        acc_ref[...] = refs[0][...]
        others = refs[1 : extra_in + 1] + refs[extra_in + 2 :]
    step = functools.partial(pairs, tables, mask_ref, t_ref, s_ref, w_ref, acc_ref)
    split = tables.shape[0] - late_bodies()
    if tables.shape[0] == 1:
        step(0, 0)
    else:
        lax.fori_loop(0, split, step, 0)
    if extra is not None:
        extra(*others)


def pair_table(kind, to_right=False):
    out = []
    for t in range(LEAVES):
        i, j = divmod(t, SIDE)
        for a, b in near_steps:
            o = cycle_steps.index((a, b)) if max(abs(a), abs(b)) == 2 else 16
            si, sj = i + a, j + b
            in_row, in_column = 0 <= si < SIDE, 0 <= sj < SIDE
            if kind == "own" and in_row and in_column:
                out.append((t, si * SIDE + sj, o))
            if kind == "slab" and not in_row and in_column:
                out.append((t, ((si + 2) if si < 0 else (si - 2)) * SIDE + sj, o))
            if kind == "leaf" and not in_column and (sj >= SIDE) == to_right:
                out.append((t, (si + 2) * 2 + (sj - SIDE if to_right else sj + 2), o))
    return np.array(out, np.int32)


def translate(groups, h_ref, a_ref, out_ref):
    for group, (tx, ty, weight) in enumerate(groups):
        span = slice(128 * group, 128 * group + 128)
        square = tx * tx + ty * ty
        inv_x = tx / square
        inv_y = -ty / square
        re = weight * inv_x
        im = weight * inv_y
        h_ref[0, :, span] = re
        h_ref[1, :, span] = im
        for order in range(1, 2 * ORDER - 1):
            re, im = (re * inv_x - im * inv_y) * float(order), (re * inv_y + im * inv_x) * float(order)
            h_ref[2 * order, :, span] = re
            h_ref[2 * order + 1, :, span] = im
    lane = lax.broadcasted_iota(jnp.int32, (LEAVES, 128), 1)
    table = jnp.zeros((LEAVES, 128), F32)
    half = ORDER // 2
    for first in (0, half):
        sums_re = [None] * half
        sums_im = [None] * half
        for group in range(len(groups)):
            span = slice(128 * group, 128 * group + 128)
            for k_ in range(ORDER):
                a_re = a_ref[k_ : k_ + 1, span]
                a_im = a_ref[ORDER + k_ : ORDER + k_ + 1, span]
                for m in range(half):
                    at = first + m + k_
                    h_re = h_ref[2 * at, :, span]
                    h_im = h_ref[2 * at + 1, :, span]
                    term_re = h_re * a_re - h_im * a_im
                    term_im = h_re * a_im + h_im * a_re
                    sums_re[m] = term_re if sums_re[m] is None else sums_re[m] + term_re
                    sums_im[m] = term_im if sums_im[m] is None else sums_im[m] + term_im
        for m in range(half):
            factor = 1.0 / math.factorial(first + m)
            table = jnp.where(lane == first + m, jnp.sum(sums_re[m], 1, keepdims=True) * factor, table)
            table = jnp.where(lane == 64 + first + m, jnp.sum(sums_im[m], 1, keepdims=True) * factor, table)
    out_ref[...] = table


def source_scale():
    row = row_of(24)
    which = jnp.where(row >= ORDER, row - ORDER, row)
    scale = jnp.zeros((24, 1), F32)
    for k_ in range(ORDER):
        scale = jnp.where(which == k_, (-1.0) ** (k_ + 1) / math.factorial(k_), scale)
    return scale


def leaf_field(nm_ref, m_ref, r1_ref, r2_ref, out_ref, h_ref, a_ref):
    info = position()
    leaf_even = info[3] == 0
    valid = info[4].astype(F32)
    n = row_of(LEAVES)
    ti = n >> 2
    tj = n & 3
    lane = lax.broadcasted_iota(jnp.int32, (LEAVES, 128), 1)
    near_mask = jnp.concatenate([nm_ref[i] for i in range(SIDE)], axis=0).astype(F32)
    near_shift = jnp.where(leaf_even, 4, -4)
    second = lane >= 48
    place = jnp.where(second, lane - 48, lane)
    k = place >> 4
    r = place & 15
    si = jnp.where(k == 0, r >> 2, jnp.where(k == 1, (r >> 2) - 4, (r >> 2) + 4))
    groups = []
    for column, lanes in ((jnp.where(second, near_shift, 0), 96), (-near_shift, 48)):
        dx = si - ti
        dy = (r & 3) + column - tj
        reach = jnp.maximum(jnp.abs(dx), jnp.abs(dy))
        weight = jnp.where(reach >= 3, 1.0, 0.0).astype(F32)
        for o, (a, b) in enumerate(cycle_steps):
            hit = jnp.logical_and(dx == a, dy == b)
            weight = jnp.where(hit, 1.0 - near_mask[:, o : o + 1], weight)
        inside = lane < lanes
        used = jnp.logical_and(reach >= 2, inside)
        groups.append(
            (
                jnp.where(used, dx.astype(F32), 1.0),
                jnp.where(used, dy.astype(F32), 1.0),
                jnp.where(inside, weight, 0.0),
            )
        )
    scale = source_scale()
    a_ref[:, 0:128] = (m_ref[...] + r1_ref[48:72, 0:128]) * scale
    a_ref[:, 128:256] = r2_ref[48:72, 0:128] * (valid * scale)
    translate(groups, h_ref, a_ref, out_ref)


def finish(part_ref, acc_ref, near_ref, f_ref, got_ref, out_ref, h_ref, a_ref, l_ref):
    info = position()
    n = row_of(LEAVES)
    ti = n >> 2
    tj = n & 3
    lane = lax.broadcasted_iota(jnp.int32, (LEAVES, 128), 1)
    bx = (lane >> 2) - info[0]
    by = (lane & 3) - info[1]
    remote = jnp.maximum(jnp.abs(bx), jnp.abs(by)) >= 2
    tx = jnp.where(remote, (bx * SIDE - ti).astype(F32) + 1.5, 1.0)
    ty = jnp.where(remote, (by * SIDE - tj).astype(F32) + 1.5, 1.0)
    weight = jnp.where(remote, 1.0, 0.0).astype(F32)
    a_ref[...] = (f_ref[...] + got_ref[...]) * source_scale()
    translate([(tx, ty, weight)], h_ref, a_ref, l_ref)
    local = l_ref[...] + near_ref[...]
    wx = own_rows(part_ref, 0)
    wy = own_rows(part_ref, 1)
    ox, oy = leaf_offsets()
    x = wx + ox
    y = wy + oy
    rows = lambda at: acc_ref[:, at, :] + acc_ref[:, at + 1, :] + acc_ref[:, at + 2, :]
    total = rows(0)
    sum_re = x * total - rows(3)
    sum_im = rows(6) - y * total
    p_re = jnp.ones_like(wx)
    p_im = jnp.zeros_like(wx)
    for m in range(ORDER):
        if m:
            p_re, p_im = p_re * wx - p_im * wy, p_re * wy + p_im * wx
        l_re = local[:, m : m + 1]
        l_im = local[:, 64 + m : 65 + m]
        sum_re = sum_re + (l_re * p_re - l_im * p_im)
        sum_im = sum_im + (l_re * p_im + l_im * p_re)
    sum_re = sum_re * (1.0 / TWO_PI)
    sum_im = sum_im * (1.0 / TWO_PI)
    for i in range(SIDE):
        out_ref[0, i] = sum_im[4 * i : 4 * i + 4]
        out_ref[1, i] = sum_re[4 * i : 4 * i + 4]


V = pl.BlockSpec(memory_space=pltpu.VMEM)
S = pl.BlockSpec(memory_space=pltpu.SMEM)
A = pl.BlockSpec(memory_space=pl.ANY)


def shaped(*shape, dtype=F32):
    return jax.ShapeDtypeStruct(shape, dtype)


def call(kernel, name, in_specs, outs, scratch, cost, aliases=None):
    return pl.pallas_call(
        kernel,
        out_shape=outs,
        in_specs=in_specs,
        out_specs=jax.tree.map(lambda unused: V, outs),
        scratch_shapes=scratch,
        name=name,
        input_output_aliases=aliases or {},
        cost_estimate=pl.CostEstimate(flops=cost, bytes_accessed=1 << 20, transcendentals=0),
        compiler_params=pltpu.CompilerParams(vmem_limit_bytes=VMEM_LIMIT),
    )


def features_out(count):
    return [shaped(count, SIZE, FEATURES, dtype=BF16), shaped(count, 16, SIZE, dtype=BF16)]


def stages(with_target):
    out = [pltpu.VMEM((LEAVES, FEATURES, SIZE), F32), pltpu.VMEM((LEAVES, 16, SIZE), F32)]
    return ([pltpu.VMEM((LEAVES, FEATURES, SIZE), F32)] if with_target else []) + out


SMALL = 4_000_000
PAIR = 400_000_000


def run_direct(name, tables, mask, feats, acc, extra=None, ins=(), outs=(), scratch=()):
    zero = acc is None
    args = [mask, *feats] + ([] if zero else [acc]) + list(ins)
    got = call(
        functools.partial(direct, tables, zero, extra, len(ins)),
        name,
        [V] * len(args),
        [shaped(LEAVES, 16, SIZE), *outs],
        list(scratch),
        PAIR * tables.shape[0] * tables.shape[1],
        {} if zero else {4: 0},
    )(*args)
    return got if outs else got[0]


def run_sides(name, near, far, args, late=None, extra=None, ins=(), outs=(), scratch=()):
    args = [*args, *ins]
    got = call(
        functools.partial(direct_sides, near, far, late, extra, len(ins)),
        name,
        [V] * len(args),
        [shaped(LEAVES, 16, SIZE), *outs],
        list(scratch),
        PAIR * 60,
        {6: 0},
    )(*args)
    return got if outs else got[0]


def far_scratch(width):
    return [pltpu.VMEM((4 * ORDER - 2, LEAVES, width), F32), pltpu.VMEM((24, width), F32)]


def body(particles, near_mask):
    turned = near_mask.transpose(1, 2, 0)
    t0, s0, w0, m0, f0, send_a, send_b = call(
        prepare_own,
        "prepare_own",
        [V],
        [shaped(LEAVES, FEATURES, SIZE, dtype=BF16), *features_out(LEAVES), shaped(24, 128), shaped(24, 128)]
        + [shaped(SLAB_ROWS, SIZE)] * 2,
        stages(True),
        SMALL,
    )(particles)
    recv_a = swap(send_a, "core")
    recv_b = swap(send_b, "slab")
    own = pair_table("own")
    split_pairs = own[:84].reshape(3, 28, 3)
    feats = (t0, s0, w0)
    acc, mask = run_direct(
        "direct_own_0", split_pairs, turned, feats, None, outs=[shaped(17, LEAVES, 1, SIZE)]
    )
    m1, f1, send_near, send_far = call(
        pack_slab,
        "pack_slab",
        [V, V, V, V, V, A],
        [shaped(24, 128), shaped(24, 128), shaped(LEAF_ROWS, SIZE), shaped(72, SIZE)],
        [],
        SMALL,
    )(particles, recv_a, recv_b, m0, f0, acc)
    send_near, acc = lax.optimization_barrier((send_near, acc))
    recv_near = swap(send_near, "leaf_near")
    built = dict(outs=features_out(LEAVES), scratch=stages(False))
    acc, s1, w1 = run_direct(
        "direct_own_1", own[None, 84:140], mask, feats, acc, extra=slab_halo, ins=(recv_a, recv_b), **built
    )
    f2, send_far = call(
        pack_near, "pack_near", [V, V, V, A], [shaped(24, 128), shaped(LEAF_ROWS, SIZE)], [], SMALL
    )(recv_near, f1, send_far, acc)
    send_far, acc = lax.optimization_barrier((send_far, acc))
    recv_far = swap(send_far, "leaf_far")
    acc, s2, w2 = run_direct(
        "direct_own_2", own[None, 140:], mask, feats, acc, extra=near_halo, ins=(recv_near,), **built
    )
    recv_far, acc = lax.optimization_barrier((recv_far, acc))
    f3 = f2 + recv_far[72:96, 0:128]
    f3, acc = lax.optimization_barrier((f3, acc))
    got = swap(f3, "z_near")
    slab_pairs = pair_table("slab").reshape(2, 1, 42, 3)
    acc, s3, w3 = run_direct(
        "direct_slab_0", slab_pairs[0], mask, (t0, s1, w1), acc, extra=far_halo, ins=(recv_far,), **built
    )
    got, acc = lax.optimization_barrier((got, acc))
    f4 = f3 + got
    f4, acc = lax.optimization_barrier((f4, acc))
    got = swap(f4, "z_far")
    acc = run_direct("direct_slab_1", slab_pairs[1], mask, (t0, s1, w1), acc)
    got, acc = lax.optimization_barrier((got, acc))
    f5 = f4 + got
    f5, acc = lax.optimization_barrier((f5, acc))
    got = swap(f5, "x_near")
    right = pair_table("leaf", True)
    left = pair_table("leaf", False)
    near_pairs = np.stack([right, left])
    far_pairs = np.stack([left, right])
    shared = (mask, t0, s2, w2, s3, w3)
    acc, local = run_sides(
        "direct_sides_0",
        near_pairs[:, :30],
        far_pairs[:, :30],
        (*shared, acc),
        extra=leaf_field,
        ins=(turned, m1, recv_near, recv_far),
        outs=[shaped(LEAVES, 128)],
        scratch=far_scratch(256),
    )
    got, acc = lax.optimization_barrier((got, acc))
    f6 = f5 + got
    f6, acc = lax.optimization_barrier((f6, acc))
    got = swap(f6, "x_far")
    acc = run_sides(
        "direct_sides_1", near_pairs[:, 30:], far_pairs[:, 30:], (*shared, acc), split_pairs, ins=(s0, w0)
    )
    got, acc = lax.optimization_barrier((got, acc))
    return call(
        finish,
        "finish",
        [V] * 5,
        shaped(2, SIDE, SIDE, SIZE),
        far_scratch(128) + [pltpu.VMEM((LEAVES, 128), F32)],
        SMALL,
    )(particles, acc, local, f6, got)


def solution(mesh):
    finer = Mesh(mesh.devices.reshape(4, 4, 2, mesh.shape["leaf"]), ALL)
    in_specs = (P(None, SLAB, "leaf", None), P(None, SLAB, "leaf"))
    out_specs = P(None, SLAB, "leaf", None)
    run = jax.shard_map(body, mesh=finer, in_specs=in_specs, out_specs=out_specs, check_vma=False)

    def whole(particles, near_mask):
        with jax.sharding.use_abstract_mesh(mesh.abstract_mesh):
            return run(particles, near_mask)

    return run
```
